32 devices in a mesh: dp: 4 (over y, x), mp: 8 (over z, core).
Axes of the slice: x: 2, y: 2, z: 4, core: 2. Of those that a mesh axis runs over, the one named last changes fastest.
Arguments:
- tokens: bfloat16 [8192, 1024], P(('mp', 'dp')), may hold values from -6 to 6
- cotangent: bfloat16 [8192, 1024], P(('mp', 'dp')), may hold values from -6 to 6
- domain_ids: int32 [8, 1], P('mp'), may hold values from 0 to 3
- domain_weight: float32 [4], replicated, may hold values from 0.5 to 2
- gains: float32 [2, 1024], replicated, may hold values from 0.5 to 1.5
- gain_mom: float32 [2, 1024], P(None, 'dp'), may hold values from -256 to 256
- factor_w: float32 [1024, 800], P('dp'), may hold values from -0.25 to 0.25
- factor_mom: float32 [1024, 800], P('dp'), may hold values from -160 to 160
- out_w: float32 [1024, 1024], P('dp'), may hold values from -0.75 to 0.75
- out_mom: float32 [1024, 1024], P('dp'), may hold values from -160 to 160
- gate_up_w: float32 [2, 1024, 2816], P(None, 'dp', 'mp'), may hold values from -0.1875 to 0.1875
- gate_up_mom: float32 [2, 1024, 2816], P(None, 'dp', 'mp'), may hold values from -160 to 160
- down_w: float32 [2816, 1024], P('mp', 'dp'), may hold values from -0.109375 to 0.109375
- down_mom: float32 [2816, 1024], P('mp', 'dp'), may hold values from -160 to 160
Outputs:
- block_out: bfloat16 [8192, 1024], P(('mp', 'dp'))
- input_grad: float32 [8192, 1024], P(('mp', 'dp'))
- gain_grad: float32 [2, 1024], P(None, 'dp')
- new_gains: float32 [2, 1024], P(None, 'dp')
- new_gain_mom: float32 [2, 1024], P(None, 'dp')
- new_factor_mom: float32 [1024, 800], P('dp')
- new_factor_w: float32 [1024, 800], P('dp')
- new_out_mom: float32 [1024, 1024], P('dp')
- new_out_w: float32 [1024, 1024], P('dp')
- new_gate_up_mom: float32 [2, 1024, 2816], P(None, 'dp', 'mp')
- new_gate_up_w: float32 [2, 1024, 2816], P(None, 'dp', 'mp')
- new_down_mom: float32 [2816, 1024], P('mp', 'dp')
- new_down_w: float32 [2816, 1024], P('mp', 'dp')
The draws below stay inside these ranges and needn't reach their ends.
Inputs may be any that keep to these rules, and one draw needn't show every extreme that they name: `domain_ids`: every domain is named by at least one sequence.
All inputs are finite; a program needn't handle non-finite values.
Results may differ from the reference program's by a relative error of at most 0.013.
The reference program's roundings to bfloat16 on the way count: a program that leaves them out, or rounds other values in their place, can miss the bound.
Values may be sent and summed in bfloat16 or wider, within the bound.
No kernel may reach another device: no remote copies, remote signals or barrier semaphores. Data moves between devices by JAX's collectives and lax.ppermute only.
A program may use at most 384 MiB of HBM per device.

```python
import math
import jax
import jax.numpy as jnp
from jax import lax

D = 1024
HEADS = 16
HEAD_DIM = 64
RANK_Q = 6
RANK_KV = 2
FF = 2816
SEQ_LEN = 1024
NS_STEPS = 5
DOMAINS = 4
SEQS = 8
TOKENS = 8192
FACTOR_COLS = 800


def shard_levels(key, extent, split, smallest, top_value):
    factor_of, own = 1.0, jax.random.fold_in(key, 6)
    for position, parts in split:
        heights = jnp.exp(jax.random.uniform(jax.random.fold_in(own, position), (parts,), jnp.float32, smallest / len(split), top_value / len(split)))
        factor_of = factor_of * jnp.repeat(heights, extent[position] // parts).reshape([-1 if axis == position else 1 for axis in range(len(extent))])
    return factor_of


def choose_distinct(key, rows, amount, top, lift):
    order = jax.random.permutation(jax.random.fold_in(key, 1), amount)
    boost = order
    for power in range(3):
        boost = boost * boost // amount
    boost = boost * lift // amount
    tickets = jax.random.randint(jax.random.fold_in(key, 2), (rows, amount), 0, 4096) + boost
    fixed_rows = jax.random.permutation(jax.random.fold_in(key, 3), rows)[jnp.arange(amount) % rows]
    tickets = jnp.where(jnp.arange(rows)[:, None] == fixed_rows[None, :], 1 << 14, tickets)
    score = tickets * amount + jnp.arange(amount)
    return lax.top_k(score.astype(jnp.int32), top)[1].astype(jnp.int32)


def normal_values(own_key, shape, spread, most, split=(), kind=jnp.bfloat16):
    factor_of = shard_levels(own_key, shape, split, -0.22, 0.18) if split else 1.0
    array = jax.random.normal(own_key, shape, jnp.float32) * spread * factor_of
    return jnp.minimum(jnp.maximum(array, -most), most).astype(kind)


def setup_inputs(seed: int = 0) -> dict:
    key_list = jax.random.split(jax.random.key(seed), 15)
    tokens = normal_values(key_list[0], (TOKENS, D), 1.0, 6.0, ((0, 32),))
    cotangent = normal_values(key_list[1], (TOKENS, D), 1.0, 6.0, ((0, 32),))
    domain_ids = choose_distinct(key_list[2], SEQS, DOMAINS, 1, 0)
    domain_weight = jnp.clip(jnp.exp(jax.random.uniform(key_list[3], (DOMAINS,), jnp.float32, math.log(0.5), math.log(2.0))), 0.5, 2.0)
    gains = jnp.clip(1.0 + 0.1 * jax.random.normal(key_list[4], (2, D), jnp.float32), 0.5, 1.5)
    gain_mom = normal_values(key_list[5], (2, D), (0.5 * (SEQS * SEQ_LEN) ** 0.5), 256.0, ((1, 4),), jnp.float32)
    factor_w = normal_values(key_list[6], (D, FACTOR_COLS), (D // 2) ** -0.5, 0.25, ((0, 4),), jnp.float32)
    factor_mom = normal_values(key_list[7], (D, FACTOR_COLS), (0.3 * (SEQS * SEQ_LEN) ** 0.5), 160.0, ((0, 4),), jnp.float32)
    out_w = normal_values(key_list[8], (D, D), (D // 16) ** -0.5, 0.75, ((0, 4),), jnp.float32)
    out_mom = normal_values(key_list[9], (D, D), (0.3 * (SEQS * SEQ_LEN) ** 0.5), 160.0, ((0, 4),), jnp.float32)
    gate_up_w = normal_values(key_list[10], (2, D, FF), D ** -0.5, 0.1875, ((1, 4), (2, 8)), jnp.float32)
    gate_up_mom = normal_values(key_list[11], (2, D, FF), (0.3 * (SEQS * SEQ_LEN) ** 0.5), 160.0, ((1, 4), (2, 8)), jnp.float32)
    down_w = normal_values(key_list[12], (FF, D), FF ** -0.5, 0.109375, ((0, 8), (1, 4)), jnp.float32)
    down_mom = normal_values(key_list[13], (FF, D), (0.3 * (SEQS * SEQ_LEN) ** 0.5), 160.0, ((0, 8), (1, 4)), jnp.float32)
    return dict(tokens=tokens, cotangent=cotangent, domain_ids=domain_ids, domain_weight=domain_weight, gains=gains, gain_mom=gain_mom, factor_w=factor_w, factor_mom=factor_mom, out_w=out_w, out_mom=out_mom, gate_up_w=gate_up_w, gate_up_mom=gate_up_mom, down_w=down_w, down_mom=down_mom)


EPS = 1e-06
NS_EPS = 1e-07
MOMENTUM = 0.5
LEARN = 0.2
LEARN_VEC = 0.002
COEF_A = 3.4445
COEF_B = -4.775
COEF_C = 2.0315
NEG = -1e+30
HIGH_PRECISION = lax.Precision.HIGHEST

@jax.custom_vjp
def low(v):
    return lax.optimization_barrier(v.astype(jnp.bfloat16)).astype(jnp.float32)

@jax.custom_vjp
def low_back(v):
    return v

def low_keep(v):
    return (low(v), None)

def low_pass(kept, grad):
    return (grad,)

def back_keep(v):
    return (v, None)

def back_low(kept, grad):
    return (low(grad),)
low.defvjp(low_keep, low_pass)
low_back.defvjp(back_keep, back_low)

def exact(left_mat, right_mat):
    return jnp.dot(left_mat, right_mat, precision=HIGH_PRECISION)

def rms_norm(values, gain):
    return values * lax.rsqrt(lax.optimization_barrier(jnp.mean(values * values, axis=-1, keepdims=True)) + EPS) * gain

def factor_widths():
    return [RANK_Q * HEADS, RANK_KV * HEADS, RANK_KV * HEADS, RANK_Q * HEAD_DIM, RANK_KV * HEAD_DIM, RANK_KV * HEAD_DIM]

def split_blocks(matrix):
    pieces = []
    offset = 0
    for block_width in factor_widths():
        pieces.append(matrix[..., offset:offset + block_width])
        offset = offset + block_width
    return pieces

def compose(heads_part, dims_part, rank):
    row_count = heads_part.shape[0]
    left_part = heads_part.reshape(row_count, rank, HEADS)
    right_part = dims_part.reshape(row_count, rank, HEAD_DIM)
    return jnp.einsum('trh,trd->thd', left_part, right_part, precision=HIGH_PRECISION) / rank

def attend(queries, key_vecs, values):
    scores = jnp.einsum('qhd,khd->hqk', queries, key_vecs, precision=HIGH_PRECISION) * HEAD_DIM ** (-0.5)
    scores = low_back(scores)
    places = jnp.arange(SEQ_LEN, dtype=jnp.int32)
    allowed = places[None, :] <= places[:, None]
    scores = jnp.where(allowed[None, :, :], scores, NEG)
    probability = low(jax.nn.softmax(scores, axis=-1))
    return jnp.einsum('hqk,khd->qhd', probability, values, precision=HIGH_PRECISION)

def layer(inputs, gains, factor_w, out_w, gate_up_w, down_w):
    row_count = inputs.shape[0]
    first_in = low(rms_norm(inputs, gains[0]))
    factors = low_back(exact(first_in, low(factor_w)))
    head_q, head_k, head_v, dim_q, dim_k, dim_v = split_blocks(factors)
    queries = low(compose(head_q, dim_q, RANK_Q))
    key_vecs = low(compose(head_k, dim_k, RANK_KV))
    values = low(compose(head_v, dim_v, RANK_KV))
    seq_shape = (row_count // SEQ_LEN, SEQ_LEN, HEADS, HEAD_DIM)
    attended = lax.map(jax.checkpoint(lambda triple: attend(triple[0], triple[1], triple[2])), (queries.reshape(seq_shape), key_vecs.reshape(seq_shape), values.reshape(seq_shape)))
    attended = low(low_back(attended.reshape(row_count, D)))
    residual = inputs + low_back(exact(attended, low(out_w)))
    second_in = low(rms_norm(residual, gains[1]))
    gate_value = low_back(exact(second_in, low(gate_up_w[0])))
    upward = low_back(exact(second_in, low(gate_up_w[1])))
    hidden = low(jax.nn.silu(gate_value) * upward)
    return residual + low_back(exact(hidden, low(down_w)))

def orthogonal(matrix):
    iterate = matrix / (jnp.sqrt(jnp.sum(matrix * matrix)) + NS_EPS)
    for iteration in range(NS_STEPS):
        if iterate.shape[0] <= iterate.shape[1]:
            gram_mat = exact(iterate, iterate.T)
            iterate = COEF_A * iterate + exact(COEF_B * gram_mat + COEF_C * exact(gram_mat, gram_mat), iterate)
        else:
            gram_mat = exact(iterate.T, iterate)
            iterate = COEF_A * iterate + exact(iterate, COEF_B * gram_mat + COEF_C * exact(gram_mat, gram_mat))
    return iterate

def muon(weight, momentum, gradient):
    fresh = MOMENTUM * momentum + gradient
    rate = LEARN * 0.2 * math.sqrt(max(weight.shape[0], weight.shape[1]))
    return (fresh, weight - rate * orthogonal(fresh))

def reference(tokens, cotangent, domain_ids, domain_weight, gains, gain_mom, factor_w, factor_mom, out_w, out_mom, gate_up_w, gate_up_mom, down_w, down_mom):
    seq_weight = domain_weight[domain_ids[:, 0]]
    row_weight = jnp.repeat(seq_weight, SEQ_LEN)
    group_count = SEQS
    group_rows = SEQ_LEN
    inputs = tokens.astype(jnp.float32).reshape(group_count, group_rows, D)
    cotangents = (cotangent.astype(jnp.float32) * row_weight[:, None]).reshape(group_count, group_rows, D)
    params = (gains, factor_w, out_w, gate_up_w, down_w)

    def one_group(summed, group_pair):
        outputs, pullback = jax.vjp(layer, group_pair[0], gains, factor_w, out_w, gate_up_w, down_w)
        gradients = pullback(group_pair[1])
        summed = tuple((running + fresh for running, fresh in zip(summed, gradients[1:])))
        return (summed, (outputs.astype(jnp.bfloat16), gradients[0]))
    zero_grads = tuple((jnp.zeros_like(param) for param in params))
    gradients, (outs_low, input_grads) = lax.scan(one_group, zero_grads, (inputs, cotangents))
    block_out = outs_low.reshape(TOKENS, D)
    input_grad = input_grads.reshape(TOKENS, D)
    gain_grad = gradients[0]
    new_gain_mom = MOMENTUM * gain_mom + gain_grad
    new_gains = gains - LEARN_VEC * new_gain_mom
    mom_pieces = []
    weight_pieces = []
    for weight_piece, mom_piece, grad_piece in zip(split_blocks(factor_w), split_blocks(factor_mom), split_blocks(gradients[1])):
        fresh_mom, fresh_weight = muon(weight_piece, mom_piece, grad_piece)
        mom_pieces.append(fresh_mom)
        weight_pieces.append(fresh_weight)
    new_factor_mom = jnp.concatenate(mom_pieces, axis=1)
    new_factor_w = jnp.concatenate(weight_pieces, axis=1)
    new_out_mom, new_out_w = muon(out_w, out_mom, gradients[2])
    gate_mom, gate_new = muon(gate_up_w[0], gate_up_mom[0], gradients[3][0])
    up_mom, up_new = muon(gate_up_w[1], gate_up_mom[1], gradients[3][1])
    new_gate_up_mom = jnp.stack([gate_mom, up_mom])
    new_gate_up_w = jnp.stack([gate_new, up_new])
    new_down_mom, new_down_w = muon(down_w, down_mom, gradients[4])
    return (block_out, input_grad, gain_grad, new_gains, new_gain_mom, new_factor_mom, new_factor_w, new_out_mom, new_out_w, new_gate_up_mom, new_gate_up_w, new_down_mom, new_down_w)
```

```python
import math
import jax
import jax.numpy as jnp
from jax import lax
from jax.experimental import pallas as pl
from jax.experimental.pallas import tpu as pltpu
BF=jnp.bfloat16; F32=jnp.float32
HEADS=16; HD=64; RQ=6; RK=2; D=1024
COEF_A=3.4445; COEF_B=-4.775; COEF_C=2.0315
NEG=-1e30

def split2(x):
    hi=x.astype(BF); return hi,(x-hi.astype(F32)).astype(BF)
def dot(a,b): return jnp.dot(a,b,preferred_element_type=F32)
def dot_nt(a,b): return lax.dot_general(a,b,(((1,),(1,)),((),())),preferred_element_type=F32)
def dot_tn(a,b): return lax.dot_general(a,b,(((0,),(0,)),((),())),preferred_element_type=F32)

def spread(shape, pair, rank):
    rows=lax.broadcasted_iota(jnp.int32,shape,0); lanes=lax.broadcasted_iota(jnp.int32,shape,1)
    return (rows==rank*HEADS+2*pair+lanes//HD).astype(BF)

def dup(dims,r):
    part=dims[:,r*HD:(r+1)*HD]
    return jnp.concatenate([part,part],axis=1)

def attn_fwd_body(base_ref,head_q,dim_q,head_k,dim_k,head_v,dim_v,o_ref,lse_ref,q_ref,k_ref,v_ref,bias_ref,hq,hk,hv,dq,dk,dv):
    rows,keys=o_ref.shape[0],k_ref.shape[0]
    r_id=lax.broadcasted_iota(jnp.int32,(rows,keys),0)+base_ref[0]*rows
    c_id=lax.broadcasted_iota(jnp.int32,(rows,keys),1)
    bias_ref[...]=jnp.where(c_id<=r_id,0.0,NEG)
    for src,dst in ((head_q,hq),(head_k,hk),(head_v,hv)):
        dst[0],dst[1]=split2(src[...])
    for src,dst,rank in ((dim_q,dq,RQ),(dim_k,dk,RK),(dim_v,dv,RK)):
        for r in range(rank):
            dst[r]=dup(src[...],r)*(1.0/rank)
    def compose(h,d,rank,pair):
        total=None
        for r in range(rank):
            e=spread((rank*HEADS,128),pair,r)
            term=(dot(h[0],e)+dot(h[1],e))*d[r]
            total=term if total is None else total+term
        return total.astype(BF)
    lane=lax.broadcasted_iota(jnp.int32,(1,128),1)
    def step(pair,_):
        cols=pl.ds(pl.multiple_of(pair*128,128),128)
        q=compose(hq,dq,RQ,pair); k=compose(hk,dk,RK,pair); v=compose(hv,dv,RK,pair)
        q_ref[:,cols]=q; k_ref[:,cols]=k; v_ref[:,cols]=v
        qs=q.astype(F32)*(HD**-0.5)
        out=None
        for half in range(2):
            keep=(lane//HD)==half
            qm=jnp.where(keep,qs,0.0).astype(BF)
            s=dot_nt(qm,k)+bias_ref[...]
            m=jnp.max(s,axis=1,keepdims=True)
            e=jnp.exp(s-m)
            l=jnp.sum(e,axis=1,keepdims=True)
            p=(e*(1.0/l)).astype(BF)
            o=dot(p,v)
            out=o if half==0 else jnp.where(keep,o,out)
            lse=m+jnp.log(l)
            col=lax.broadcasted_iota(jnp.int32,(1,HEADS),1)==2*pair+half
            lse_ref[...]=jnp.where(col,lse,lse_ref[...])
        o_ref[:,cols]=out.astype(BF)
        return 0
    lse_ref[...]=jnp.zeros_like(lse_ref)
    lax.fori_loop(0,HEADS//2,step,0)

def attn_fwd(base,head_q,dim_q,head_k,dim_k,head_v,dim_v,interpret=False):
    rows,keys=head_q.shape[0],head_k.shape[0]
    vm=pl.BlockSpec(memory_space=pltpu.VMEM)
    return pl.pallas_call(attn_fwd_body,
        out_shape=(jax.ShapeDtypeStruct((rows,D),BF),jax.ShapeDtypeStruct((rows,HEADS),F32),jax.ShapeDtypeStruct((rows,D),BF),jax.ShapeDtypeStruct((keys,D),BF),jax.ShapeDtypeStruct((keys,D),BF)),
        in_specs=[pl.BlockSpec(memory_space=pltpu.SMEM)]+[vm]*6,
        out_specs=(vm,)*5,
        scratch_shapes=[pltpu.VMEM((rows,keys),F32),pltpu.VMEM((2,rows,RQ*HEADS),BF),pltpu.VMEM((2,keys,RK*HEADS),BF),pltpu.VMEM((2,keys,RK*HEADS),BF),
          pltpu.VMEM((RQ,rows,128),F32),pltpu.VMEM((RK,keys,128),F32),pltpu.VMEM((RK,keys,128),F32)],
        compiler_params=pltpu.CompilerParams(vmem_limit_bytes=48<<20),name="attn_fwd",interpret=interpret,
    )(base,head_q,dim_q,head_k,dim_k,head_v,dim_v)

def attn_bwd_body(base_ref,q_ref,k_ref,v_ref,do_ref,lse_ref,head_q,dim_q,head_k,dim_k,head_v,dim_v,
                  dhq_ref,ddq_ref,dhk_ref,ddk_ref,dhv_ref,ddv_ref,bias_ref,hq,hk,hv,dq,dk,dv,aq,ak,av):
    rows,keys=q_ref.shape[0],k_ref.shape[0]
    r_id=lax.broadcasted_iota(jnp.int32,(rows,keys),0)+base_ref[0]*rows
    c_id=lax.broadcasted_iota(jnp.int32,(rows,keys),1)
    bias_ref[...]=jnp.where(c_id<=r_id,0.0,NEG)
    for src,dst in ((head_q,hq),(head_k,hk),(head_v,hv)):
        dst[0],dst[1]=split2(src[...])
    for src,dst,rank in ((dim_q,dq,RQ),(dim_k,dk,RK),(dim_v,dv,RK)):
        for r in range(rank):
            dst[r]=dup(src[...],r)
    for ref in (aq,ak,av,dhq_ref,dhk_ref,dhv_ref): ref[...]=jnp.zeros_like(ref)
    lane=lax.broadcasted_iota(jnp.int32,(1,128),1)
    def back(grad,h,d,acc,dh_ref,rank,pair):
        total=None
        for r in range(rank):
            e=spread((rank*HEADS,128),pair,r)
            acc[r]+=grad*(dot(h[0],e)+dot(h[1],e))
            hi,lo=split2(grad*d[r])
            t=dot_nt(hi,e)+dot_nt(lo,e)
            total=t if total is None else total+t
        dh_ref[...]+=total
    def step(pair,_):
        cols=pl.ds(pl.multiple_of(pair*128,128),128)
        q=q_ref[:,cols]; k=k_ref[:,cols]; v=v_ref[:,cols]; do=do_ref[:,cols]
        qs=q.astype(F32)*(HD**-0.5); dof=do.astype(F32)
        gq=gk=gv=None
        for half in range(2):
            keep=(lane//HD)==half
            qm=jnp.where(keep,qs,0.0).astype(BF); dom=jnp.where(keep,dof,0.0).astype(BF)
            col=lax.broadcasted_iota(jnp.int32,(1,HEADS),1)==2*pair+half
            lse=jnp.sum(jnp.where(col,lse_ref[...],0.0),axis=1,keepdims=True)
            p=jnp.exp(dot_nt(qm,k)+bias_ref[...]-lse)
            dp=dot_nt(dom,v)
            inner=jnp.sum(p*dp,axis=1,keepdims=True)
            ds=(p*(dp-inner)).astype(BF)
            nq=dot(ds,k); nk=dot_tn(ds,qm); nv=dot_tn(p.astype(BF),dom)
            if half==0: gq,gk,gv=nq,nk,nv
            else:
                gq=jnp.where(keep,nq,gq); gk=gk+nk; gv=gv+nv
        scale=HD**-0.5
        back(gq*(scale/RQ),hq,dq,aq,dhq_ref,RQ,pair)
        back(gk*(1.0/RK),hk,dk,ak,dhk_ref,RK,pair)
        back(gv*(1.0/RK),hv,dv,av,dhv_ref,RK,pair)
        return 0
    lax.fori_loop(0,HEADS//2,step,0)
    for acc,ref,rank in ((aq,ddq_ref,RQ),(ak,ddk_ref,RK),(av,ddv_ref,RK)):
        for r in range(rank):
            ref[:,r*HD:(r+1)*HD]=acc[r][:,:HD]+acc[r][:,HD:]

def attn_bwd(base,q,k,v,do,lse,head_q,dim_q,head_k,dim_k,head_v,dim_v,interpret=False):
    rows,keys=q.shape[0],k.shape[0]
    vm=pl.BlockSpec(memory_space=pltpu.VMEM)
    sd=jax.ShapeDtypeStruct
    return pl.pallas_call(attn_bwd_body,
        out_shape=(sd((rows,RQ*HEADS),F32),sd((rows,RQ*HD),F32),sd((keys,RK*HEADS),F32),sd((keys,RK*HD),F32),sd((keys,RK*HEADS),F32),sd((keys,RK*HD),F32)),
        in_specs=[pl.BlockSpec(memory_space=pltpu.SMEM)]+[vm]*11,
        out_specs=(vm,)*6,
        scratch_shapes=[pltpu.VMEM((rows,keys),F32),pltpu.VMEM((2,rows,RQ*HEADS),BF),pltpu.VMEM((2,keys,RK*HEADS),BF),pltpu.VMEM((2,keys,RK*HEADS),BF),
          pltpu.VMEM((RQ,rows,128),F32),pltpu.VMEM((RK,keys,128),F32),pltpu.VMEM((RK,keys,128),F32),
          pltpu.VMEM((RQ,rows,128),F32),pltpu.VMEM((RK,keys,128),F32),pltpu.VMEM((RK,keys,128),F32)],
        compiler_params=pltpu.CompilerParams(vmem_limit_bytes=56<<20),name="attn_bwd",interpret=interpret,
    )(base,q,k,v,do,lse,head_q,dim_q,head_k,dim_k,head_v,dim_v)

BK=256
def tri_cols(j): return (j*(j+1)//2)*BK

def store_sym(hi,lo,i,j,val):
    h,l=split2(val)
    hi[i*BK:(i+1)*BK,j*BK:(j+1)*BK]=h; lo[i*BK:(i+1)*BK,j*BK:(j+1)*BK]=l
    if i!=j:
        t=val.T
        h,l=split2(t)
        hi[j*BK:(j+1)*BK,i*BK:(i+1)*BK]=h; lo[j*BK:(j+1)*BK,i*BK:(i+1)*BK]=l

def mul_upper(xh,xl,yh,yl,n,emit):
    for j in range(n):
        top=(j+1)*BK; cs=slice(j*BK,(j+1)*BK)
        r=dot(xh[:top,:],yh[:,cs])+dot(xh[:top,:],yl[:,cs])+dot(xl[:top,:],yh[:,cs])
        for i in range(j+1): emit(i,j,r[i*BK:(i+1)*BK])

def ns_body(g_ref,y_ref,o_ref,a_up,ah,al,ph,pw,bh,bl):
    n=o_ref.shape[1]//BK
    eye=(lax.broadcasted_iota(jnp.int32,(BK,BK),0)==lax.broadcasted_iota(jnp.int32,(BK,BK),1)).astype(F32)
    blk=lambda i,j:(slice(i*BK,(i+1)*BK),slice(j*BK,(j+1)*BK))
    trace=None
    for j in range(n):
        off=tri_cols(j)+j*BK
        part=g_ref[:,off:off+BK]*eye
        trace=part if trace is None else trace+part
    trace=jnp.sum(jnp.sum(trace,axis=1,keepdims=True),axis=0,keepdims=True)
    scale=1.0/(jnp.sqrt(trace)+1e-7)
    for j in range(n):
        for i in range(j+1):
            off=tri_cols(j)+i*BK
            val=g_ref[:,off:off+BK]*(scale*scale)
            a_up[blk(i,j)]=val; store_sym(ah,al,i,j,val)
    o_ref[...]=y_ref[...]*scale
    def poly():
        def emit(i,j,c):
            store_sym(ph,pw,i,j,COEF_B*a_up[blk(i,j)]+COEF_C*c)
        mul_upper(ah,al,ah,al,n,emit)
    def apply():
        y=o_ref[...]; yh,yl=split2(y)
        o_ref[...]=COEF_A*y+(dot(yh,ph[...])+dot(yh,pw[...])+dot(yl,ph[...]))
    def step(_,c):
        poly()
        apply()
        def emit_b(i,j,m):
            val=COEF_A*a_up[blk(i,j)]+m
            a_up[blk(i,j)]=val; store_sym(bh,bl,i,j,val)
        mul_upper(ah,al,ph,pw,n,emit_b)
        def emit_a(i,j,m):
            val=COEF_A*a_up[blk(i,j)]+m
            a_up[blk(i,j)]=val; store_sym(ah,al,i,j,val)
        mul_upper(bh,bl,ph,pw,n,emit_a)
        return c
    lax.fori_loop(0,4,step,0)
    poly(); apply()

def ns_big(gram,y,interpret=False):
    w,d=y.shape
    vm=pl.BlockSpec(memory_space=pltpu.VMEM)
    return pl.pallas_call(ns_body,out_shape=jax.ShapeDtypeStruct((w,d),F32),
        in_specs=[vm,vm],out_specs=vm,
        scratch_shapes=[pltpu.VMEM((d,d),F32)]+[pltpu.VMEM((d,d),BF)]*6,
        compiler_params=pltpu.CompilerParams(vmem_limit_bytes=56<<20),name="ns_gram",interpret=interpret)(gram,y)

def gram_body(y_ref,g_ref):
    n=y_ref.shape[1]//BK
    yh,yl=split2(y_ref[...])
    for j in range(n):
        top=(j+1)*BK; cs=slice(j*BK,top)
        r=dot_tn(yh[:,:top],yh[:,cs])+dot_tn(yh[:,:top],yl[:,cs])+dot_tn(yl[:,:top],yh[:,cs])
        for i in range(j+1):
            off=tri_cols(j)+i*BK
            g_ref[:,off:off+BK]=r[i*BK:(i+1)*BK]

def gram_upper(y,interpret=False):
    d=y.shape[1]; n=d//BK
    vm=pl.BlockSpec(memory_space=pltpu.VMEM)
    return pl.pallas_call(gram_body,out_shape=jax.ShapeDtypeStruct((BK,n*(n+1)//2*BK),F32),in_specs=[vm],out_specs=vm,
        compiler_params=pltpu.CompilerParams(vmem_limit_bytes=48<<20),name="gram_upper",interpret=interpret)(y)

def mm3(x,y,f=dot):
    xh,xl=split2(x); yh,yl=split2(y)
    return f(xh,yh)+f(xh,yl)+f(xl,yh)

HEAD_SEGS=(RQ*HEADS,RK*HEADS,RK*HEADS)
def seg_mask(n,widths):
    def ids(axis):
        pos=lax.broadcasted_iota(jnp.int32,(n,n),axis); out=jnp.zeros_like(pos); edge=0
        for w in widths:
            edge+=w; out=out+(pos>=edge).astype(jnp.int32)
        return out
    return (ids(0)==ids(1)).astype(F32)

def ns_factor_body(fh_ref,fd_ref,oh_ref,od_ref,rh_ref,rd_ref):
    nh=fh_ref.shape[1]
    wq=RQ*HD; wk=RK*HD
    groups=((fh_ref,oh_ref,rh_ref,slice(0,nh),HEAD_SEGS),(fd_ref,od_ref,rd_ref,slice(0,wq),(wq,)),(fd_ref,od_ref,rd_ref,slice(wq,wq+2*wk),(wk,wk)))
    for full,own,out,cs,widths in groups:
        n=cs.stop-cs.start
        mask=seg_mask(n,widths)
        eye=(lax.broadcasted_iota(jnp.int32,(n,n),0)==lax.broadcasted_iota(jnp.int32,(n,n),1)).astype(F32)
        a=mm3(full[:,cs],full[:,cs],dot_tn)*mask
        diag=a*eye
        row=jnp.sum(mask*jnp.sum(diag,axis=1,keepdims=True),axis=0,keepdims=True)
        col=jnp.sum(mask*jnp.sum(diag,axis=0,keepdims=True),axis=1,keepdims=True)
        row=1.0/(jnp.sqrt(row)+1e-7); col=1.0/(jnp.sqrt(col)+1e-7)
        a=a*row*col; x=own[:,cs]*row
        def step(_,c):
            a,x=c
            p=COEF_B*a+COEF_C*mm3(a,a)
            x=COEF_A*x+mm3(x,p)
            b=COEF_A*a+mm3(a,p)
            return COEF_A*b+mm3(b,p),x
        a,x=lax.fori_loop(0,4,step,(a,x))
        out[:,cs]=COEF_A*x+mm3(x,COEF_B*a+COEF_C*mm3(a,a))

def ns_factor(fh,fd,oh,od,interpret=False):
    vm=pl.BlockSpec(memory_space=pltpu.VMEM)
    return pl.pallas_call(ns_factor_body,out_shape=(jax.ShapeDtypeStruct(oh.shape,F32),jax.ShapeDtypeStruct(od.shape,F32)),in_specs=[vm]*4,out_specs=(vm,vm),
        compiler_params=pltpu.CompilerParams(vmem_limit_bytes=48<<20),name="ns_factor",interpret=interpret)(fh,fd,oh,od)


EPS = 1e-06
MOMENTUM = 0.5
LEARN = 0.2
LEARN_VEC = 0.002
P = jax.sharding.PartitionSpec
NQ, NK = RQ * HEADS, RK * HEADS
WQ, WK = RQ * HD, RK * HD
FFN = 3


def normalize(values):
    row_scale = lax.rsqrt(jnp.mean(values * values, axis=-1, keepdims=True) + EPS)
    return values * row_scale, row_scale


def norm_back(grad_in, normed, row_scale, gain):
    scaled = grad_in * gain
    inner_sum = jnp.mean(scaled * normed, axis=-1, keepdims=True)
    return row_scale * (scaled - normed * inner_sum), jnp.sum(grad_in * normed, axis=0)


def dp_pairs(shift, keep=lambda target: True):
    return [(j, j ^ shift) for j in range(lax.axis_size("dp")) if keep(j ^ shift)]


def place(parts, axis):
    me = lax.axis_index("dp")
    step = parts[0].shape[axis]
    shape = list(parts[0].shape)
    shape[axis] *= len(parts)
    out = jnp.zeros(shape, parts[0].dtype)
    for shift, part in enumerate(parts):
        out = lax.dynamic_update_slice_in_dim(out, part, (me ^ shift) * step, axis)
    return out


def gather_dp(own, axis=0):
    return place([own] + [lax.ppermute(own, "dp", dp_pairs(s)) for s in range(1, lax.axis_size("dp"))], axis)


def scatter_mp(partial):
    mp = lax.axis_size("mp")
    if mp != 8:
        return lax.psum_scatter(partial, "mp", scatter_dimension=0, tiled=True)
    me = lax.axis_index("mp")
    rows = partial.shape[0] // mp
    blocks = partial.reshape(mp // 2, 2, rows, partial.shape[1])
    core, place_z = me % 2, me // 2
    away = lax.dynamic_index_in_dim(blocks, 1 - core, 1, keepdims=False).astype(BF)
    near = lax.dynamic_index_in_dim(blocks, core, 1, keepdims=False)
    near = near + lax.ppermute(away, "mp", [(j, j ^ 1) for j in range(mp)]).astype(F32)
    total = lax.dynamic_index_in_dim(near, place_z, 0, keepdims=False)
    for shift in range(1, mp // 2):
        block = lax.dynamic_index_in_dim(near, place_z ^ shift, 0, keepdims=False).astype(BF)
        total = total + lax.ppermute(block, "mp", [(j, j ^ (2 * shift)) for j in range(mp)]).astype(F32)
    return total


def body(
    tokens,
    cotangent,
    domain_ids,
    domain_weight,
    gains,
    gain_mom,
    factor_w,
    factor_mom,
    out_w,
    out_mom,
    gate_up_w,
    gate_up_mom,
    down_w,
    down_mom,
):
    n_dp, n_mp = lax.axis_size("dp"), lax.axis_size("mp")
    me, mz = lax.axis_index("dp"), lax.axis_index("mp")
    rows = tokens.shape[0]
    d_own = factor_w.shape[0]
    hidden_own = gate_up_w.shape[2]
    out_own = D // n_mp
    base = me.astype(jnp.int32).reshape(1)
    shifts = range(1, n_dp)
    ffn_slot = jnp.minimum(me, FFN - 1)

    factor_low = gather_dp(factor_w.astype(BF))
    x_float = tokens.astype(F32)
    first_normed, first_scale = normalize(x_float)
    first_own = (first_normed * gains[0]).astype(BF)
    factors = dot(first_own, factor_low)
    heads_q, heads_kv = factors[:, :NQ], factors[:, NQ : NQ + 2 * NK]
    dims_q, dims_kv = factors[:, NQ + 2 * NK : NQ + 2 * NK + WQ], factors[:, NQ + 2 * NK + WQ :]
    kv_all = gather_dp(jnp.concatenate([heads_kv, dims_kv], axis=1))
    parts = (
        heads_q,
        dims_q,
        kv_all[:, :NK],
        kv_all[:, 2 * NK : 2 * NK + WK],
        kv_all[:, NK : 2 * NK],
        kv_all[:, 2 * NK + WK :],
    )
    attended, lse, queries, key_vecs, values = attn_fwd(base, *parts)
    out_low = lax.all_gather(out_w.astype(BF), "dp", axis=0, tiled=True)
    residual = x_float + dot(attended, out_low)
    second_normed, second_scale = normalize(residual)

    ffn_old = jnp.stack([gate_up_w[0], gate_up_w[1], down_w.T])
    ffn_low = lax.all_gather(ffn_old.astype(BF), "dp", axis=1, tiled=True)
    gate_low, up_low, down_low = ffn_low[0], ffn_low[1], ffn_low[2]
    domain_range = jnp.arange(domain_weight.shape[0], dtype=jnp.int32)
    seq_weight = jnp.sum(jnp.where(domain_ids[0, 0] == domain_range, domain_weight, 0.0))
    d_output = cotangent.astype(F32) * seq_weight
    d_output_all = lax.all_gather(d_output.astype(BF), "mp", axis=0, tiled=True)
    second_in = lax.all_gather((second_normed * gains[1]).astype(BF), "mp", axis=0, tiled=True)
    gate_value = dot(second_in, gate_low)
    upward = dot(second_in, up_low)
    sigmoid_gate = jax.nn.sigmoid(gate_value)
    active = gate_value * sigmoid_gate
    hidden = (active * upward).astype(BF)
    d_hidden = dot(d_output_all, down_low)
    d_gate = (d_hidden * upward * sigmoid_gate * (1.0 + gate_value * (1.0 - sigmoid_gate))).astype(BF)
    d_upward = (d_hidden * active).astype(BF)
    d_second = scatter_mp(dot_nt(d_gate, gate_low) + dot_nt(d_upward, up_low))
    grads = jnp.stack([dot_tn(d_gate, second_in), dot_tn(d_upward, second_in), dot_tn(hidden, d_output_all)])
    branch = scatter_mp(dot_nt(hidden, down_low))
    block_out = (residual + branch).astype(BF)

    ffn_mom = jnp.stack([gate_up_mom[0].T, gate_up_mom[1].T, down_mom])
    to_ffn = lambda target: target < FFN
    own_mom = [lax.dynamic_index_in_dim(ffn_mom, ffn_slot, 0, keepdims=False)]
    matrix = lax.dynamic_index_in_dim(grads, ffn_slot, 0, keepdims=False)
    for s in shifts:
        slot = jnp.minimum(me ^ s, FFN - 1)
        own_mom.append(lax.ppermute(lax.dynamic_index_in_dim(ffn_mom, slot, 0, keepdims=False), "dp", dp_pairs(s, to_ffn)))
        matrix = matrix + lax.ppermute(lax.dynamic_index_in_dim(grads, slot, 0, keepdims=False), "dp", dp_pairs(s, to_ffn))
    matrix = matrix + MOMENTUM * place(own_mom, 1)

    d_resid_norm, gain_second = norm_back(d_second, second_normed, second_scale, gains[1])
    d_residual = d_output + d_resid_norm
    d_residual_low = d_residual.astype(BF)
    grad_out = None
    for s in range(n_dp):
        cols = lax.dynamic_slice_in_dim(attended, (me ^ s) * d_own, d_own, 1)
        block = dot_tn(d_residual_low, cols)
        if s:
            block = lax.ppermute(block, "dp", dp_pairs(s))
        grad_out = block if grad_out is None else grad_out + block
    grad_out = lax.psum_scatter(grad_out, "mp", scatter_dimension=0, tiled=True)
    out_tile = MOMENTUM * lax.dynamic_slice_in_dim(out_mom, mz * out_own, out_own, 1).T + grad_out
    new_out_mom = lax.all_gather(out_tile, "mp", axis=0, tiled=True).T
    out_rows = place([out_tile] + [lax.ppermute(out_tile, "dp", [(j ^ s, j) for j in range(FFN, n_dp)]) for s in shifts], 1)
    out_rows = jnp.pad(out_rows, ((0, hidden_own - out_own), (0, 0)))
    matrix = jnp.where(me < FFN, matrix, out_rows)
    gram = lax.psum(gram_upper(matrix), "mp")
    ortho = ns_big(gram, matrix)

    def give_back(whole):
        pieces = [lax.dynamic_slice_in_dim(whole, (me ^ s) * d_own, d_own, 1) for s in range(n_dp)]
        return place([pieces[0][None]] + [lax.ppermute(pieces[s], "dp", dp_pairs(s))[None] for s in shifts], 0)

    mom_back = give_back(matrix)
    ortho_back = give_back(ortho)
    turn = lambda stack: jnp.stack([stack[0].T, stack[1].T])
    ffn_rate = LEARN * 0.2 * math.sqrt(max(D, hidden_own * n_mp))
    new_gate_up_mom, new_down_mom = turn(mom_back), mom_back[2]
    new_gate_up_w = gate_up_w - ffn_rate * turn(ortho_back)
    new_down_w = down_w - ffn_rate * ortho_back[2]
    out_ortho = lax.all_gather(ortho_back[FFN, :out_own], "mp", axis=0, tiled=True).T
    new_out_w = out_w - LEARN * 0.2 * math.sqrt(D) * out_ortho

    d_attended = dot_nt(d_residual_low, out_low).astype(BF)
    dq_heads, dq_dims, dk_heads, dk_dims, dv_heads, dv_dims = attn_bwd(
        base, queries, key_vecs, values, d_attended, lse, *parts
    )
    d_kv_all = jnp.concatenate([dk_heads, dv_heads, dk_dims, dv_dims], axis=1)
    d_kv = None
    for s in range(n_dp):
        block = lax.dynamic_slice_in_dim(d_kv_all, (me ^ s) * rows, rows, 0)
        if s:
            block = lax.ppermute(block, "dp", dp_pairs(s))
        d_kv = block if d_kv is None else d_kv + block
    d_factors = jnp.concatenate([dq_heads, d_kv[:, : 2 * NK], dq_dims, d_kv[:, 2 * NK :]], axis=1).astype(BF)
    d_first = dot_nt(d_factors, factor_low)
    d_input_norm, gain_first = norm_back(d_first, first_normed, first_scale, gains[0])
    input_grad = d_residual + d_input_norm

    grad_factor = None
    for s in range(n_dp):
        cols = lax.dynamic_slice_in_dim(first_own, (me ^ s) * d_own, d_own, 1)
        block = dot_tn(cols, d_factors)
        if s:
            block = lax.ppermute(block, "dp", dp_pairs(s))
        grad_factor = block if grad_factor is None else grad_factor + block
    grad_factor = lax.psum(grad_factor, "mp")
    new_factor_mom = MOMENTUM * factor_mom + grad_factor
    head_cols = NQ + 2 * NK
    mom_heads = jnp.pad(new_factor_mom[:, :head_cols], ((0, 0), (0, 256 - head_cols)))
    mom_dims = new_factor_mom[:, head_cols:]
    factor_all = gather_dp(new_factor_mom)
    ortho_heads, ortho_dims = ns_factor(
        jnp.pad(factor_all[:, :head_cols], ((0, 0), (0, 256 - head_cols))), factor_all[:, head_cols:], mom_heads, mom_dims
    )
    widths = [NQ, NK, NK, WQ, WK, WK]
    factor_rate = jnp.concatenate([jnp.full((w,), LEARN * 0.2 * math.sqrt(max(D, w)), F32) for w in widths])
    new_factor_w = factor_w - factor_rate * jnp.concatenate([ortho_heads[:, :head_cols], ortho_dims], axis=1)

    gain_all = lax.psum(jnp.stack([gain_first, gain_second]), ("dp", "mp"))
    feature_count = gain_mom.shape[1]
    gain_grad = lax.dynamic_slice_in_dim(gain_all, me * feature_count, feature_count, 1)
    new_gain_mom = MOMENTUM * gain_mom + gain_grad
    new_gains = lax.dynamic_slice_in_dim(gains, me * feature_count, feature_count, 1) - LEARN_VEC * new_gain_mom
    return (
        block_out,
        input_grad,
        gain_grad,
        new_gains,
        new_gain_mom,
        new_factor_mom,
        new_factor_w,
        new_out_mom,
        new_out_w,
        new_gate_up_mom,
        new_gate_up_w,
        new_down_mom,
        new_down_w,
    )


def solution(mesh):
    token = P(("mp", "dp"), None)
    row = P("dp", None)
    ffn = P(None, "dp", "mp")
    down = P("mp", "dp")
    vec = P(None, "dp")
    return jax.shard_map(
        body,
        mesh=mesh,
        in_specs=(token, token, P("mp", None), P(), P(), vec, row, row, row, row, ffn, ffn, down, down),
        out_specs=(token, token, vec, vec, vec, row, row, row, row, ffn, ffn, down, down),
        check_vma=False,
    )
```

```python
import math
import jax
import jax.numpy as jnp
from jax import lax
from jax.experimental import pallas as pl
from jax.experimental.pallas import tpu as pltpu
BF=jnp.bfloat16; F32=jnp.float32
HEADS=16; HD=64; RQ=6; RK=2; D=1024
COEF_A=3.4445; COEF_B=-4.775; COEF_C=2.0315
NEG=-1e30
NS_STEPS=5

def split2(x):
    hi=x.astype(BF); return hi,(x-hi.astype(F32)).astype(BF)
def dot(a,b): return jnp.dot(a,b,preferred_element_type=F32)
def dot_nt(a,b): return lax.dot_general(a,b,(((1,),(1,)),((),())),preferred_element_type=F32)
def dot_tn(a,b): return lax.dot_general(a,b,(((0,),(0,)),((),())),preferred_element_type=F32)

def one_hot(rows, first, pair):
    row=lax.broadcasted_iota(jnp.int32,(rows,128),0); lane=lax.broadcasted_iota(jnp.int32,(rows,128),1)
    return (row==first+2*pair+(lane>=HD).astype(jnp.int32)).astype(BF)

def twice(dims,r,scale):
    part=dims[:,r*HD:(r+1)*HD]*scale
    return jnp.concatenate([part,part],axis=1)

WQ,WK=RQ*HD,RK*HD
NQ,NK=RQ*HEADS,RK*HEADS
SIDES=((0,RQ,0),(0,RK,0),(RK,RK,NK))

def attn_setup(base_ref,fq_ref,fk_ref,bias_ref,hq,hk,dq,dk,scaled):
    rows,keys=bias_ref.shape
    r_id=lax.broadcasted_iota(jnp.int32,(rows,keys),0)+base_ref[0]*rows
    c_id=lax.broadcasted_iota(jnp.int32,(rows,keys),1)
    bias_ref[...]=jnp.where(c_id<=r_id,0.0,NEG)
    hq[0],hq[1]=split2(fq_ref[:,WQ:]); hk[0],hk[1]=split2(fk_ref[:,2*WK:])
    for r in range(RQ): dq[r]=twice(fq_ref,r,1.0/RQ if scaled else 1.0)
    for r in range(2*RK): dk[r]=twice(fk_ref,r,1.0/RK if scaled else 1.0)

def attn_scratch(rows,keys):
    return [pltpu.VMEM((rows,keys),F32),pltpu.VMEM((2,rows,NQ),BF),pltpu.VMEM((2,keys,2*NK),BF),pltpu.VMEM((RQ,rows,128),F32),pltpu.VMEM((2*RK,keys,128),F32)]

def attn_fwd_body(base_ref,fq_ref,fk_ref,o_ref,lse_ref,q_ref,k_ref,v_ref,bias_ref,hq,hk,dq,dk):
    attn_setup(base_ref,fq_ref,fk_ref,bias_ref,hq,hk,dq,dk,True)
    def compose(h,d,side,pair):
        first,rank,head=side
        total=None
        for r in range(rank):
            e=one_hot(h.shape[2],head+r*HEADS,pair)
            term=(dot(h[0],e)+dot(h[1],e))*d[first+r]
            total=term if total is None else total+term
        return total.astype(BF)
    lane=lax.broadcasted_iota(jnp.int32,(1,128),1)
    head_id=lax.broadcasted_iota(jnp.int32,(1,HEADS),1)
    lse_ref[...]=jnp.zeros_like(lse_ref)
    def step(pair,_):
        cols=pl.ds(pl.multiple_of(pair*128,128),128)
        q=compose(hq,dq,SIDES[0],pair); k=compose(hk,dk,SIDES[1],pair); v=compose(hk,dk,SIDES[2],pair)
        q_ref[:,cols]=q; k_ref[:,cols]=k; v_ref[:,cols]=v
        qs=q.astype(F32)*(HD**-0.5)
        out=None
        for half in range(2):
            keep=(lane>=HD) if half else (lane<HD)
            qm=jnp.where(keep,qs,0.0).astype(BF)
            s=dot_nt(qm,k)+bias_ref[...]
            m=jnp.max(s,axis=1,keepdims=True)
            e=jnp.exp(s-m)
            l=jnp.sum(e,axis=1,keepdims=True)
            p=(e*(1.0/l)).astype(BF)
            o=dot(p,v)
            out=jnp.where(keep,o,out) if half else o
            lse_ref[...]=jnp.where(head_id==2*pair+half,m+jnp.log(l),lse_ref[...])
        o_ref[:,cols]=out.astype(BF)
        return 0
    lax.fori_loop(0,HEADS//2,step,0)

VM=pl.BlockSpec(memory_space=pltpu.VMEM)
SM=pl.BlockSpec(memory_space=pltpu.SMEM)
def shape(dims,dtype=F32): return jax.ShapeDtypeStruct(dims,dtype)
def cost(us): return pl.CostEstimate(flops=int(us*1.15e9),transcendentals=0,bytes_accessed=1<<20)
def limit(mib): return pltpu.CompilerParams(vmem_limit_bytes=mib<<20)

def attn_fwd(base,fq,fk,interpret=False):
    rows,keys=fq.shape[0],fk.shape[0]
    return pl.pallas_call(attn_fwd_body,
        out_shape=(shape((rows,D),BF),shape((rows,HEADS)),shape((rows,D),BF),shape((keys,D),BF),shape((keys,D),BF)),
        in_specs=[SM,VM,VM],out_specs=(VM,)*5,scratch_shapes=attn_scratch(rows,keys),
        compiler_params=limit(48),cost_estimate=cost(18),name="attn_fwd",interpret=interpret)(base,fq,fk)

def attn_bwd_body(base_ref,q_ref,k_ref,v_ref,do_ref,lse_ref,fq_ref,fk_ref,gq_ref,gk_ref,bias_ref,hq,hk,dq,dk,aq,ak,tq,tk):
    attn_setup(base_ref,fq_ref,fk_ref,bias_ref,hq,hk,dq,dk,False)
    for ref in (aq,ak,tq,tk): ref[...]=jnp.zeros_like(ref)
    lane=lax.broadcasted_iota(jnp.int32,(1,128),1)
    head_id=lax.broadcasted_iota(jnp.int32,(1,HEADS),1)
    def back(grad,h,d,acc,tot,side,pair):
        first,rank,head=side
        total=None
        for r in range(rank):
            e=one_hot(h.shape[2],head+r*HEADS,pair)
            acc[first+r]+=grad*(dot(h[0],e)+dot(h[1],e))
            hi,lo=split2(grad*d[first+r])
            t=dot_nt(hi,e)+dot_nt(lo,e)
            total=t if total is None else total+t
        tot[...]+=total
    def step(pair,_):
        cols=pl.ds(pl.multiple_of(pair*128,128),128)
        q=q_ref[:,cols]; k=k_ref[:,cols]; v=v_ref[:,cols]; do=do_ref[:,cols]
        qs=q.astype(F32)*(HD**-0.5); dof=do.astype(F32)
        gq=gk=gv=None
        for half in range(2):
            keep=(lane>=HD) if half else (lane<HD)
            qm=jnp.where(keep,qs,0.0).astype(BF); dom=jnp.where(keep,dof,0.0).astype(BF)
            lse=jnp.sum(jnp.where(head_id==2*pair+half,lse_ref[...],0.0),axis=1,keepdims=True)
            p=jnp.exp(dot_nt(qm,k)+bias_ref[...]-lse)
            dp=dot_nt(dom,v)
            inner=jnp.sum(p*dp,axis=1,keepdims=True)
            ds=(p*(dp-inner)).astype(BF)
            nq=dot(ds,k); nk=dot_tn(ds,qm); nv=dot_tn(p.astype(BF),dom)
            if half==0: gq,gk,gv=nq,nk,nv
            else:
                gq=jnp.where(keep,nq,gq); gk=gk+nk; gv=gv+nv
        back(gq*(HD**-0.5/RQ),hq,dq,aq,tq,SIDES[0],pair)
        back(gk*(1.0/RK),hk,dk,ak,tk,SIDES[1],pair)
        back(gv*(1.0/RK),hk,dk,ak,tk,SIDES[2],pair)
        return 0
    lax.fori_loop(0,HEADS//2,step,0)
    for acc,tot,ref in ((aq,tq,gq_ref),(ak,tk,gk_ref)):
        count=acc.shape[0]
        for r in range(0,count,2):
            even=acc[r]; odd=acc[r+1]
            ref[:,r*HD:(r+2)*HD]=jnp.concatenate([even[:,:HD]+even[:,HD:],odd[:,:HD]+odd[:,HD:]],axis=1)
        ref[:,count*HD:]=tot[...]

def attn_bwd(base,q,k,v,do,lse,fq,fk,interpret=False):
    rows,keys=q.shape[0],k.shape[0]
    return pl.pallas_call(attn_bwd_body,out_shape=(shape(fq.shape),shape(fk.shape)),
        in_specs=[SM]+[VM]*7,out_specs=(VM,)*2,
        scratch_shapes=attn_scratch(rows,keys)+[pltpu.VMEM((RQ,rows,128),F32),pltpu.VMEM((2*RK,keys,128),F32),pltpu.VMEM((rows,NQ),F32),pltpu.VMEM((keys,2*NK),F32)],
        compiler_params=limit(56),cost_estimate=cost(36),name="attn_bwd",interpret=interpret)(base,q,k,v,do,lse,fq,fk)

BK=256
def tri_cols(j): return (j*(j+1)//2)*BK

def store_sym(hi,lo,i,j,val):
    h,l=split2(val)
    hi[i*BK:(i+1)*BK,j*BK:(j+1)*BK]=h; lo[i*BK:(i+1)*BK,j*BK:(j+1)*BK]=l
    if i!=j:
        t=val.T
        h,l=split2(t)
        hi[j*BK:(j+1)*BK,i*BK:(i+1)*BK]=h; lo[j*BK:(j+1)*BK,i*BK:(i+1)*BK]=l

def mul_upper(xh,xl,yh,yl,n,emit):
    for j in range(n):
        top=(j+1)*BK; cs=slice(j*BK,(j+1)*BK)
        r=dot(xh[:top,:],yh[:,cs])+dot(xh[:top,:],yl[:,cs])+dot(xl[:top,:],yh[:,cs])
        for i in range(j+1): emit(i,j,r[i*BK:(i+1)*BK])

def ns_body(g_ref,y_ref,o_ref,a_up,ah,al,ph,pw,bh,bl):
    n=o_ref.shape[1]//BK
    eye=(lax.broadcasted_iota(jnp.int32,(BK,BK),0)==lax.broadcasted_iota(jnp.int32,(BK,BK),1)).astype(F32)
    blk=lambda i,j:(slice(i*BK,(i+1)*BK),slice(j*BK,(j+1)*BK))
    trace=None
    for j in range(n):
        off=tri_cols(j)+j*BK
        part=g_ref[:,off:off+BK]*eye
        trace=part if trace is None else trace+part
    trace=jnp.sum(jnp.sum(trace,axis=1,keepdims=True),axis=0,keepdims=True)
    scale=1.0/(jnp.sqrt(trace)+1e-7)
    for j in range(n):
        for i in range(j+1):
            off=tri_cols(j)+i*BK
            val=g_ref[:,off:off+BK]*(scale*scale)
            a_up[blk(i,j)]=val; store_sym(ah,al,i,j,val)
    o_ref[...]=y_ref[...]*scale
    def poly():
        def emit(i,j,c):
            store_sym(ph,pw,i,j,COEF_B*a_up[blk(i,j)]+COEF_C*c)
        mul_upper(ah,al,ah,al,n,emit)
    def apply():
        y=o_ref[...]; yh,yl=split2(y)
        o_ref[...]=COEF_A*y+(dot(yh,ph[...])+dot(yh,pw[...])+dot(yl,ph[...]))
    def step(k,c):
        poly()
        apply()
        def emit_b(i,j,m):
            val=COEF_A*a_up[blk(i,j)]+m
            a_up[blk(i,j)]=val; store_sym(bh,bl,i,j,val)
        mul_upper(ah,al,ph,pw,n,emit_b)
        def emit_a(i,j,m):
            val=COEF_A*a_up[blk(i,j)]+m
            a_up[blk(i,j)]=val; store_sym(ah,al,i,j,val)
        mul_upper(bh,bl,ph,pw,n,emit_a)
        return c
    lax.fori_loop(0,NS_STEPS-1,step,0)
    poly(); apply()

def ns_big(gram,y,interpret=False):
    w,d=y.shape
    vm=pl.BlockSpec(memory_space=pltpu.VMEM)
    return pl.pallas_call(ns_body,out_shape=jax.ShapeDtypeStruct((w,d),F32),
        in_specs=[vm,vm],out_specs=vm,
        scratch_shapes=[pltpu.VMEM((d,d),F32)]+[pltpu.VMEM((d,d),BF)]*6,
        compiler_params=pltpu.CompilerParams(vmem_limit_bytes=56<<20),cost_estimate=cost(86),name="ns_gram",interpret=interpret)(gram,y)

def gram_body(y_ref,g_ref):
    n=y_ref.shape[1]//BK
    yh,yl=split2(y_ref[...])
    for j in range(n):
        top=(j+1)*BK; cs=slice(j*BK,top)
        r=dot_tn(yh[:,:top],yh[:,cs])+dot_tn(yh[:,:top],yl[:,cs])+dot_tn(yl[:,:top],yh[:,cs])
        for i in range(j+1):
            off=tri_cols(j)+i*BK
            g_ref[:,off:off+BK]=r[i*BK:(i+1)*BK]

def gram_upper(y,interpret=False):
    d=y.shape[1]; n=d//BK
    vm=pl.BlockSpec(memory_space=pltpu.VMEM)
    return pl.pallas_call(gram_body,out_shape=jax.ShapeDtypeStruct((BK,n*(n+1)//2*BK),F32),in_specs=[vm],out_specs=vm,
        compiler_params=pltpu.CompilerParams(vmem_limit_bytes=48<<20),cost_estimate=cost(3),name="gram_upper",interpret=interpret)(y)


def mm3(x,y,f=dot):
    xh,xl=split2(x); yh,yl=split2(y)
    return f(xh,yh)+f(xh,yl)+f(xl,yh)

def seg_mask(n,widths):
    def ids(axis):
        pos=lax.broadcasted_iota(jnp.int32,(n,n),axis); out=jnp.zeros_like(pos); edge=0
        for w in widths:
            edge+=w; out=out+(pos>=edge).astype(jnp.int32)
        return out
    return (ids(0)==ids(1)).astype(F32)

GROUPS=((0,(NQ,NK,NK)),(NQ+2*NK,(WQ,)),(NQ+2*NK+WQ,(WK,WK)))

def ns_factor_body(all_ref,own_ref,out_ref):
    out_ref[sum(GROUPS[-1][1])+GROUPS[-1][0]:,:]=jnp.zeros((out_ref.shape[0]-sum(GROUPS[-1][1])-GROUPS[-1][0],out_ref.shape[1]),F32)
    for start,widths in GROUPS:
        n=sum(widths); rs=slice(start,start+n)
        mask=seg_mask(n,widths)
        eye=(lax.broadcasted_iota(jnp.int32,(n,n),0)==lax.broadcasted_iota(jnp.int32,(n,n),1)).astype(F32)
        a=mask*sum(mm3(all_ref[d,rs,:],all_ref[d,rs,:],dot_nt) for d in range(all_ref.shape[0]))
        diag=a*eye
        row=jnp.sum(mask*jnp.sum(diag,axis=1,keepdims=True),axis=0,keepdims=True)
        col=jnp.sum(mask*jnp.sum(diag,axis=0,keepdims=True),axis=1,keepdims=True)
        row=1.0/(jnp.sqrt(row)+1e-7); col=1.0/(jnp.sqrt(col)+1e-7)
        a=a*row*col; x=own_ref[rs,:]*col
        def step(_,c):
            a,x=c
            p=COEF_B*a+COEF_C*mm3(a,a)
            x=COEF_A*x+mm3(p,x)
            b=COEF_A*a+mm3(a,p)
            return COEF_A*b+mm3(b,p),x
        a,x=lax.fori_loop(0,NS_STEPS-1,step,(a,x))
        out_ref[rs,:]=COEF_A*x+mm3(COEF_B*a+COEF_C*mm3(a,a),x)

def ns_factor(tiles,own,interpret=False):
    return pl.pallas_call(ns_factor_body,out_shape=shape(own.shape),in_specs=[VM]*2,out_specs=VM,
        compiler_params=limit(48),cost_estimate=cost(22),name="ns_factor",interpret=interpret)(tiles,own)

def ffn_chunk_body(ids_ref,x_ref,g_ref,w_ref,hin,gin,uin,keep_ref,away_ref,hid_ref,dg_ref,du_ref):
    del ids_ref,hin,gin,uin
    x=x_ref[...]
    gate=dot_nt(x,w_ref[0]); up=dot_nt(x,w_ref[1]); dh=dot_nt(g_ref[...],w_ref[2])
    sig=1.0/(1.0+jnp.exp(-gate))
    act=gate*sig
    hid_ref[...]=(act*up).astype(BF)
    dg=(dh*up*sig*(1.0+gate*(1.0-sig))).astype(BF)
    du=(dh*act).astype(BF)
    dg_ref[...]=dg; du_ref[...]=du
    total=dot(dg,w_ref[0])+dot(du,w_ref[1])
    @pl.when(pl.program_id(0)==0)
    def _(): keep_ref[...]=total
    @pl.when(pl.program_id(0)==1)
    def _(): away_ref[...]=total.astype(BF)

def ffn_chunk(ids,x_all,g_all,w,saved,rows,interpret=False):
    hid=w.shape[1]
    block=pl.BlockSpec((rows,D),lambda i,ids:(ids[i],0))
    part=pl.BlockSpec((rows,hid),lambda i,ids:(ids[i],0))
    whole=pl.BlockSpec((rows,D),lambda i,ids:(0,0))
    stay=pl.BlockSpec(memory_space=pl.ANY)
    return pl.pallas_call(ffn_chunk_body,
        out_shape=(shape((rows,D)),shape((rows,D),BF))+tuple(shape(v.shape,BF) for v in saved),
        grid_spec=pltpu.PrefetchScalarGridSpec(num_scalar_prefetch=1,grid=(2,),
            in_specs=[block,block,pl.BlockSpec(w.shape,lambda i,ids:(0,0,0)),stay,stay,stay],
            out_specs=(whole,whole,part,part,part)),
        input_output_aliases={4:2,5:3,6:4},
        compiler_params=limit(40),cost_estimate=cost(6),name="ffn_chunk",interpret=interpret)(ids,x_all,g_all,w,*saved)


EPS = 1e-06
MOMENTUM = 0.5
LEARN = 0.2
LEARN_VEC = 0.002
P = jax.sharding.PartitionSpec
FFN = 3


def normalize(values):
    row_scale = lax.rsqrt(jnp.mean(values * values, axis=-1, keepdims=True) + EPS)
    return values * row_scale, row_scale


def norm_back(grad_in, normed, row_scale, gain):
    scaled = grad_in * gain
    inner_sum = jnp.mean(scaled * normed, axis=-1, keepdims=True)
    return row_scale * (scaled - normed * inner_sum), jnp.sum(grad_in * normed, axis=0)


def dp_pairs(shift, keep=lambda target: True):
    return [(j, j ^ shift) for j in range(lax.axis_size("dp")) if keep(j ^ shift)]


def place(parts, axis, me=None):
    me = lax.axis_index("dp") if me is None else me
    step = parts[0].shape[axis]
    shape = list(parts[0].shape)
    shape[axis] *= len(parts)
    out = jnp.zeros(shape, parts[0].dtype)
    for shift, part in enumerate(parts):
        out = lax.dynamic_update_slice_in_dim(out, part, (me ^ shift) * step, axis)
    return out


def gather_dp(own, axis=0):
    return place([own] + [lax.ppermute(own, "dp", dp_pairs(s)) for s in range(1, lax.axis_size("dp"))], axis)


def sum_dp(block_for, during=None, alongside=None, gate=None):
    me = lax.axis_index("dp")
    sent = [block_for(me ^ s).astype(BF) for s in range(1, lax.axis_size("dp"))]
    if gate is not None:
        sent = [after(block, gate) for block in sent]
    total = block_for(me)
    aside = None
    if during is not None:
        aside = during(*sent)
        total = after(total, *aside, alongside)
    for s, block in enumerate(sent, 1):
        total = total + lax.ppermute(block, "dp", dp_pairs(s)).astype(F32)
    return total if during is None else (total, aside)


def after(value, *others):
    return lax.optimization_barrier((value, *others))[0]


def pass_core(x):
    return lax.ppermute(x, "mp", [(j, j ^ 1) for j in range(lax.axis_size("mp"))])


def pass_chip(x, shift):
    return lax.ppermute(x, "mp", [(j, j ^ (2 * shift)) for j in range(lax.axis_size("mp"))])


def pick(x, index):
    return lax.dynamic_index_in_dim(x, index, 0, keepdims=False)


CHIPS = 4


def collect(near):
    total = near[0]
    for s in (2, 3, 1):
        total = total + pass_chip(near[s].astype(BF), s).astype(F32)
    return total


def scatter_mp(partial):
    mp = lax.axis_size("mp")
    if mp != 2 * CHIPS:
        return (lax.psum_scatter(partial, "mp", scatter_dimension=0, tiled=True),) * 2
    me = lax.axis_index("mp")
    blocks = partial.reshape(CHIPS, 2, partial.shape[0] // mp, partial.shape[1])
    away = lax.dynamic_index_in_dim(blocks, 1 - me % 2, 1, keepdims=False).astype(BF)
    near = lax.dynamic_index_in_dim(blocks, me % 2, 1, keepdims=False) + pass_core(away).astype(F32)
    near = [pick(near, (me // 2) ^ s) for s in range(CHIPS)]
    return collect(near), near[0]


def ffn_pieces(second_own, d_output_all, low, early):
    second_in = lax.all_gather(second_own, "mp", axis=0, tiled=True)
    if lax.axis_size("mp") != 2 * CHIPS:
        gate_value, upward, d_hidden = dot_nt(second_in, low[0]), dot_nt(second_in, low[1]), dot_nt(d_output_all, low[2])
        sigmoid_gate = jax.nn.sigmoid(gate_value)
        active = gate_value * sigmoid_gate
        hidden = (active * upward).astype(BF)
        d_gate = (d_hidden * upward * sigmoid_gate * (1.0 + gate_value * (1.0 - sigmoid_gate))).astype(BF)
        d_upward = (d_hidden * active).astype(BF)
        d_second, _ = scatter_mp(dot(d_gate, low[0]) + dot(d_upward, low[1]))
        return d_second, *ffn_products(hidden, d_gate, d_upward, second_in, d_output_all, low)
    me = lax.axis_index("mp").astype(jnp.int32)
    rows = second_own.shape[0]
    saved = tuple(jnp.zeros((second_in.shape[0], low.shape[1]), BF) for _ in range(3))
    near = [None] * CHIPS
    order = (2, 3, 1, 0)
    for turn, s in enumerate(order):
        ids = jnp.stack([me ^ (2 * s), me ^ (2 * s + 1)])
        ids = after(ids, near[order[turn - 2]] if turn > 1 else early)
        keep, away, *saved = ffn_chunk(ids, second_in, d_output_all, low, saved, rows)
        near[s] = keep + pass_core(away).astype(F32)
        near[s] = near[s].astype(BF) if s else near[s]
    grads, branch = ffn_products(*saved, second_in, d_output_all, low)
    near[0] = after(near[0], grads, branch)
    return collect(near), grads, branch


def ffn_products(hidden, d_gate, d_upward, second_in, d_output_all, low):
    grads = [dot_tn(d_gate, second_in), dot_tn(d_upward, second_in), dot_tn(hidden, d_output_all)]
    spare = jnp.zeros((low.shape[1] * (lax.axis_size("dp") - FFN), D), BF)
    return jnp.concatenate([g.astype(BF) for g in grads] + [spare]), dot(hidden, low[2]).astype(BF)


def body(
    tokens,
    cotangent,
    domain_ids,
    domain_weight,
    gains,
    gain_mom,
    factor_w,
    factor_mom,
    out_w,
    out_mom,
    gate_up_w,
    gate_up_mom,
    down_w,
    down_mom,
):
    n_dp, n_mp = lax.axis_size("dp"), lax.axis_size("mp")
    me, mz = lax.axis_index("dp"), lax.axis_index("mp")
    rows = tokens.shape[0]
    d_own = factor_w.shape[0]
    hidden_own = gate_up_w.shape[2]
    out_own = d_own // n_mp
    base = me.astype(jnp.int32).reshape(1)
    shifts = range(1, n_dp)

    edge = NQ + 2 * NK

    def q_rows(m):
        return jnp.concatenate([m[edge : edge + WQ], m[:NQ]])

    def kv_rows(m):
        return jnp.concatenate([m[edge + WQ :], m[NQ:edge]])

    factor_own = factor_w.T.astype(BF)
    kv_low = gather_dp(kv_rows(factor_own), 1)
    x_float = tokens.astype(F32)
    first_normed, first_scale = normalize(x_float)
    first_own = (first_normed * gains[0]).astype(BF)
    domain_range = jnp.arange(domain_weight.shape[0], dtype=jnp.int32)
    seq_weight = jnp.sum(jnp.where(domain_ids[0, 0] == domain_range, domain_weight, 0.0))
    d_output = cotangent.astype(F32) * seq_weight
    d_output_all = lax.all_gather(d_output.astype(BF), "mp", axis=0, tiled=True)
    kv_all = gather_dp(dot_nt(first_own, kv_low))
    q_low = gather_dp(after(q_rows(factor_own), kv_low), 1)
    q_own = dot_nt(first_own, q_low)
    attended, lse, queries, key_vecs, values = attn_fwd(base, q_own, kv_all)
    out_low = gather_dp(after(out_w.astype(BF), kv_all))
    residual = x_float + dot(attended, out_low)
    second_normed, second_scale = normalize(residual)

    ffn_own = jnp.stack([gate_up_w[0].T, gate_up_w[1].T, down_w])
    ffn_low = gather_dp(after(ffn_own.astype(BF), out_low), 2)
    second_own = (second_normed * gains[1]).astype(BF)
    to_ffn = lambda target: target < FFN
    ffn_slot = jnp.minimum(me, FFN - 1)
    ffn_mom = after(jnp.stack([gate_up_mom[0].T, gate_up_mom[1].T, down_mom]), ffn_low)
    own_mom = [pick(ffn_mom, ffn_slot)]
    for s in shifts:
        own_mom.append(lax.ppermute(pick(ffn_mom, jnp.minimum(me ^ s, FFN - 1)), "dp", dp_pairs(s, to_ffn)))
    own_mom = MOMENTUM * place(own_mom, 1)
    d_second, grads, branch = ffn_pieces(second_own, d_output_all, ffn_low, own_mom)
    matrix = lax.psum_scatter(grads, "dp", scatter_dimension=0, tiled=True)

    d_resid_norm, gain_second = norm_back(d_second, second_normed, second_scale, gains[1])
    d_residual = d_output + d_resid_norm
    d_residual_low = d_residual.astype(BF)
    out_block = lambda t: dot_tn(lax.dynamic_slice_in_dim(attended, t * d_own, d_own, 1), d_residual_low)
    d_attended = dot_nt(d_residual_low, out_low).astype(BF)
    backward = lambda *sent: attn_bwd(after(base, *sent), queries, key_vecs, values, d_attended, lse, q_own, kv_all)
    grad_out, (d_q, d_kv) = sum_dp(out_block, during=backward, alongside=matrix)
    grad_out, grad_out_chip = scatter_mp(grad_out)
    out_tile = MOMENTUM * lax.dynamic_slice_in_dim(out_mom, mz * out_own, out_own, 0) + grad_out
    out_rows = place([out_tile] + [lax.ppermute(out_tile, "dp", [(j ^ s, j) for j in range(FFN, n_dp)]) for s in shifts], 0)
    out_rows = jnp.pad(out_rows, ((0, hidden_own - out_rows.shape[0]), (0, 0)))
    matrix = jnp.where(me < FFN, own_mom + matrix.astype(F32), out_rows)
    gram_part = gram_upper(matrix)
    gram = lax.psum(gram_part, "mp")

    d_kv = after(d_kv, grad_out_chip)
    d_kv = sum_dp(lambda t: lax.dynamic_slice_in_dim(d_kv, t * rows, rows, 0))
    d_q, d_kv = d_q.astype(BF), d_kv.astype(BF)
    d_first = dot(d_q, q_low) + dot(d_kv, kv_low)
    d_input_norm, gain_first = norm_back(d_first, first_normed, first_scale, gains[0])
    input_grad = d_residual + d_input_norm

    gain_rows = jnp.stack([gain_first, gain_second])
    filler = -(factor_w.shape[1] + 2) % (8 * n_mp)

    def factor_block(t):
        cols = lax.dynamic_slice_in_dim(first_own, t * d_own, d_own, 1)
        q, kv = dot_tn(d_q, cols), dot_tn(d_kv, cols)
        tail = jnp.pad(lax.dynamic_slice_in_dim(gain_rows, t * d_own, d_own, 1), ((0, filler), (0, 0)))
        return jnp.concatenate([q[WQ:], kv[2 * WK :], q[:WQ], kv[: 2 * WK], tail])

    d_q, d_kv = after((d_q, d_kv), grad_out)
    grad_factor = sum_dp(factor_block, gate=gram_part)
    grad_factor, _ = scatter_mp(grad_factor)
    height = grad_factor.shape[0]
    factor_piece = jnp.pad(MOMENTUM * factor_mom.T, ((0, filler + 2), (0, 0)))
    factor_piece = lax.dynamic_slice_in_dim(factor_piece, mz * height, height, 0) + grad_factor
    factor_all = lax.all_gather(factor_piece, ("dp", "mp"), axis=0, tiled=True).reshape(n_dp, n_mp * height, d_own)
    factor_tile = pick(factor_all, me)
    gain_grad = factor_tile[factor_w.shape[1] : factor_w.shape[1] + 2]
    branch = lax.psum_scatter(after(branch, factor_piece), "mp", scatter_dimension=0, tiled=True)
    block_out = (residual + branch.astype(F32)).astype(BF)

    def give_back(whole):
        pieces = [lax.dynamic_slice_in_dim(whole, (me ^ s) * d_own, d_own, 1) for s in range(n_dp)]
        came = [lax.ppermute(pieces[s], "dp", dp_pairs(s, lambda t: t ^ s < FFN))[None] for s in shifts]
        return place([pieces[0][None]] + came, 0), pieces[1:]

    ortho = ns_big(gram, after(matrix, factor_piece))
    out_ortho = lax.dynamic_slice_in_dim(ortho, me * out_own, out_own, 0)
    for s in shifts:
        piece = lax.dynamic_slice_in_dim(ortho, (me ^ s) * out_own, out_own, 0)
        piece = lax.ppermute(piece, "dp", [(j, j ^ s) for j in range(FFN, n_dp)])
        out_ortho = jnp.where(me ^ s == FFN, piece, out_ortho)
    out_both = after(jnp.stack([out_tile, out_ortho]), factor_all, branch)
    out_both = lax.all_gather(out_both, "mp", axis=1, tiled=True)
    new_out_mom = out_both[0]
    new_out_w = out_w - LEARN * 0.2 * math.sqrt(D) * out_both[1]
    mom_back, _ = give_back(after(matrix, ortho))
    ortho_back, sent = give_back(ortho)
    turn = lambda stack: jnp.stack([stack[0].T, stack[1].T])
    ffn_rate = LEARN * 0.2 * math.sqrt(max(D, hidden_own * n_mp))
    new_gate_up_mom, new_down_mom = turn(mom_back), mom_back[2]
    new_gate_up_w = gate_up_w - ffn_rate * turn(ortho_back)
    new_down_w = down_w - ffn_rate * ortho_back[2]

    factor_ortho = ns_factor(factor_all, after(factor_tile, *sent))
    widths = [NQ, NK, NK, WQ, WK, WK]
    factor_rate = jnp.concatenate([jnp.full((w, 1), LEARN * 0.2 * math.sqrt(max(D, w)), F32) for w in widths])
    new_factor_mom = factor_tile[: factor_w.shape[1]].T
    new_factor_w = factor_w - (factor_rate * factor_ortho[: factor_w.shape[1]]).T

    new_gain_mom = MOMENTUM * gain_mom + gain_grad
    new_gains = lax.dynamic_slice_in_dim(gains, me * d_own, d_own, 1) - LEARN_VEC * new_gain_mom
    return (
        block_out,
        input_grad,
        gain_grad,
        new_gains,
        new_gain_mom,
        new_factor_mom,
        new_factor_w,
        new_out_mom,
        new_out_w,
        new_gate_up_mom,
        new_gate_up_w,
        new_down_mom,
        new_down_w,
    )


def solution(mesh):
    token = P(("mp", "dp"), None)
    row = P("dp", None)
    ffn = P(None, "dp", "mp")
    down = P("mp", "dp")
    vec = P(None, "dp")
    return jax.shard_map(
        body,
        mesh=mesh,
        in_specs=(token, token, P("mp", None), P(), P(), vec, row, row, row, row, ffn, ffn, down, down),
        out_specs=(token, token, vec, vec, vec, row, row, row, row, ffn, ffn, down, down),
        check_vma=False,
    )
```

```python
import functools
import math
import jax
import jax.numpy as jnp
from jax import lax
from jax.experimental import pallas as pl
from jax.experimental.pallas import tpu as pltpu
BF=jnp.bfloat16; F32=jnp.float32
HEADS=16; HD=64; RQ=6; RK=2; D=1024
COEF_A=3.4445; COEF_B=-4.775; COEF_C=2.0315
NEG=-1e30
NS_STEPS=5

def split2(x):
    hi=x.astype(BF); return hi,(x-hi.astype(F32)).astype(BF)
def dot(a,b): return jnp.dot(a,b,preferred_element_type=F32)
def dot_nt(a,b): return lax.dot_general(a,b,(((1,),(1,)),((),())),preferred_element_type=F32)
def dot_tn(a,b): return lax.dot_general(a,b,(((0,),(0,)),((),())),preferred_element_type=F32)

def index_map(ref, heads):
    row=lax.broadcasted_iota(jnp.int32,ref.shape,0); col=lax.broadcasted_iota(jnp.int32,ref.shape,1)
    row=jnp.where(row>=heads,row-heads,row)
    ref[...]=row-HEADS*lax.shift_right_logical(col,7)-(lax.bitwise_and(col,127)>=HD).astype(jnp.int32)

def one_hot(ref, pair): return jnp.where(ref[...]==2*pair,1.0,0.0).astype(BF)

def twice(dims,r,scale):
    part=dims[:,r*HD:(r+1)*HD]*scale
    return jnp.concatenate([part,part],axis=1)

WQ,WK=RQ*HD,RK*HD
NQ,NK=RQ*HEADS,RK*HEADS

def attn_setup(base_ref,fq_ref,fk_ref,bias_ref,hq,hk,dq,dk,iq,ik,scaled):
    rows,keys=bias_ref.shape
    r_id=lax.broadcasted_iota(jnp.int32,(rows,keys),0)+base_ref[0]*rows
    c_id=lax.broadcasted_iota(jnp.int32,(rows,keys),1)
    bias_ref[...]=jnp.where(c_id<=r_id,0.0,NEG)
    hq[...]=jnp.concatenate(split2(fq_ref[:,WQ:]),axis=1); hk[...]=jnp.concatenate(split2(fk_ref[:,2*WK:]),axis=1)
    for r in range(RQ): dq[r]=twice(fq_ref,r,1.0/RQ if scaled else 1.0)
    for r in range(2*RK): dk[r]=twice(fk_ref,r,1.0/RK if scaled else 1.0)
    index_map(iq,NQ); index_map(ik,2*NK)

def attn_scratch(rows,keys):
    return [pltpu.VMEM((rows,keys),F32),pltpu.VMEM((rows,2*NQ),BF),pltpu.VMEM((keys,4*NK),BF),pltpu.VMEM((RQ,rows,128),F32),pltpu.VMEM((2*RK,keys,128),F32),
        pltpu.VMEM((2*NQ,RQ*128),jnp.int32),pltpu.VMEM((4*NK,2*RK*128),jnp.int32)]

def lanes(x,r): return x[:,r*128:(r+1)*128]

def attn_fwd_body(base_ref,fq_ref,fk_ref,o_ref,lse_ref,q_ref,k_ref,v_ref,bias_ref,hq,hk,dq,dk,iq,ik):
    attn_setup(base_ref,fq_ref,fk_ref,bias_ref,hq,hk,dq,dk,iq,ik,True)
    lane=lax.broadcasted_iota(jnp.int32,(1,128),1)
    head_id=lax.broadcasted_iota(jnp.int32,(1,HEADS),1)
    lse_ref[...]=jnp.zeros_like(lse_ref)
    def step(pair,_):
        cols=pl.ds(pl.multiple_of(pair*128,128),128)
        wide_q=dot(hq[...],one_hot(iq,pair)); wide_k=dot(hk[...],one_hot(ik,pair))
        q=sum(lanes(wide_q,r)*dq[r] for r in range(RQ)).astype(BF)
        k=sum(lanes(wide_k,r)*dk[r] for r in range(RK)).astype(BF)
        v=sum(lanes(wide_k,r)*dk[r] for r in range(RK,2*RK)).astype(BF)
        q_ref[:,cols]=q; k_ref[:,cols]=k; v_ref[:,cols]=v
        qs=q.astype(F32)*(HD**-0.5)
        out=None
        for half in range(2):
            keep=(lane>=HD) if half else (lane<HD)
            qm=jnp.where(keep,qs,0.0).astype(BF)
            s=dot_nt(qm,k)+bias_ref[...]
            m=jnp.max(s,axis=1,keepdims=True)
            e=jnp.exp(s-m)
            l=jnp.sum(e,axis=1,keepdims=True)
            p=(e*(1.0/l)).astype(BF)
            o=dot(p,v)
            out=jnp.where(keep,o,out) if half else o
            lse_ref[...]=jnp.where(head_id==2*pair+half,m+jnp.log(l),lse_ref[...])
        o_ref[:,cols]=out.astype(BF)
        return 0
    lax.fori_loop(0,HEADS//2,step,0)

VM=pl.BlockSpec(memory_space=pltpu.VMEM)
SM=pl.BlockSpec(memory_space=pltpu.SMEM)
def shape(dims,dtype=F32): return jax.ShapeDtypeStruct(dims,dtype)
def cost(us): return pl.CostEstimate(flops=int(us*1.15e9),transcendentals=0,bytes_accessed=1<<20)
def limit(mib): return pltpu.CompilerParams(vmem_limit_bytes=mib<<20)

def attn_fwd(base,fq,fk,interpret=False):
    rows,keys=fq.shape[0],fk.shape[0]
    return pl.pallas_call(attn_fwd_body,
        out_shape=(shape((rows,D),BF),shape((rows,HEADS)),shape((rows,D),BF),shape((keys,D),BF),shape((keys,D),BF)),
        in_specs=[SM,VM,VM],out_specs=(VM,)*5,scratch_shapes=attn_scratch(rows,keys),
        compiler_params=limit(28),cost_estimate=cost(16),name="attn_fwd",interpret=interpret)(base,fq,fk)

def attn_bwd_body(first,last,base_ref,q_ref,k_ref,v_ref,do_ref,lse_ref,fq_ref,fk_ref,gq_ref,gk_ref,bias_ref,hq,hk,dq,dk,iq,ik,aq,ak,tq,tk):
    attn_setup(base_ref,fq_ref,fk_ref,bias_ref,hq,hk,dq,dk,iq,ik,False)
    for ref in (aq,ak,tq,tk): ref[...]=jnp.zeros_like(ref)
    lane=lax.broadcasted_iota(jnp.int32,(1,128),1)
    head_id=lax.broadcasted_iota(jnp.int32,(1,HEADS),1)
    def back(grads,h,d,index,acc,tot,pair):
        e=one_hot(index,pair)
        wide=dot(h[...],e)
        for r,grad in enumerate(grads): acc[r]+=grad*lanes(wide,r)
        terms=jnp.concatenate([(grad*d[r]).astype(BF) for r,grad in enumerate(grads)],axis=1)
        tot[...]+=dot_nt(terms,e[:tot.shape[1]])
    def step(pair,_):
        cols=pl.ds(pl.multiple_of(pair*128,128),128)
        q=q_ref[:,cols]; k=k_ref[:,cols]; v=v_ref[:,cols]; do=do_ref[:,cols]
        qs=q.astype(F32)*(HD**-0.5); dof=do.astype(F32)
        gq=gk=gv=None
        for half in range(2):
            keep=(lane>=HD) if half else (lane<HD)
            qm=jnp.where(keep,qs,0.0).astype(BF); dom=jnp.where(keep,dof,0.0).astype(BF)
            lse=jnp.sum(jnp.where(head_id==2*pair+half,lse_ref[...],0.0),axis=1,keepdims=True)
            p=jnp.exp(dot_nt(qm,k)+bias_ref[...]-lse)
            dp=dot_nt(dom,v)
            inner=jnp.sum(p*dp,axis=1,keepdims=True)
            ds=(p*(dp-inner)).astype(BF)
            nq=dot(ds,k); nk=dot_tn(ds,qm); nv=dot_tn(p.astype(BF),dom)
            if half==0: gq,gk,gv=nq,nk,nv
            else:
                gq=jnp.where(keep,nq,gq); gk=gk+nk; gv=gv+nv
        gq=gq*(HD**-0.5/RQ); gk=gk*(1.0/RK); gv=gv*(1.0/RK)
        back([gq]*RQ,hq,dq,iq,aq,tq,pair)
        back([gk]*RK+[gv]*RK,hk,dk,ik,ak,tk,pair)
        return 0
    lax.fori_loop(first,last,step,0)
    for acc,tot,ref in ((aq,tq,gq_ref),(ak,tk,gk_ref)):
        count=acc.shape[0]
        for r in range(0,count,2):
            even=acc[r]; odd=acc[r+1]
            ref[:,r*HD:(r+2)*HD]=jnp.concatenate([even[:,:HD]+even[:,HD:],odd[:,:HD]+odd[:,HD:]],axis=1)
        ref[:,count*HD:]=tot[...]

def attn_bwd(pairs,base,q,k,v,do,lse,fq,fk,us,interpret=False):
    rows,keys=q.shape[0],k.shape[0]
    return pl.pallas_call(functools.partial(attn_bwd_body,*pairs),out_shape=(shape(fq.shape),shape(fk.shape)),
        in_specs=[SM]+[VM]*7,out_specs=(VM,)*2,
        scratch_shapes=attn_scratch(rows,keys)+[pltpu.VMEM((RQ,rows,128),F32),pltpu.VMEM((2*RK,keys,128),F32),pltpu.VMEM((rows,NQ),F32),pltpu.VMEM((keys,2*NK),F32)],
        compiler_params=limit(36),cost_estimate=cost(us),name="attn_bwd",interpret=interpret)(base,q,k,v,do,lse,fq,fk)

BK=256
def tri_cols(j): return (j*(j+1)//2)*BK

def store_sym(hi,lo,i,j,val):
    h,l=split2(val)
    hi[i*BK:(i+1)*BK,j*BK:(j+1)*BK]=h; lo[i*BK:(i+1)*BK,j*BK:(j+1)*BK]=l
    if i!=j:
        t=val.T
        h,l=split2(t)
        hi[j*BK:(j+1)*BK,i*BK:(i+1)*BK]=h; lo[j*BK:(j+1)*BK,i*BK:(i+1)*BK]=l

def mul_upper(xh,xl,yh,yl,n,emit):
    for j in reversed(range(n)):
        top=(j+1)*BK; cs=slice(j*BK,(j+1)*BK)
        r=dot(xh[:top,:],yh[:,cs])+dot(xh[:top,:],yl[:,cs])+dot(xl[:top,:],yh[:,cs])
        for i in range(j+1): emit(i,j,r[i*BK:(i+1)*BK])

def ns_body(g_ref,y_ref,o_ref,a_up,ah,al,ph,pw,bh,bl):
    n=o_ref.shape[1]//BK
    eye=(lax.broadcasted_iota(jnp.int32,(BK,BK),0)==lax.broadcasted_iota(jnp.int32,(BK,BK),1)).astype(F32)
    blk=lambda i,j:(slice(i*BK,(i+1)*BK),slice(j*BK,(j+1)*BK))
    trace=None
    for j in range(n):
        off=tri_cols(j)+j*BK
        part=g_ref[:,off:off+BK]*eye
        trace=part if trace is None else trace+part
    trace=jnp.sum(jnp.sum(trace,axis=1,keepdims=True),axis=0,keepdims=True)
    scale=1.0/(jnp.sqrt(trace)+1e-7)
    for j in range(n):
        for i in range(j+1):
            off=tri_cols(j)+i*BK
            val=g_ref[:,off:off+BK]*(scale*scale)
            a_up[blk(i,j)]=val; store_sym(ah,al,i,j,val)
    o_ref[...]=y_ref[...]*scale
    def poly():
        def emit(i,j,c):
            store_sym(ph,pw,i,j,COEF_B*a_up[blk(i,j)]+COEF_C*c)
        mul_upper(ah,al,ah,al,n,emit)
    def apply():
        y=o_ref[...]; yh,yl=split2(y)
        o_ref[...]=COEF_A*y+(dot(yh,ph[...])+dot(yh,pw[...])+dot(yl,ph[...]))
    def step(k,c):
        poly()
        def emit_b(i,j,m):
            val=COEF_A*a_up[blk(i,j)]+m
            a_up[blk(i,j)]=val; store_sym(bh,bl,i,j,val)
        mul_upper(ah,al,ph,pw,n,emit_b)
        apply()
        def emit_a(i,j,m):
            val=COEF_A*a_up[blk(i,j)]+m
            a_up[blk(i,j)]=val; store_sym(ah,al,i,j,val)
        mul_upper(bh,bl,ph,pw,n,emit_a)
        return c
    lax.fori_loop(0,NS_STEPS-1,step,0)
    poly(); apply()

def ns_big(gram,y,interpret=False):
    w,d=y.shape
    vm=pl.BlockSpec(memory_space=pltpu.VMEM)
    return pl.pallas_call(ns_body,out_shape=jax.ShapeDtypeStruct((w,d),F32),
        in_specs=[vm,vm],out_specs=vm,
        scratch_shapes=[pltpu.VMEM((d,d),F32)]+[pltpu.VMEM((d,d),BF)]*6,
        compiler_params=pltpu.CompilerParams(vmem_limit_bytes=40<<20),cost_estimate=cost(71),name="ns_gram",interpret=interpret)(gram,y)

def gram_body(y_ref,g_ref):
    n=y_ref.shape[1]//BK
    yh,yl=split2(y_ref[...])
    for j in range(n):
        top=(j+1)*BK; cs=slice(j*BK,top)
        r=dot_tn(yh[:,:top],yh[:,cs])+dot_tn(yh[:,:top],yl[:,cs])+dot_tn(yl[:,:top],yh[:,cs])
        for i in range(j+1):
            off=tri_cols(j)+i*BK
            g_ref[:,off:off+BK]=r[i*BK:(i+1)*BK]

def gram_upper(y,interpret=False):
    d=y.shape[1]; n=d//BK
    vm=pl.BlockSpec(memory_space=pltpu.VMEM)
    return pl.pallas_call(gram_body,out_shape=jax.ShapeDtypeStruct((BK,n*(n+1)//2*BK),F32),in_specs=[vm],out_specs=vm,
        compiler_params=pltpu.CompilerParams(vmem_limit_bytes=16<<20),cost_estimate=cost(3),name="gram_upper",interpret=interpret)(y)


def mm3(x,y,f=dot):
    xh,xl=split2(x); yh,yl=split2(y)
    return f(xh,yh)+f(xh,yl)+f(xl,yh)

def seg_mask(n,widths):
    def ids(axis):
        pos=lax.broadcasted_iota(jnp.int32,(n,n),axis); out=jnp.zeros_like(pos); edge=0
        for w in widths:
            edge+=w; out=out+(pos>=edge).astype(jnp.int32)
        return out
    return (ids(0)==ids(1)).astype(F32)

GROUPS=((0,(NQ,NK,NK)),(NQ+2*NK,(WQ,)),(NQ+2*NK+WQ,(WK,WK)))

def ns_factor_body(all_ref,own_ref,out_ref):
    out_ref[sum(GROUPS[-1][1])+GROUPS[-1][0]:,:]=jnp.zeros((out_ref.shape[0]-sum(GROUPS[-1][1])-GROUPS[-1][0],out_ref.shape[1]),F32)
    state=[]
    for start,widths in GROUPS:
        n=sum(widths); rs=slice(start,start+n)
        mask=seg_mask(n,widths)
        eye=(lax.broadcasted_iota(jnp.int32,(n,n),0)==lax.broadcasted_iota(jnp.int32,(n,n),1)).astype(F32)
        a=mask*sum(mm3(all_ref[d,rs,:],all_ref[d,rs,:],dot_nt) for d in range(all_ref.shape[0]))
        diag=a*eye
        row=jnp.sum(mask*jnp.sum(diag,axis=1,keepdims=True),axis=0,keepdims=True)
        col=jnp.sum(mask*jnp.sum(diag,axis=0,keepdims=True),axis=1,keepdims=True)
        row=1.0/(jnp.sqrt(row)+1e-7); col=1.0/(jnp.sqrt(col)+1e-7)
        state+=[a*row*col,own_ref[rs,:]*col]
    def step(_,c):
        out=[]
        for a,x in zip(c[::2],c[1::2]):
            p=COEF_B*a+COEF_C*mm3(a,a)
            x=COEF_A*x+mm3(p,x)
            b=COEF_A*a+mm3(a,p)
            out+=[COEF_A*b+mm3(b,p),x]
        return tuple(out)
    state=lax.fori_loop(0,NS_STEPS-1,step,tuple(state))
    for (start,widths),a,x in zip(GROUPS,state[::2],state[1::2]):
        out_ref[start:start+sum(widths),:]=COEF_A*x+mm3(COEF_B*a+COEF_C*mm3(a,a),x)

def ns_factor(tiles,own,interpret=False):
    return pl.pallas_call(ns_factor_body,out_shape=shape(own.shape),in_specs=[VM]*2,out_specs=VM,
        compiler_params=limit(28),cost_estimate=cost(22),name="ns_factor",interpret=interpret)(tiles,own)

def ffn_body(x_ref,g_ref,w_ref,second_ref,branch_ref,hid_ref,dg_ref,du_ref):
    x=x_ref[...]
    gate=dot_nt(x,w_ref[0]); up=dot_nt(x,w_ref[1]); dh=dot_nt(g_ref[...],w_ref[2])
    sig=1.0/(1.0+jnp.exp(-gate))
    act=gate*sig
    hid=(act*up).astype(BF)
    dg=(dh*up*sig*(1.0+gate*(1.0-sig))).astype(BF)
    du=(dh*act).astype(BF)
    hid_ref[...]=hid; dg_ref[...]=dg; du_ref[...]=du
    second_ref[...]=(dot(dg,w_ref[0])+dot(du,w_ref[1])).astype(BF)
    branch_ref[...]=dot(hid,w_ref[2]).astype(BF)

def in_hbm(x): return pltpu.with_memory_space_constraint(x,pltpu.HBM)

def ffn_tokens(x_all,g_all,w,interpret=False):
    tokens=x_all.shape[0]; rows=256; hid=w.shape[1]
    block=pl.BlockSpec((rows,D),lambda i:(i,0)); part=pl.BlockSpec((rows,hid),lambda i:(i,0))
    return pl.pallas_call(ffn_body,out_shape=(pltpu.HBM((tokens,D),BF),shape((tokens,D),BF))+(shape((tokens,hid),BF),)*3,
        grid=(tokens//rows,),in_specs=[block,block,pl.BlockSpec(w.shape,lambda i:(0,0,0),pipeline_mode=pl.Buffered(1))],
        out_specs=(block,block,part,part,part),
        compiler_params=limit(20),cost_estimate=cost(20),name="ffn_tokens",interpret=interpret)(in_hbm(x_all),in_hbm(g_all),w)

def ffn_grads_body(steps,hid_ref,dg_ref,du_ref,x_ref,g_ref,grad_ref,*total):
    width=hid_ref.shape[1]
    for c,(left,right) in enumerate(((dg_ref,x_ref),(du_ref,x_ref),(hid_ref,g_ref))):
        here=slice(c*width,(c+1)*width)
        part=dot_tn(left[...],right[...])
        if steps>1:
            part=jnp.where(pl.program_id(0)==0,part,part+total[0][c])
            total[0][c]=part
        grad_ref[here,:]=part.astype(BF)
    grad_ref[3*width:,:]=jnp.zeros((grad_ref.shape[0]-3*width,D),BF)

def ffn_grads(saved,x_all,g_all,n_dp,interpret=False):
    tokens,hid=saved[0].shape; rows=min(tokens,2048); steps=tokens//rows
    block=pl.BlockSpec((rows,D),lambda i:(i,0)); part=pl.BlockSpec((rows,hid),lambda i:(i,0))
    out=(n_dp*hid,D)
    return pl.pallas_call(functools.partial(ffn_grads_body,steps),out_shape=shape(out,BF),grid=(steps,),
        in_specs=[part]*3+[block]*2,out_specs=pl.BlockSpec(out,lambda i:(0,0)),
        scratch_shapes=[] if steps==1 else [pltpu.VMEM((3,hid,D),F32)],
        compiler_params=limit(40),cost_estimate=cost(10),name="ffn_grads",interpret=interpret)(*saved,x_all,g_all)


EPS = 1e-06
MOMENTUM = 0.5
LEARN = 0.2
LEARN_VEC = 0.002
P = jax.sharding.PartitionSpec
FFN = 3


def normalize(values):
    row_scale = lax.rsqrt(jnp.mean(values * values, axis=-1, keepdims=True) + EPS)
    return values * row_scale, row_scale


def norm_back(grad_in, normed, row_scale, gain):
    scaled = grad_in * gain
    inner_sum = jnp.mean(scaled * normed, axis=-1, keepdims=True)
    return row_scale * (scaled - normed * inner_sum), jnp.sum(grad_in * normed, axis=0)


def dp_pairs(shift, keep=lambda target: True):
    return [(j, j ^ shift) for j in range(lax.axis_size("dp")) if keep(j ^ shift)]


def place(parts, axis, me=None):
    me = lax.axis_index("dp") if me is None else me
    step = parts[0].shape[axis]
    shape = list(parts[0].shape)
    shape[axis] *= len(parts)
    out = jnp.zeros(shape, parts[0].dtype)
    for shift, part in enumerate(parts):
        out = lax.dynamic_update_slice_in_dim(out, part, (me ^ shift) * step, axis)
    return out


def gather_dp(own, axis=0):
    return place([own] + [lax.ppermute(own, "dp", dp_pairs(s)) for s in range(1, lax.axis_size("dp"))], axis)


def sum_dp(block_for, during=None, alongside=(), gate=None):
    me = lax.axis_index("dp")
    sent = [block_for(me ^ s).astype(BF) for s in range(1, lax.axis_size("dp"))]
    if gate is not None:
        sent = [after(block, gate) for block in sent]
    total = block_for(me)
    aside = None
    if during is not None:
        aside = during(*sent)
        total = after(total, *aside, *alongside)
    for s, block in enumerate(sent, 1):
        total = total + lax.ppermute(block, "dp", dp_pairs(s)).astype(F32)
    return total if during is None else (total, aside)


def after(value, *others):
    return lax.optimization_barrier((value, *others))[0]


def pass_core(x):
    return lax.ppermute(x, "mp", [(j, j ^ 1) for j in range(lax.axis_size("mp"))])


def pass_chip(x, shift):
    return lax.ppermute(x, "mp", [(j, j ^ (2 * shift)) for j in range(lax.axis_size("mp"))])


def pick(x, index):
    return lax.dynamic_index_in_dim(x, index, 0, keepdims=False)


CHIPS = 4


def cross_chips(near):
    if len(near) == 1:
        return [lax.psum_scatter(near[0], "mp", scatter_dimension=0, tiled=True)]
    return [near[0]] + [pass_chip(near[s].astype(BF), s) for s in range(1, len(near))]


def collect(near):
    return sum(part.astype(F32) for part in cross_chips(near))


def core_half(partial, axis):
    core = lax.axis_index("mp") % 2
    away = lax.dynamic_index_in_dim(partial, 1 - core, axis, keepdims=False).astype(BF)
    return lax.dynamic_index_in_dim(partial, core, axis, keepdims=False) + pass_core(away).astype(F32)


def chip_sums(partial):
    if lax.axis_size("mp") != 2 * CHIPS:
        return [partial]
    near = core_half(partial.reshape(CHIPS, 2, -1, partial.shape[1]), 1)
    near = [pick(near, (lax.axis_index("mp") // 2) ^ s) for s in range(CHIPS)]
    return [near[0]] + [part.astype(BF) for part in near[1:]]


def body(
    tokens,
    cotangent,
    domain_ids,
    domain_weight,
    gains,
    gain_mom,
    factor_w,
    factor_mom,
    out_w,
    out_mom,
    gate_up_w,
    gate_up_mom,
    down_w,
    down_mom,
):
    n_dp, n_mp = lax.axis_size("dp"), lax.axis_size("mp")
    me, mz = lax.axis_index("dp"), lax.axis_index("mp")
    rows = tokens.shape[0]
    d_own = factor_w.shape[0]
    hidden_own = gate_up_w.shape[2]
    out_own = d_own // n_mp
    base = me.astype(jnp.int32).reshape(1)
    shifts = range(1, n_dp)

    edge = NQ + 2 * NK

    def q_rows(m):
        return jnp.concatenate([m[edge : edge + WQ], m[:NQ]])

    def kv_rows(m):
        return jnp.concatenate([m[edge + WQ :], m[NQ:edge]])

    factor_own = factor_w.T.astype(BF)
    kv_low = gather_dp(kv_rows(factor_own), 1)
    x_float = tokens.astype(F32)
    first_normed, first_scale = normalize(x_float)
    first_own = (first_normed * gains[0]).astype(BF)
    domain_range = jnp.arange(domain_weight.shape[0], dtype=jnp.int32)
    seq_weight = jnp.sum(jnp.where(domain_ids[0, 0] == domain_range, domain_weight, 0.0))
    d_output = cotangent.astype(F32) * seq_weight
    d_output_all = lax.all_gather(d_output.astype(BF), "mp", axis=0, tiled=True)
    kv_all = gather_dp(dot_nt(first_own, kv_low))
    q_low = gather_dp(after(q_rows(factor_own), kv_low), 1)
    q_own = dot_nt(first_own, q_low)
    attended, lse, queries, key_vecs, values = attn_fwd(base, q_own, kv_all)
    out_low = gather_dp(after(out_w.astype(BF), kv_all))
    residual = x_float + dot(attended, out_low)
    second_normed, second_scale = normalize(residual)

    ffn_own = jnp.stack([gate_up_w[0].T, gate_up_w[1].T, down_w])
    ffn_low = gather_dp(after(ffn_own.astype(BF), out_low), 2)
    second_own = (second_normed * gains[1]).astype(BF)
    to_ffn = lambda target: target < FFN
    ffn_slot = jnp.minimum(me, FFN - 1)
    ffn_mom = after(jnp.stack([gate_up_mom[0].T, gate_up_mom[1].T, down_mom]), ffn_low)
    own_mom = [pick(ffn_mom, ffn_slot)]
    for s in shifts:
        own_mom.append(lax.ppermute(pick(ffn_mom, jnp.minimum(me ^ s, FFN - 1)), "dp", dp_pairs(s, to_ffn)))
    second_in = lax.all_gather(second_own, "mp", axis=0, tiled=True)
    d_second, branch, *saved = ffn_tokens(second_in, d_output_all, after(ffn_low, *own_mom[1:]))
    d_second = lax.psum_scatter(d_second, "mp", scatter_dimension=0, tiled=True).astype(F32)
    grads = ffn_grads(saved, second_in, d_output_all, n_dp)
    branch = chip_sums(branch)
    d_second = after(d_second, grads, *branch)
    own_mom = MOMENTUM * place(own_mom, 1)
    matrix = lax.psum_scatter(grads, "dp", scatter_dimension=0, tiled=True)

    d_resid_norm, gain_second = norm_back(d_second, second_normed, second_scale, gains[1])
    d_residual = d_output + d_resid_norm
    d_residual_low = d_residual.astype(BF)
    d_attended = dot_nt(d_residual_low, out_low).astype(BF)

    def backward(pairs, us, *gates):
        return attn_bwd(pairs, after(base, *gates), queries, key_vecs, values, d_attended, lse, q_own, kv_all, us)

    grad_out = dot_tn(attended, d_residual_low)
    if n_mp == 2 * CHIPS:
        grad_out = core_half(grad_out.reshape(n_dp, CHIPS, 2, out_own, D), 2)
    grad_out = grad_out.reshape(n_dp, -1, D)
    last, branch = branch[3:], cross_chips([after(part, d_second) for part in branch[:3]])
    grad_out, (d_q, d_kv) = sum_dp(
        lambda t: pick(grad_out, t), during=functools.partial(backward, (0, HEADS // 2), 26), alongside=(matrix, *branch[1:])
    )
    d_q, d_kv = after((d_q, d_kv), grad_out)
    if n_mp == 2 * CHIPS:
        grad_out = grad_out.reshape(CHIPS, out_own, D)
        near = [pick(grad_out, (mz // 2) ^ s) for s in range(CHIPS)]
        near = near[:1] + [part.astype(BF) for part in near[1:]]
        grad_out = collect(near)
    else:
        grad_out = lax.psum_scatter(grad_out, "mp", scatter_dimension=0, tiled=True)
    out_tile = MOMENTUM * lax.dynamic_slice_in_dim(out_mom, mz * out_own, out_own, 0) + grad_out
    out_rows = place([out_tile] + [lax.ppermute(out_tile, "dp", [(j ^ s, j) for j in range(FFN, n_dp)]) for s in shifts], 0)
    out_rows = jnp.pad(out_rows, ((0, hidden_own - out_rows.shape[0]), (0, 0)))
    matrix = jnp.where(me < FFN, own_mom + matrix.astype(F32), out_rows)
    gram_part = gram_upper(matrix)
    gram = lax.psum(gram_part, "mp")

    d_kv = sum_dp(lambda t: lax.dynamic_slice_in_dim(d_kv, t * rows, rows, 0))
    d_q, d_kv = d_q.astype(BF), d_kv.astype(BF)
    d_first = dot(d_q, q_low) + dot(d_kv, kv_low)
    d_input_norm, gain_first = norm_back(d_first, first_normed, first_scale, gains[0])
    input_grad = d_residual + d_input_norm

    gain_rows = jnp.stack([gain_first, gain_second])
    filler = -(factor_w.shape[1] + 2) % (8 * n_mp)

    d_all = jnp.concatenate([d_q[:, WQ:], d_kv[:, 2 * WK :], d_q[:, :WQ], d_kv[:, : 2 * WK]], axis=1)
    grad_factor = jnp.concatenate([dot_tn(d_all, first_own), jnp.pad(gain_rows, ((0, filler), (0, 0)))])
    height = grad_factor.shape[0] // n_mp
    if n_mp == 2 * CHIPS:
        grad_factor = core_half(grad_factor.reshape(CHIPS, 2, height, D), 1).reshape(CHIPS * height, D)
    grad_factor = sum_dp(lambda t: lax.dynamic_slice_in_dim(grad_factor, t * d_own, d_own, 1))
    dp_summed = grad_factor
    if n_mp == 2 * CHIPS:
        grad_factor = grad_factor.reshape(CHIPS, height, d_own)
        grad_factor = collect([pick(grad_factor, (mz // 2) ^ s) for s in range(CHIPS)])
    else:
        grad_factor = lax.psum_scatter(grad_factor, "mp", scatter_dimension=0, tiled=True)
    factor_piece = jnp.pad(MOMENTUM * factor_mom.T, ((0, filler + 2), (0, 0)))
    factor_piece = lax.dynamic_slice_in_dim(factor_piece, mz * height, height, 0) + grad_factor
    factor_all = lax.all_gather(factor_piece, ("dp", "mp"), axis=0, tiled=True).reshape(n_dp, n_mp * height, d_own)
    factor_tile = pick(factor_all, me)
    gain_grad = factor_tile[factor_w.shape[1] : factor_w.shape[1] + 2]

    def give_back(whole):
        pieces = [lax.dynamic_slice_in_dim(whole, (me ^ s) * d_own, d_own, 1) for s in range(n_dp)]
        came = [lax.ppermute(pieces[s], "dp", dp_pairs(s, lambda t: t ^ s < FFN))[None] for s in shifts]
        return place([pieces[0][None]] + came, 0), pieces[1:]

    mom_back, _ = give_back(after(matrix, dp_summed))
    ortho = ns_big(gram, after(matrix, factor_piece, mom_back))
    ortho = after(ortho, factor_all)
    branch += [pass_chip(after(part, ortho), 3) for part in last]
    block_out = (residual + sum(part.astype(F32) for part in branch)).astype(BF)
    out_ortho = lax.dynamic_slice_in_dim(ortho, me * out_own, out_own, 0)
    for s in shifts:
        piece = lax.dynamic_slice_in_dim(ortho, (me ^ s) * out_own, out_own, 0)
        piece = lax.ppermute(piece, "dp", [(j, j ^ s) for j in range(FFN, n_dp)])
        out_ortho = jnp.where(me ^ s == FFN, piece, out_ortho)
    out_pair = after(jnp.stack([out_tile, out_ortho]), factor_all)
    out_both = lax.all_gather(out_pair, "mp", axis=1, tiled=True)
    new_out_mom = out_both[0]
    new_out_w = out_w - LEARN * 0.2 * math.sqrt(D) * out_both[1]
    ortho_back, sent = give_back(after(ortho, out_ortho))
    factor_ortho = ns_factor(factor_all, after(factor_tile, out_pair, *sent))
    ortho_back = after(ortho_back, factor_ortho)
    turn = lambda stack: jnp.stack([stack[0].T, stack[1].T])
    ffn_rate = LEARN * 0.2 * math.sqrt(max(D, hidden_own * n_mp))
    new_gate_up_mom, new_down_mom = turn(mom_back), mom_back[2]
    new_gate_up_w = gate_up_w - ffn_rate * turn(ortho_back)
    new_down_w = down_w - ffn_rate * ortho_back[2]
    widths = [NQ, NK, NK, WQ, WK, WK]
    factor_rate = jnp.concatenate([jnp.full((w, 1), LEARN * 0.2 * math.sqrt(max(D, w)), F32) for w in widths])
    new_factor_mom = factor_tile[: factor_w.shape[1]].T
    new_factor_w = factor_w - (factor_rate * factor_ortho[: factor_w.shape[1]]).T

    new_gain_mom = MOMENTUM * gain_mom + gain_grad
    new_gains = lax.dynamic_slice_in_dim(gains, me * d_own, d_own, 1) - LEARN_VEC * new_gain_mom
    return (
        block_out,
        input_grad,
        gain_grad,
        new_gains,
        new_gain_mom,
        new_factor_mom,
        new_factor_w,
        new_out_mom,
        new_out_w,
        new_gate_up_mom,
        new_gate_up_w,
        new_down_mom,
        new_down_w,
    )


def solution(mesh):
    token = P(("mp", "dp"), None)
    row = P("dp", None)
    ffn = P(None, "dp", "mp")
    down = P("mp", "dp")
    vec = P(None, "dp")
    return jax.shard_map(
        body,
        mesh=mesh,
        in_specs=(token, token, P("mp", None), P(), P(), vec, row, row, row, row, ffn, ffn, down, down),
        out_specs=(token, token, vec, vec, vec, row, row, row, row, ffn, ffn, down, down),
        check_vma=False,
    )
```

```python
import functools
import math
import jax
import jax.numpy as jnp
from jax import lax
from jax.experimental import pallas as pl
from jax.experimental.pallas import tpu as pltpu
BF=jnp.bfloat16; F32=jnp.float32
HEADS=16; HD=64; RQ=6; RK=2; D=1024
COEF_A=3.4445; COEF_B=-4.775; COEF_C=2.0315
NEG=-1e30
NS_STEPS=5

def split2(x):
    hi=x.astype(BF); return hi,(x-hi.astype(F32)).astype(BF)
def dot(a,b): return jnp.dot(a,b,preferred_element_type=F32)
def dot_nt(a,b): return lax.dot_general(a,b,(((1,),(1,)),((),())),preferred_element_type=F32)
def dot_tn(a,b): return lax.dot_general(a,b,(((0,),(0,)),((),())),preferred_element_type=F32)

def index_map(ref, heads):
    row=lax.broadcasted_iota(jnp.int32,ref.shape,0); col=lax.broadcasted_iota(jnp.int32,ref.shape,1)
    row=jnp.where(row>=heads,row-heads,row)
    ref[...]=row-HEADS*lax.shift_right_logical(col,7)-(lax.bitwise_and(col,127)>=HD).astype(jnp.int32)

def one_hot(ref, pair): return jnp.where(ref[...]==2*pair,1.0,0.0).astype(BF)

def twice(dims,r,scale):
    part=dims[:,r*HD:(r+1)*HD]*scale
    return jnp.concatenate([part,part],axis=1)

WQ,WK=RQ*HD,RK*HD
NQ,NK=RQ*HEADS,RK*HEADS

def attn_setup(base_ref,fq_ref,fk_ref,bias_ref,hq,hk,dq,dk,iq,ik,scaled):
    rows,keys=bias_ref.shape
    r_id=lax.broadcasted_iota(jnp.int32,(rows,keys),0)+base_ref[0]*rows
    c_id=lax.broadcasted_iota(jnp.int32,(rows,keys),1)
    bias_ref[...]=jnp.where(c_id<=r_id,0.0,NEG)
    hq[...]=jnp.concatenate(split2(fq_ref[:,WQ:]),axis=1); hk[...]=jnp.concatenate(split2(fk_ref[:,2*WK:]),axis=1)
    for r in range(RQ): dq[r]=twice(fq_ref,r,1.0/RQ if scaled else 1.0)
    for r in range(2*RK): dk[r]=twice(fk_ref,r,1.0/RK if scaled else 1.0)
    index_map(iq,NQ); index_map(ik,2*NK)

def attn_scratch(rows,keys):
    return [pltpu.VMEM((rows,keys),F32),pltpu.VMEM((rows,2*NQ),BF),pltpu.VMEM((keys,4*NK),BF),pltpu.VMEM((RQ,rows,128),F32),pltpu.VMEM((2*RK,keys,128),F32),
        pltpu.VMEM((2*NQ,RQ*128),jnp.int32),pltpu.VMEM((4*NK,2*RK*128),jnp.int32)]

def lanes(x,r): return x[:,r*128:(r+1)*128]

def attn_fwd_body(base_ref,fq_ref,fk_ref,o_ref,lse_ref,q_ref,k_ref,v_ref,bias_ref,hq,hk,dq,dk,iq,ik):
    attn_setup(base_ref,fq_ref,fk_ref,bias_ref,hq,hk,dq,dk,iq,ik,True)
    lane=lax.broadcasted_iota(jnp.int32,(1,128),1)
    head_id=lax.broadcasted_iota(jnp.int32,(1,HEADS),1)
    lse_ref[...]=jnp.zeros_like(lse_ref)
    def step(pair,_):
        cols=pl.ds(pl.multiple_of(pair*128,128),128)
        wide_q=dot(hq[...],one_hot(iq,pair)); wide_k=dot(hk[...],one_hot(ik,pair))
        q=sum(lanes(wide_q,r)*dq[r] for r in range(RQ)).astype(BF)
        k=sum(lanes(wide_k,r)*dk[r] for r in range(RK)).astype(BF)
        v=sum(lanes(wide_k,r)*dk[r] for r in range(RK,2*RK)).astype(BF)
        q_ref[:,cols]=q; k_ref[:,cols]=k; v_ref[:,cols]=v
        qs=q.astype(F32)*(HD**-0.5)
        out=None
        for half in range(2):
            keep=(lane>=HD) if half else (lane<HD)
            qm=jnp.where(keep,qs,0.0).astype(BF)
            s=dot_nt(qm,k)+bias_ref[...]
            m=jnp.max(s,axis=1,keepdims=True)
            e=jnp.exp(s-m)
            l=jnp.sum(e,axis=1,keepdims=True)
            p=(e*(1.0/l)).astype(BF)
            o=dot(p,v)
            out=jnp.where(keep,o,out) if half else o
            lse_ref[...]=jnp.where(head_id==2*pair+half,m+jnp.log(l),lse_ref[...])
        o_ref[:,cols]=out.astype(BF)
        return 0
    lax.fori_loop(0,HEADS//2,step,0)

VM=pl.BlockSpec(memory_space=pltpu.VMEM)
SM=pl.BlockSpec(memory_space=pltpu.SMEM)
def shape(dims,dtype=F32): return jax.ShapeDtypeStruct(dims,dtype)
def cost(us): return pl.CostEstimate(flops=int(us*1.15e9),transcendentals=0,bytes_accessed=1<<20)
def limit(mib): return pltpu.CompilerParams(vmem_limit_bytes=mib<<20)

def attn_fwd(base,fq,fk,interpret=False):
    rows,keys=fq.shape[0],fk.shape[0]
    return pl.pallas_call(attn_fwd_body,
        out_shape=(shape((rows,D),BF),shape((rows,HEADS)),shape((rows,D),BF),shape((keys,D),BF),shape((keys,D),BF)),
        in_specs=[SM,VM,VM],out_specs=(VM,)*5,scratch_shapes=attn_scratch(rows,keys),
        compiler_params=limit(28),cost_estimate=cost(16),name="attn_fwd",interpret=interpret)(base,fq,fk)

def attn_bwd_body(first,last,base_ref,q_ref,k_ref,v_ref,do_ref,lse_ref,fq_ref,fk_ref,gq_ref,gk_ref,bias_ref,hq,hk,dq,dk,iq,ik,aq,ak,tq,tk):
    attn_setup(base_ref,fq_ref,fk_ref,bias_ref,hq,hk,dq,dk,iq,ik,False)
    for ref in (aq,ak,tq,tk): ref[...]=jnp.zeros_like(ref)
    lane=lax.broadcasted_iota(jnp.int32,(1,128),1)
    head_id=lax.broadcasted_iota(jnp.int32,(1,HEADS),1)
    def back(grads,h,d,index,acc,tot,pair):
        e=one_hot(index,pair)
        wide=dot(h[...],e)
        for r,grad in enumerate(grads): acc[r]+=grad*lanes(wide,r)
        terms=jnp.concatenate([(grad*d[r]).astype(BF) for r,grad in enumerate(grads)],axis=1)
        tot[...]+=dot_nt(terms,e[:tot.shape[1]])
    def step(pair,_):
        cols=pl.ds(pl.multiple_of(pair*128,128),128)
        q=q_ref[:,cols]; k=k_ref[:,cols]; v=v_ref[:,cols]; do=do_ref[:,cols]
        qs=q.astype(F32)*(HD**-0.5); dof=do.astype(F32)
        gq=gk=gv=None
        for half in range(2):
            keep=(lane>=HD) if half else (lane<HD)
            qm=jnp.where(keep,qs,0.0).astype(BF); dom=jnp.where(keep,dof,0.0).astype(BF)
            lse=jnp.sum(jnp.where(head_id==2*pair+half,lse_ref[...],0.0),axis=1,keepdims=True)
            p=jnp.exp(dot_nt(qm,k)+bias_ref[...]-lse)
            dp=dot_nt(dom,v)
            inner=jnp.sum(p*dp,axis=1,keepdims=True)
            ds=(p*(dp-inner)).astype(BF)
            nq=dot(ds,k); nk=dot_tn(ds,qm); nv=dot_tn(p.astype(BF),dom)
            if half==0: gq,gk,gv=nq,nk,nv
            else:
                gq=jnp.where(keep,nq,gq); gk=gk+nk; gv=gv+nv
        gq=gq*(HD**-0.5/RQ); gk=gk*(1.0/RK); gv=gv*(1.0/RK)
        back([gq]*RQ,hq,dq,iq,aq,tq,pair)
        back([gk]*RK+[gv]*RK,hk,dk,ik,ak,tk,pair)
        return 0
    lax.fori_loop(first,last,step,0)
    for acc,tot,ref in ((aq,tq,gq_ref),(ak,tk,gk_ref)):
        count=acc.shape[0]
        for r in range(0,count,2):
            even=acc[r]; odd=acc[r+1]
            ref[:,r*HD:(r+2)*HD]=jnp.concatenate([even[:,:HD]+even[:,HD:],odd[:,:HD]+odd[:,HD:]],axis=1)
        ref[:,count*HD:]=tot[...]

def attn_bwd(pairs,base,q,k,v,do,lse,fq,fk,us,interpret=False):
    rows,keys=q.shape[0],k.shape[0]
    return pl.pallas_call(functools.partial(attn_bwd_body,*pairs),out_shape=(shape(fq.shape),shape(fk.shape)),
        in_specs=[SM]+[VM]*7,out_specs=(VM,)*2,
        scratch_shapes=attn_scratch(rows,keys)+[pltpu.VMEM((RQ,rows,128),F32),pltpu.VMEM((2*RK,keys,128),F32),pltpu.VMEM((rows,NQ),F32),pltpu.VMEM((keys,2*NK),F32)],
        compiler_params=limit(36),cost_estimate=cost(us),name="attn_bwd",interpret=interpret)(base,q,k,v,do,lse,fq,fk)

BK=256
def tri_cols(j): return (j*(j+1)//2)*BK

def store_sym(hi,lo,i,j,val):
    h,l=split2(val)
    hi[i*BK:(i+1)*BK,j*BK:(j+1)*BK]=h; lo[i*BK:(i+1)*BK,j*BK:(j+1)*BK]=l
    if i!=j:
        t=val.T
        h,l=split2(t)
        hi[j*BK:(j+1)*BK,i*BK:(i+1)*BK]=h; lo[j*BK:(j+1)*BK,i*BK:(i+1)*BK]=l

def mul_upper(xh,xl,yh,yl,n,emit):
    for j in reversed(range(n)):
        top=(j+1)*BK; cs=slice(j*BK,(j+1)*BK)
        r=dot(xh[:top,:],yh[:,cs])+dot(xh[:top,:],yl[:,cs])+dot(xl[:top,:],yh[:,cs])
        for i in range(j+1): emit(i,j,r[i*BK:(i+1)*BK])

def ns_body(g_ref,y_ref,o_ref,a_up,ah,al,ph,pw,bh,bl):
    n=o_ref.shape[1]//BK
    eye=(lax.broadcasted_iota(jnp.int32,(BK,BK),0)==lax.broadcasted_iota(jnp.int32,(BK,BK),1)).astype(F32)
    blk=lambda i,j:(slice(i*BK,(i+1)*BK),slice(j*BK,(j+1)*BK))
    trace=None
    for j in range(n):
        off=tri_cols(j)+j*BK
        part=g_ref[:,off:off+BK]*eye
        trace=part if trace is None else trace+part
    trace=jnp.sum(jnp.sum(trace,axis=1,keepdims=True),axis=0,keepdims=True)
    scale=1.0/(jnp.sqrt(trace)+1e-7)
    for j in range(n):
        for i in range(j+1):
            off=tri_cols(j)+i*BK
            val=g_ref[:,off:off+BK]*(scale*scale)
            a_up[blk(i,j)]=val; store_sym(ah,al,i,j,val)
    o_ref[...]=y_ref[...]*scale
    def poly():
        def emit(i,j,c):
            store_sym(ph,pw,i,j,COEF_B*a_up[blk(i,j)]+COEF_C*c)
        mul_upper(ah,al,ah,al,n,emit)
    def apply():
        y=o_ref[...]; yh,yl=split2(y)
        o_ref[...]=COEF_A*y+(dot(yh,ph[...])+dot(yh,pw[...])+dot(yl,ph[...]))
    def step(k,c):
        poly()
        def emit_b(i,j,m):
            val=COEF_A*a_up[blk(i,j)]+m
            a_up[blk(i,j)]=val; store_sym(bh,bl,i,j,val)
        mul_upper(ah,al,ph,pw,n,emit_b)
        apply()
        def emit_a(i,j,m):
            val=COEF_A*a_up[blk(i,j)]+m
            a_up[blk(i,j)]=val; store_sym(ah,al,i,j,val)
        mul_upper(bh,bl,ph,pw,n,emit_a)
        return c
    lax.fori_loop(0,NS_STEPS-1,step,0)
    poly(); apply()

def ns_big(gram,y,interpret=False):
    w,d=y.shape
    vm=pl.BlockSpec(memory_space=pltpu.VMEM)
    return pl.pallas_call(ns_body,out_shape=jax.ShapeDtypeStruct((w,d),F32),
        in_specs=[vm,vm],out_specs=vm,
        scratch_shapes=[pltpu.VMEM((d,d),F32)]+[pltpu.VMEM((d,d),BF)]*6,
        compiler_params=pltpu.CompilerParams(vmem_limit_bytes=40<<20),cost_estimate=cost(71),name="ns_gram",interpret=interpret)(gram,y)

def gram_body(y_ref,g_ref):
    n=y_ref.shape[1]//BK
    yh,yl=split2(y_ref[...])
    for j in range(n):
        top=(j+1)*BK; cs=slice(j*BK,top)
        r=dot_tn(yh[:,:top],yh[:,cs])+dot_tn(yh[:,:top],yl[:,cs])+dot_tn(yl[:,:top],yh[:,cs])
        for i in range(j+1):
            off=tri_cols(j)+i*BK
            g_ref[:,off:off+BK]=r[i*BK:(i+1)*BK]

def gram_upper(y,interpret=False):
    d=y.shape[1]; n=d//BK
    vm=pl.BlockSpec(memory_space=pltpu.VMEM)
    return pl.pallas_call(gram_body,out_shape=jax.ShapeDtypeStruct((BK,n*(n+1)//2*BK),F32),in_specs=[vm],out_specs=vm,
        compiler_params=pltpu.CompilerParams(vmem_limit_bytes=16<<20),cost_estimate=cost(3),name="gram_upper",interpret=interpret)(y)


def mm3(x,y,f=dot):
    xh,xl=split2(x); yh,yl=split2(y)
    return f(xh,yh)+f(xh,yl)+f(xl,yh)

def seg_mask(n,widths):
    def ids(axis):
        pos=lax.broadcasted_iota(jnp.int32,(n,n),axis); out=jnp.zeros_like(pos); edge=0
        for w in widths:
            edge+=w; out=out+(pos>=edge).astype(jnp.int32)
        return out
    return (ids(0)==ids(1)).astype(F32)

GROUPS=((0,(NQ,NK,NK)),(NQ+2*NK,(WQ,)),(NQ+2*NK+WQ,(WK,WK)))

def ns_factor_body(all_ref,own_ref,out_ref):
    out_ref[sum(GROUPS[-1][1])+GROUPS[-1][0]:,:]=jnp.zeros((out_ref.shape[0]-sum(GROUPS[-1][1])-GROUPS[-1][0],out_ref.shape[1]),F32)
    state=[]
    for start,widths in GROUPS:
        n=sum(widths); rs=slice(start,start+n)
        mask=seg_mask(n,widths)
        eye=(lax.broadcasted_iota(jnp.int32,(n,n),0)==lax.broadcasted_iota(jnp.int32,(n,n),1)).astype(F32)
        a=mask*sum(mm3(all_ref[d,rs,:],all_ref[d,rs,:],dot_nt) for d in range(all_ref.shape[0]))
        diag=a*eye
        row=jnp.sum(mask*jnp.sum(diag,axis=1,keepdims=True),axis=0,keepdims=True)
        col=jnp.sum(mask*jnp.sum(diag,axis=0,keepdims=True),axis=1,keepdims=True)
        row=1.0/(jnp.sqrt(row)+1e-7); col=1.0/(jnp.sqrt(col)+1e-7)
        state+=[a*row*col,own_ref[rs,:]*col]
    def step(_,c):
        out=[]
        for a,x in zip(c[::2],c[1::2]):
            p=COEF_B*a+COEF_C*mm3(a,a)
            x=COEF_A*x+mm3(p,x)
            b=COEF_A*a+mm3(a,p)
            out+=[COEF_A*b+mm3(b,p),x]
        return tuple(out)
    state=lax.fori_loop(0,NS_STEPS-1,step,tuple(state))
    for (start,widths),a,x in zip(GROUPS,state[::2],state[1::2]):
        out_ref[start:start+sum(widths),:]=COEF_A*x+mm3(COEF_B*a+COEF_C*mm3(a,a),x)

def ns_factor(tiles,own,interpret=False):
    return pl.pallas_call(ns_factor_body,out_shape=shape(own.shape),in_specs=[VM]*2,out_specs=VM,
        compiler_params=limit(28),cost_estimate=cost(22),name="ns_factor",interpret=interpret)(tiles,own)

def ffn_body(x_ref,g_ref,w_ref,second_ref,branch_ref,hid_ref,dg_ref,du_ref):
    x=x_ref[...]
    gate=dot_nt(x,w_ref[0]); up=dot_nt(x,w_ref[1]); dh=dot_nt(g_ref[...],w_ref[2])
    sig=1.0/(1.0+jnp.exp(-gate))
    act=gate*sig
    hid=(act*up).astype(BF)
    dg=(dh*up*sig*(1.0+gate*(1.0-sig))).astype(BF)
    du=(dh*act).astype(BF)
    hid_ref[...]=hid; dg_ref[...]=dg; du_ref[...]=du
    second_ref[...]=(dot(dg,w_ref[0])+dot(du,w_ref[1])).astype(BF)
    branch_ref[...]=dot(hid,w_ref[2]).astype(BF)

def in_hbm(x): return pltpu.with_memory_space_constraint(x,pltpu.HBM)

def ffn_tokens(x_all,g_all,w,interpret=False):
    tokens=x_all.shape[0]; rows=256; hid=w.shape[1]
    block=pl.BlockSpec((rows,D),lambda i:(i,0)); part=pl.BlockSpec((rows,hid),lambda i:(i,0))
    return pl.pallas_call(ffn_body,out_shape=(pltpu.HBM((tokens,D),BF),)*2+(pltpu.HBM((tokens,hid),BF),)*3,
        grid=(tokens//rows,),in_specs=[block,block,pl.BlockSpec(w.shape,lambda i:(0,0,0),pipeline_mode=pl.Buffered(1))],
        out_specs=(block,block,part,part,part),
        compiler_params=limit(20),cost_estimate=cost(20),name="ffn_tokens",interpret=interpret)(in_hbm(x_all),in_hbm(g_all),w)

def ffn_grads_body(steps,hid_ref,dg_ref,du_ref,x_ref,g_ref,grad_ref,*total):
    width=hid_ref.shape[1]
    for c,(left,right) in enumerate(((dg_ref,x_ref),(du_ref,x_ref),(hid_ref,g_ref))):
        here=slice(c*width,(c+1)*width)
        part=dot_tn(left[...],right[...])
        if steps>1:
            part=jnp.where(pl.program_id(0)==0,part,part+total[0][c])
            total[0][c]=part
        grad_ref[here,:]=part.astype(BF)
    grad_ref[3*width:,:]=jnp.zeros((grad_ref.shape[0]-3*width,D),BF)

def ffn_grads(saved,x_all,g_all,n_dp,interpret=False):
    tokens,hid=saved[0].shape; rows=min(tokens,2048); steps=tokens//rows
    block=pl.BlockSpec((rows,D),lambda i:(i,0)); part=pl.BlockSpec((rows,hid),lambda i:(i,0))
    out=(n_dp*hid,D)
    return pl.pallas_call(functools.partial(ffn_grads_body,steps),out_shape=shape(out,BF),grid=(steps,),
        in_specs=[part]*3+[block]*2,out_specs=pl.BlockSpec(out,lambda i:(0,0)),
        scratch_shapes=[] if steps==1 else [pltpu.VMEM((3,hid,D),F32)],
        compiler_params=limit(40),cost_estimate=cost(10),name="ffn_grads",interpret=interpret)(*saved,x_all,g_all)


EPS = 1e-06
MOMENTUM = 0.5
LEARN = 0.2
LEARN_VEC = 0.002
P = jax.sharding.PartitionSpec
FFN = 3


def normalize(values):
    row_scale = lax.rsqrt(jnp.mean(values * values, axis=-1, keepdims=True) + EPS)
    return values * row_scale, row_scale


def norm_back(grad_in, normed, row_scale, gain):
    scaled = grad_in * gain
    inner_sum = jnp.mean(scaled * normed, axis=-1, keepdims=True)
    return row_scale * (scaled - normed * inner_sum), jnp.sum(grad_in * normed, axis=0)


def dp_pairs(shift, keep=lambda target: True):
    return [(j, j ^ shift) for j in range(lax.axis_size("dp")) if keep(j ^ shift)]


def place(parts, axis, me=None):
    me = lax.axis_index("dp") if me is None else me
    step = parts[0].shape[axis]
    shape = list(parts[0].shape)
    shape[axis] *= len(parts)
    out = jnp.zeros(shape, parts[0].dtype)
    for shift, part in enumerate(parts):
        out = lax.dynamic_update_slice_in_dim(out, part, (me ^ shift) * step, axis)
    return out


def gather_dp(own, axis=0):
    return place([own] + [lax.ppermute(own, "dp", dp_pairs(s)) for s in range(1, lax.axis_size("dp"))], axis)


def sum_dp(block_for, during=None, alongside=(), gate=None):
    me = lax.axis_index("dp")
    sent = [block_for(me ^ s).astype(BF) for s in range(1, lax.axis_size("dp"))]
    if gate is not None:
        sent = [after(block, gate) for block in sent]
    total = block_for(me)
    aside = None
    if during is not None:
        aside = during(*sent)
        total = after(total, *aside, *alongside)
    for s, block in enumerate(sent, 1):
        total = total + lax.ppermute(block, "dp", dp_pairs(s)).astype(F32)
    return total if during is None else (total, aside)


def after(value, *others):
    return lax.optimization_barrier((value, *others))[0]


def pass_core(x):
    return lax.ppermute(x, "mp", [(j, j ^ 1) for j in range(lax.axis_size("mp"))])


def pass_chip(x, shift):
    return lax.ppermute(x, "mp", [(j, j ^ (2 * shift)) for j in range(lax.axis_size("mp"))])


def pick(x, index):
    return lax.dynamic_index_in_dim(x, index, 0, keepdims=False)


CHIPS = 4


def cross_chips(near):
    if len(near) == 1:
        return [lax.psum_scatter(near[0], "mp", scatter_dimension=0, tiled=True)]
    return [near[0]] + [pass_chip(near[s].astype(BF), s) for s in range(1, len(near))]


def collect(near):
    return sum(part.astype(F32) for part in cross_chips(near))


def core_half(partial, axis):
    core = lax.axis_index("mp") % 2
    away = lax.dynamic_index_in_dim(partial, 1 - core, axis, keepdims=False).astype(BF)
    return lax.dynamic_index_in_dim(partial, core, axis, keepdims=False) + pass_core(away).astype(F32)


def chip_sums(partial):
    if lax.axis_size("mp") != 2 * CHIPS:
        return [partial]
    near = core_half(partial.reshape(CHIPS, 2, -1, partial.shape[1]), 1)
    near = [pick(near, (lax.axis_index("mp") // 2) ^ s) for s in range(CHIPS)]
    return [near[0]] + [part.astype(BF) for part in near[1:]]


def body(
    tokens,
    cotangent,
    domain_ids,
    domain_weight,
    gains,
    gain_mom,
    factor_w,
    factor_mom,
    out_w,
    out_mom,
    gate_up_w,
    gate_up_mom,
    down_w,
    down_mom,
):
    n_dp, n_mp = lax.axis_size("dp"), lax.axis_size("mp")
    me, mz = lax.axis_index("dp"), lax.axis_index("mp")
    rows = tokens.shape[0]
    d_own = factor_w.shape[0]
    hidden_own = gate_up_w.shape[2]
    out_own = d_own // n_mp
    base = me.astype(jnp.int32).reshape(1)
    shifts = range(1, n_dp)

    edge = NQ + 2 * NK

    def q_rows(m):
        return jnp.concatenate([m[edge : edge + WQ], m[:NQ]])

    def kv_rows(m):
        return jnp.concatenate([m[edge + WQ :], m[NQ:edge]])

    factor_own = factor_w.T.astype(BF)
    kv_low = gather_dp(kv_rows(factor_own), 1)
    x_float = tokens.astype(F32)
    first_normed, first_scale = normalize(x_float)
    first_own = (first_normed * gains[0]).astype(BF)
    domain_range = jnp.arange(domain_weight.shape[0], dtype=jnp.int32)
    seq_weight = jnp.sum(jnp.where(domain_ids[0, 0] == domain_range, domain_weight, 0.0))
    d_output = cotangent.astype(F32) * seq_weight
    d_output_all = lax.all_gather(d_output.astype(BF), "mp", axis=0, tiled=True)
    kv_all = gather_dp(dot_nt(first_own, kv_low))
    q_low = gather_dp(after(q_rows(factor_own), kv_low), 1)
    q_own = dot_nt(first_own, q_low)
    attended, lse, queries, key_vecs, values = attn_fwd(base, q_own, kv_all)
    out_low = gather_dp(after(out_w.astype(BF), kv_all))
    residual = x_float + dot(attended, out_low)
    second_normed, second_scale = normalize(residual)

    ffn_own = jnp.stack([gate_up_w[0].T, gate_up_w[1].T, down_w])
    ffn_low = gather_dp(after(ffn_own.astype(BF), out_low), 2)
    second_own = (second_normed * gains[1]).astype(BF)
    to_ffn = lambda target: target < FFN
    ffn_slot = jnp.minimum(me, FFN - 1)
    ffn_mom = after(jnp.stack([gate_up_mom[0].T, gate_up_mom[1].T, down_mom]), ffn_low)
    own_mom = [pick(ffn_mom, ffn_slot)]
    for s in shifts:
        own_mom.append(lax.ppermute(pick(ffn_mom, jnp.minimum(me ^ s, FFN - 1)), "dp", dp_pairs(s, to_ffn)))
    second_in = lax.all_gather(second_own, "mp", axis=0, tiled=True)
    d_second, branch, *saved = ffn_tokens(second_in, d_output_all, after(ffn_low, *own_mom[1:]))
    d_second = lax.psum_scatter(d_second, "mp", scatter_dimension=0, tiled=True).astype(F32)
    grads = ffn_grads(saved, second_in, d_output_all, n_dp)
    branch = chip_sums(branch)
    d_second = after(d_second, grads, *branch)
    own_mom = MOMENTUM * place(own_mom, 1)
    matrix = lax.psum_scatter(grads, "dp", scatter_dimension=0, tiled=True)

    d_resid_norm, gain_second = norm_back(d_second, second_normed, second_scale, gains[1])
    d_residual = d_output + d_resid_norm
    d_residual_low = d_residual.astype(BF)
    d_attended = dot_nt(d_residual_low, out_low).astype(BF)

    def backward(pairs, us, *gates):
        return attn_bwd(pairs, after(base, *gates), queries, key_vecs, values, d_attended, lse, q_own, kv_all, us)

    grad_out = dot_tn(attended, d_residual_low)
    if n_mp == 2 * CHIPS:
        grad_out = core_half(grad_out.reshape(n_dp, CHIPS, 2, out_own, D), 2)
    grad_out = grad_out.reshape(n_dp, -1, D)
    last, branch = branch[3:], cross_chips([after(part, d_second) for part in branch[:3]])
    grad_out, (d_q, d_kv) = sum_dp(
        lambda t: pick(grad_out, t), during=functools.partial(backward, (0, HEADS // 2), 26), alongside=branch[1:]
    )
    d_q, d_kv = after((d_q, d_kv), grad_out)
    if n_mp == 2 * CHIPS:
        grad_out = grad_out.reshape(CHIPS, out_own, D)
        near = [pick(grad_out, (mz // 2) ^ s) for s in range(CHIPS)]
        near = near[:1] + [part.astype(BF) for part in near[1:]]
        grad_out = collect(near)
    else:
        grad_out = lax.psum_scatter(grad_out, "mp", scatter_dimension=0, tiled=True)
    out_tile = MOMENTUM * lax.dynamic_slice_in_dim(out_mom, mz * out_own, out_own, 0) + grad_out
    out_tile = after(out_tile, matrix)
    out_rows = place([out_tile] + [lax.ppermute(out_tile, "dp", [(j ^ s, j) for j in range(FFN, n_dp)]) for s in shifts], 0)
    out_rows = jnp.pad(out_rows, ((0, hidden_own - out_rows.shape[0]), (0, 0)))
    matrix = jnp.where(me < FFN, own_mom + matrix.astype(F32), out_rows)
    gram_part = gram_upper(matrix)
    gram = lax.psum(gram_part, "mp")

    d_kv = sum_dp(lambda t: lax.dynamic_slice_in_dim(d_kv, t * rows, rows, 0))
    d_q, d_kv = d_q.astype(BF), d_kv.astype(BF)
    d_first = dot(d_q, q_low) + dot(d_kv, kv_low)
    d_input_norm, gain_first = norm_back(d_first, first_normed, first_scale, gains[0])
    input_grad = d_residual + d_input_norm

    gain_rows = jnp.stack([gain_first, gain_second])
    filler = -(factor_w.shape[1] + 2) % (8 * n_mp)

    d_all = jnp.concatenate([d_q[:, WQ:], d_kv[:, 2 * WK :], d_q[:, :WQ], d_kv[:, : 2 * WK]], axis=1)
    grad_factor = jnp.concatenate([dot_tn(d_all, first_own), jnp.pad(gain_rows, ((0, filler), (0, 0)))])
    height = grad_factor.shape[0] // n_mp
    if n_mp == 2 * CHIPS:
        grad_factor = core_half(grad_factor.reshape(CHIPS, 2, height, D), 1).reshape(CHIPS * height, D)
    grad_factor = sum_dp(lambda t: lax.dynamic_slice_in_dim(grad_factor, t * d_own, d_own, 1))
    dp_summed = grad_factor
    if n_mp == 2 * CHIPS:
        grad_factor = grad_factor.reshape(CHIPS, height, d_own)
        grad_factor = collect([pick(grad_factor, (mz // 2) ^ s) for s in range(CHIPS)])
    else:
        grad_factor = lax.psum_scatter(grad_factor, "mp", scatter_dimension=0, tiled=True)
    factor_piece = jnp.pad(MOMENTUM * factor_mom.T, ((0, filler + 2), (0, 0)))
    factor_piece = lax.dynamic_slice_in_dim(factor_piece, mz * height, height, 0) + grad_factor
    factor_all = lax.all_gather(factor_piece, ("dp", "mp"), axis=0, tiled=True).reshape(n_dp, n_mp * height, d_own)
    factor_tile = pick(factor_all, me)
    gain_grad = factor_tile[factor_w.shape[1] : factor_w.shape[1] + 2]

    def give_back(whole):
        pieces = [lax.dynamic_slice_in_dim(whole, (me ^ s) * d_own, d_own, 1) for s in range(n_dp)]
        came = [lax.ppermute(pieces[s], "dp", dp_pairs(s, lambda t: t ^ s < FFN))[None] for s in shifts]
        return place([pieces[0][None]] + came, 0), pieces[1:]

    mom_back, _ = give_back(after(matrix, dp_summed))
    ortho = ns_big(gram, after(matrix, factor_piece, mom_back))
    ortho = after(ortho, factor_all)
    branch += [pass_chip(after(part, gram), 3) for part in last]
    ortho = after(ortho, *branch[3:])
    block_out = (residual + sum(part.astype(F32) for part in branch)).astype(BF)
    out_ortho = lax.dynamic_slice_in_dim(ortho, me * out_own, out_own, 0)
    for s in shifts:
        piece = lax.dynamic_slice_in_dim(ortho, (me ^ s) * out_own, out_own, 0)
        piece = lax.ppermute(piece, "dp", [(j, j ^ s) for j in range(FFN, n_dp)])
        out_ortho = jnp.where(me ^ s == FFN, piece, out_ortho)
    out_pair = after(jnp.stack([out_tile, out_ortho]), factor_all)
    out_both = lax.all_gather(out_pair, "mp", axis=1, tiled=True)
    new_out_mom = out_both[0]
    new_out_w = out_w - LEARN * 0.2 * math.sqrt(D) * out_both[1]
    ortho_back, sent = give_back(after(ortho, out_ortho))
    factor_ortho = ns_factor(factor_all, after(factor_tile, out_pair, *sent))
    ortho_back = after(ortho_back, factor_ortho)
    turn = lambda stack: jnp.stack([stack[0].T, stack[1].T])
    ffn_rate = LEARN * 0.2 * math.sqrt(max(D, hidden_own * n_mp))
    new_gate_up_mom, new_down_mom = turn(mom_back), mom_back[2]
    new_gate_up_w = gate_up_w - ffn_rate * turn(ortho_back)
    new_down_w = down_w - ffn_rate * ortho_back[2]
    widths = [NQ, NK, NK, WQ, WK, WK]
    factor_rate = jnp.concatenate([jnp.full((w, 1), LEARN * 0.2 * math.sqrt(max(D, w)), F32) for w in widths])
    new_factor_mom = factor_tile[: factor_w.shape[1]].T
    new_factor_w = factor_w - (factor_rate * factor_ortho[: factor_w.shape[1]]).T

    new_gain_mom = MOMENTUM * gain_mom + gain_grad
    new_gains = lax.dynamic_slice_in_dim(gains, me * d_own, d_own, 1) - LEARN_VEC * new_gain_mom
    return (
        block_out,
        input_grad,
        gain_grad,
        new_gains,
        new_gain_mom,
        new_factor_mom,
        new_factor_w,
        new_out_mom,
        new_out_w,
        new_gate_up_mom,
        new_gate_up_w,
        new_down_mom,
        new_down_w,
    )


def solution(mesh):
    token = P(("mp", "dp"), None)
    row = P("dp", None)
    ffn = P(None, "dp", "mp")
    down = P("mp", "dp")
    vec = P(None, "dp")
    return jax.shard_map(
        body,
        mesh=mesh,
        in_specs=(token, token, P("mp", None), P(), P(), vec, row, row, row, row, ffn, ffn, down, down),
        out_specs=(token, token, vec, vec, vec, row, row, row, row, ffn, ffn, down, down),
        check_vma=False,
    )
```

```python
import functools
import math
import jax
import jax.numpy as jnp
from jax import lax
from jax.experimental import pallas as pl
from jax.experimental.pallas import tpu as pltpu
BF=jnp.bfloat16; F32=jnp.float32
HEADS=16; HD=64; RQ=6; RK=2; D=1024
COEF_A=3.4445; COEF_B=-4.775; COEF_C=2.0315
NEG=-1e30
NS_STEPS=5

def split2(x):
    hi=x.astype(BF); return hi,(x-hi.astype(F32)).astype(BF)
def dot(a,b): return jnp.dot(a,b,preferred_element_type=F32)
def dot_nt(a,b): return lax.dot_general(a,b,(((1,),(1,)),((),())),preferred_element_type=F32)
def dot_tn(a,b): return lax.dot_general(a,b,(((0,),(0,)),((),())),preferred_element_type=F32)

def index_map(ref, heads):
    row=lax.broadcasted_iota(jnp.int32,ref.shape,0); col=lax.broadcasted_iota(jnp.int32,ref.shape,1)
    row=jnp.where(row>=heads,row-heads,row)
    ref[...]=row-HEADS*lax.shift_right_logical(col,7)-(lax.bitwise_and(col,127)>=HD).astype(jnp.int32)

def one_hot(ref, pair): return jnp.where(ref[...]==2*pair,1.0,0.0).astype(BF)

def twice(dims,r,scale):
    part=dims[:,r*HD:(r+1)*HD]*scale
    return jnp.concatenate([part,part],axis=1)

WQ,WK=RQ*HD,RK*HD
NQ,NK=RQ*HEADS,RK*HEADS

def attn_setup(base_ref,fq_ref,fk_ref,bias_ref,hq,hk,dq,dk,iq,ik,scaled):
    rows,keys=bias_ref.shape
    r_id=lax.broadcasted_iota(jnp.int32,(rows,keys),0)+base_ref[0]*rows
    c_id=lax.broadcasted_iota(jnp.int32,(rows,keys),1)
    bias_ref[...]=jnp.where(c_id<=r_id,0.0,NEG)
    hq[...]=jnp.concatenate(split2(fq_ref[:,WQ:]),axis=1); hk[...]=jnp.concatenate(split2(fk_ref[:,2*WK:]),axis=1)
    for r in range(RQ): dq[r]=twice(fq_ref,r,1.0/RQ if scaled else 1.0)
    for r in range(2*RK): dk[r]=twice(fk_ref,r,1.0/RK if scaled else 1.0)
    index_map(iq,NQ); index_map(ik,2*NK)

def attn_scratch(rows,keys):
    return [pltpu.VMEM((rows,keys),F32),pltpu.VMEM((rows,2*NQ),BF),pltpu.VMEM((keys,4*NK),BF),pltpu.VMEM((RQ,rows,128),F32),pltpu.VMEM((2*RK,keys,128),F32),
        pltpu.VMEM((2*NQ,RQ*128),jnp.int32),pltpu.VMEM((4*NK,2*RK*128),jnp.int32)]

def lanes(x,r): return x[:,r*128:(r+1)*128]

def attn_fwd_body(base_ref,fq_ref,fk_ref,o_ref,lse_ref,q_ref,k_ref,v_ref,bias_ref,hq,hk,dq,dk,iq,ik):
    attn_setup(base_ref,fq_ref,fk_ref,bias_ref,hq,hk,dq,dk,iq,ik,True)
    lane=lax.broadcasted_iota(jnp.int32,(1,128),1)
    head_id=lax.broadcasted_iota(jnp.int32,(1,HEADS),1)
    lse_ref[...]=jnp.zeros_like(lse_ref)
    def step(pair,_):
        cols=pl.ds(pl.multiple_of(pair*128,128),128)
        wide_q=dot(hq[...],one_hot(iq,pair)); wide_k=dot(hk[...],one_hot(ik,pair))
        q=sum(lanes(wide_q,r)*dq[r] for r in range(RQ)).astype(BF)
        k=sum(lanes(wide_k,r)*dk[r] for r in range(RK)).astype(BF)
        v=sum(lanes(wide_k,r)*dk[r] for r in range(RK,2*RK)).astype(BF)
        q_ref[:,cols]=q; k_ref[:,cols]=k; v_ref[:,cols]=v
        qs=q.astype(F32)*(HD**-0.5)
        out=None
        for half in range(2):
            keep=(lane>=HD) if half else (lane<HD)
            qm=jnp.where(keep,qs,0.0).astype(BF)
            s=dot_nt(qm,k)+bias_ref[...]
            m=jnp.max(s,axis=1,keepdims=True)
            e=jnp.exp(s-m)
            l=jnp.sum(e,axis=1,keepdims=True)
            p=(e*(1.0/l)).astype(BF)
            o=dot(p,v)
            out=jnp.where(keep,o,out) if half else o
            lse_ref[...]=jnp.where(head_id==2*pair+half,m+jnp.log(l),lse_ref[...])
        o_ref[:,cols]=out.astype(BF)
        return 0
    lax.fori_loop(0,HEADS//2,step,0)

VM=pl.BlockSpec(memory_space=pltpu.VMEM)
SM=pl.BlockSpec(memory_space=pltpu.SMEM)
def shape(dims,dtype=F32): return jax.ShapeDtypeStruct(dims,dtype)
def cost(us): return pl.CostEstimate(flops=int(us*1.15e9),transcendentals=0,bytes_accessed=1<<20)
def limit(mib): return pltpu.CompilerParams(vmem_limit_bytes=mib<<20)

def attn_fwd(base,fq,fk,interpret=False):
    rows,keys=fq.shape[0],fk.shape[0]
    return pl.pallas_call(attn_fwd_body,
        out_shape=(shape((rows,D),BF),shape((rows,HEADS)),shape((rows,D),BF),shape((keys,D),BF),shape((keys,D),BF)),
        in_specs=[SM,VM,VM],out_specs=(VM,)*5,scratch_shapes=attn_scratch(rows,keys),
        compiler_params=limit(28),cost_estimate=cost(16),name="attn_fwd",interpret=interpret)(base,fq,fk)

def attn_bwd_body(first,last,base_ref,q_ref,k_ref,v_ref,do_ref,lse_ref,fq_ref,fk_ref,gq_ref,gk_ref,bias_ref,hq,hk,dq,dk,iq,ik,aq,ak,tq,tk):
    attn_setup(base_ref,fq_ref,fk_ref,bias_ref,hq,hk,dq,dk,iq,ik,False)
    for ref in (aq,ak,tq,tk): ref[...]=jnp.zeros_like(ref)
    lane=lax.broadcasted_iota(jnp.int32,(1,128),1)
    head_id=lax.broadcasted_iota(jnp.int32,(1,HEADS),1)
    def back(grads,h,d,index,acc,tot,pair):
        e=one_hot(index,pair)
        wide=dot(h[...],e)
        for r,grad in enumerate(grads): acc[r]+=grad*lanes(wide,r)
        terms=jnp.concatenate([(grad*d[r]).astype(BF) for r,grad in enumerate(grads)],axis=1)
        tot[...]+=dot_nt(terms,e[:tot.shape[1]])
    def step(pair,_):
        cols=pl.ds(pl.multiple_of(pair*128,128),128)
        q=q_ref[:,cols]; k=k_ref[:,cols]; v=v_ref[:,cols]; do=do_ref[:,cols]
        qs=q.astype(F32)*(HD**-0.5); dof=do.astype(F32)
        gq=gk=gv=None
        for half in range(2):
            keep=(lane>=HD) if half else (lane<HD)
            qm=jnp.where(keep,qs,0.0).astype(BF); dom=jnp.where(keep,dof,0.0).astype(BF)
            lse=jnp.sum(jnp.where(head_id==2*pair+half,lse_ref[...],0.0),axis=1,keepdims=True)
            p=jnp.exp(dot_nt(qm,k)+bias_ref[...]-lse)
            dp=dot_nt(dom,v)
            inner=jnp.sum(p*dp,axis=1,keepdims=True)
            ds=(p*(dp-inner)).astype(BF)
            nq=dot(ds,k); nk=dot_tn(ds,qm); nv=dot_tn(p.astype(BF),dom)
            if half==0: gq,gk,gv=nq,nk,nv
            else:
                gq=jnp.where(keep,nq,gq); gk=gk+nk; gv=gv+nv
        gq=gq*(HD**-0.5/RQ); gk=gk*(1.0/RK); gv=gv*(1.0/RK)
        back([gq]*RQ,hq,dq,iq,aq,tq,pair)
        back([gk]*RK+[gv]*RK,hk,dk,ik,ak,tk,pair)
        return 0
    lax.fori_loop(first,last,step,0)
    for acc,tot,ref in ((aq,tq,gq_ref),(ak,tk,gk_ref)):
        count=acc.shape[0]
        for r in range(0,count,2):
            even=acc[r]; odd=acc[r+1]
            ref[:,r*HD:(r+2)*HD]=jnp.concatenate([even[:,:HD]+even[:,HD:],odd[:,:HD]+odd[:,HD:]],axis=1)
        ref[:,count*HD:]=tot[...]

def attn_bwd(pairs,base,q,k,v,do,lse,fq,fk,us,interpret=False):
    rows,keys=q.shape[0],k.shape[0]
    return pl.pallas_call(functools.partial(attn_bwd_body,*pairs),out_shape=(shape(fq.shape),shape(fk.shape)),
        in_specs=[SM]+[VM]*7,out_specs=(VM,)*2,
        scratch_shapes=attn_scratch(rows,keys)+[pltpu.VMEM((RQ,rows,128),F32),pltpu.VMEM((2*RK,keys,128),F32),pltpu.VMEM((rows,NQ),F32),pltpu.VMEM((keys,2*NK),F32)],
        compiler_params=limit(36),cost_estimate=cost(us),name="attn_bwd",interpret=interpret)(base,q,k,v,do,lse,fq,fk)

BK=256
def tri_cols(j): return (j*(j+1)//2)*BK

def store_sym(hi,lo,i,j,val):
    h,l=split2(val)
    hi[i*BK:(i+1)*BK,j*BK:(j+1)*BK]=h; lo[i*BK:(i+1)*BK,j*BK:(j+1)*BK]=l
    if i!=j:
        t=val.T
        h,l=split2(t)
        hi[j*BK:(j+1)*BK,i*BK:(i+1)*BK]=h; lo[j*BK:(j+1)*BK,i*BK:(i+1)*BK]=l

def mul_upper(xh,xl,yh,yl,n,emit):
    for j in reversed(range(n)):
        top=(j+1)*BK; cs=slice(j*BK,(j+1)*BK)
        r=dot(xh[:top,:],yh[:,cs])+dot(xh[:top,:],yl[:,cs])+dot(xl[:top,:],yh[:,cs])
        for i in range(j+1): emit(i,j,r[i*BK:(i+1)*BK])

def ns_body(g_ref,y_ref,o_ref,a_up,ah,al,ph,pw,bh,bl):
    n=o_ref.shape[1]//BK
    eye=(lax.broadcasted_iota(jnp.int32,(BK,BK),0)==lax.broadcasted_iota(jnp.int32,(BK,BK),1)).astype(F32)
    blk=lambda i,j:(slice(i*BK,(i+1)*BK),slice(j*BK,(j+1)*BK))
    trace=None
    for j in range(n):
        off=tri_cols(j)+j*BK
        part=g_ref[:,off:off+BK]*eye
        trace=part if trace is None else trace+part
    trace=jnp.sum(jnp.sum(trace,axis=1,keepdims=True),axis=0,keepdims=True)
    scale=1.0/(jnp.sqrt(trace)+1e-7)
    for j in range(n):
        for i in range(j+1):
            off=tri_cols(j)+i*BK
            val=g_ref[:,off:off+BK]*(scale*scale)
            a_up[blk(i,j)]=val; store_sym(ah,al,i,j,val)
    o_ref[...]=y_ref[...]*scale
    def poly():
        def emit(i,j,c):
            store_sym(ph,pw,i,j,COEF_B*a_up[blk(i,j)]+COEF_C*c)
        mul_upper(ah,al,ah,al,n,emit)
    def apply():
        y=o_ref[...]; yh,yl=split2(y)
        o_ref[...]=COEF_A*y+(dot(yh,ph[...])+dot(yh,pw[...])+dot(yl,ph[...]))
    def step(k,c):
        poly()
        def emit_b(i,j,m):
            val=COEF_A*a_up[blk(i,j)]+m
            a_up[blk(i,j)]=val; store_sym(bh,bl,i,j,val)
        mul_upper(ah,al,ph,pw,n,emit_b)
        apply()
        def emit_a(i,j,m):
            val=COEF_A*a_up[blk(i,j)]+m
            a_up[blk(i,j)]=val; store_sym(ah,al,i,j,val)
        mul_upper(bh,bl,ph,pw,n,emit_a)
        return c
    lax.fori_loop(0,NS_STEPS-1,step,0)
    poly(); apply()

def ns_big(gram,y,interpret=False):
    w,d=y.shape
    vm=pl.BlockSpec(memory_space=pltpu.VMEM)
    return pl.pallas_call(ns_body,out_shape=jax.ShapeDtypeStruct((w,d),F32),
        in_specs=[vm,vm],out_specs=vm,
        scratch_shapes=[pltpu.VMEM((d,d),F32)]+[pltpu.VMEM((d,d),BF)]*6,
        compiler_params=pltpu.CompilerParams(vmem_limit_bytes=40<<20),cost_estimate=cost(71),name="ns_gram",interpret=interpret)(gram,y)

def gram_body(y_ref,g_ref):
    n=y_ref.shape[1]//BK
    yh,yl=split2(y_ref[...])
    for j in range(n):
        top=(j+1)*BK; cs=slice(j*BK,top)
        r=dot_tn(yh[:,:top],yh[:,cs])+dot_tn(yh[:,:top],yl[:,cs])+dot_tn(yl[:,:top],yh[:,cs])
        for i in range(j+1):
            off=tri_cols(j)+i*BK
            g_ref[:,off:off+BK]=r[i*BK:(i+1)*BK]

def gram_upper(y,interpret=False):
    d=y.shape[1]; n=d//BK
    vm=pl.BlockSpec(memory_space=pltpu.VMEM)
    return pl.pallas_call(gram_body,out_shape=jax.ShapeDtypeStruct((BK,n*(n+1)//2*BK),F32),in_specs=[vm],out_specs=vm,
        compiler_params=pltpu.CompilerParams(vmem_limit_bytes=16<<20),cost_estimate=cost(3),name="gram_upper",interpret=interpret)(y)


def mm3(x,y,f=dot):
    xh,xl=split2(x); yh,yl=split2(y)
    return f(xh,yh)+f(xh,yl)+f(xl,yh)

def seg_mask(n,widths):
    def ids(axis):
        pos=lax.broadcasted_iota(jnp.int32,(n,n),axis); out=jnp.zeros_like(pos); edge=0
        for w in widths:
            edge+=w; out=out+(pos>=edge).astype(jnp.int32)
        return out
    return (ids(0)==ids(1)).astype(F32)

GROUPS=((0,(NQ,NK,NK)),(NQ+2*NK,(WQ,)),(NQ+2*NK+WQ,(WK,WK)))

def ns_factor_body(all_ref,own_ref,out_ref):
    out_ref[sum(GROUPS[-1][1])+GROUPS[-1][0]:,:]=jnp.zeros((out_ref.shape[0]-sum(GROUPS[-1][1])-GROUPS[-1][0],out_ref.shape[1]),F32)
    state=[]
    for start,widths in GROUPS:
        n=sum(widths); rs=slice(start,start+n)
        mask=seg_mask(n,widths)
        eye=(lax.broadcasted_iota(jnp.int32,(n,n),0)==lax.broadcasted_iota(jnp.int32,(n,n),1)).astype(F32)
        a=mask*sum(mm3(all_ref[d,rs,:],all_ref[d,rs,:],dot_nt) for d in range(all_ref.shape[0]))
        diag=a*eye
        row=jnp.sum(mask*jnp.sum(diag,axis=1,keepdims=True),axis=0,keepdims=True)
        col=jnp.sum(mask*jnp.sum(diag,axis=0,keepdims=True),axis=1,keepdims=True)
        row=1.0/(jnp.sqrt(row)+1e-7); col=1.0/(jnp.sqrt(col)+1e-7)
        state+=[a*row*col,own_ref[rs,:]*col]
    def step(_,c):
        out=[]
        for a,x in zip(c[::2],c[1::2]):
            p=COEF_B*a+COEF_C*mm3(a,a)
            x=COEF_A*x+mm3(p,x)
            b=COEF_A*a+mm3(a,p)
            out+=[COEF_A*b+mm3(b,p),x]
        return tuple(out)
    state=lax.fori_loop(0,NS_STEPS-1,step,tuple(state))
    for (start,widths),a,x in zip(GROUPS,state[::2],state[1::2]):
        out_ref[start:start+sum(widths),:]=COEF_A*x+mm3(COEF_B*a+COEF_C*mm3(a,a),x)

def ns_factor(tiles,own,interpret=False):
    return pl.pallas_call(ns_factor_body,out_shape=shape(own.shape),in_specs=[VM]*2,out_specs=VM,
        compiler_params=limit(28),cost_estimate=cost(22),name="ns_factor",interpret=interpret)(tiles,own)

def ffn_body(x_ref,g_ref,w_ref,second_ref,branch_ref,hid_ref,dg_ref,du_ref):
    x=x_ref[...]
    gate=dot_nt(x,w_ref[0]); up=dot_nt(x,w_ref[1]); dh=dot_nt(g_ref[...],w_ref[2])
    sig=1.0/(1.0+jnp.exp(-gate))
    act=gate*sig
    hid=(act*up).astype(BF)
    dg=(dh*up*sig*(1.0+gate*(1.0-sig))).astype(BF)
    du=(dh*act).astype(BF)
    hid_ref[...]=hid; dg_ref[...]=dg; du_ref[...]=du
    second_ref[...]=(dot(dg,w_ref[0])+dot(du,w_ref[1])).astype(BF)
    branch_ref[...]=dot(hid,w_ref[2]).astype(BF)

def in_hbm(x): return pltpu.with_memory_space_constraint(x,pltpu.HBM)

def ffn_tokens(x_all,g_all,w,interpret=False):
    tokens=x_all.shape[0]; rows=256; hid=w.shape[1]
    block=pl.BlockSpec((rows,D),lambda i:(i,0)); part=pl.BlockSpec((rows,hid),lambda i:(i,0))
    return pl.pallas_call(ffn_body,out_shape=(pltpu.HBM((tokens,D),BF),)*2+(pltpu.HBM((tokens,hid),BF),)*3,
        grid=(tokens//rows,),in_specs=[block,block,pl.BlockSpec(w.shape,lambda i:(0,0,0),pipeline_mode=pl.Buffered(1))],
        out_specs=(block,block,part,part,part),
        compiler_params=limit(20),cost_estimate=cost(20),name="ffn_tokens",interpret=interpret)(in_hbm(x_all),in_hbm(g_all),w)

def ffn_grads_body(steps,hid_ref,dg_ref,du_ref,x_ref,g_ref,grad_ref,*total):
    width=hid_ref.shape[1]
    for c,(left,right) in enumerate(((dg_ref,x_ref),(du_ref,x_ref),(hid_ref,g_ref))):
        here=slice(c*width,(c+1)*width)
        part=dot_tn(left[...],right[...])
        if steps>1:
            part=jnp.where(pl.program_id(0)==0,part,part+total[0][c])
            total[0][c]=part
        grad_ref[here,:]=part.astype(BF)
    grad_ref[3*width:,:]=jnp.zeros((grad_ref.shape[0]-3*width,D),BF)

def ffn_grads(saved,x_all,g_all,n_dp,interpret=False):
    tokens,hid=saved[0].shape; rows=min(tokens,2048); steps=tokens//rows
    block=pl.BlockSpec((rows,D),lambda i:(i,0)); part=pl.BlockSpec((rows,hid),lambda i:(i,0))
    out=(n_dp*hid,D)
    return pl.pallas_call(functools.partial(ffn_grads_body,steps),out_shape=shape(out,BF),grid=(steps,),
        in_specs=[part]*3+[block]*2,out_specs=pl.BlockSpec(out,lambda i:(0,0)),
        scratch_shapes=[] if steps==1 else [pltpu.VMEM((3,hid,D),F32)],
        compiler_params=limit(40),cost_estimate=cost(10),name="ffn_grads",interpret=interpret)(*saved,x_all,g_all)


EPS = 1e-06
MOMENTUM = 0.5
LEARN = 0.2
LEARN_VEC = 0.002
P = jax.sharding.PartitionSpec
FFN = 3


def normalize(values):
    row_scale = lax.rsqrt(jnp.mean(values * values, axis=-1, keepdims=True) + EPS)
    return values * row_scale, row_scale


def norm_back(grad_in, normed, row_scale, gain):
    scaled = grad_in * gain
    inner_sum = jnp.mean(scaled * normed, axis=-1, keepdims=True)
    return row_scale * (scaled - normed * inner_sum), jnp.sum(grad_in * normed, axis=0)


def dp_pairs(shift, keep=lambda target: True):
    return [(j, j ^ shift) for j in range(lax.axis_size("dp")) if keep(j ^ shift)]


def place(parts, axis, me=None):
    me = lax.axis_index("dp") if me is None else me
    step = parts[0].shape[axis]
    shape = list(parts[0].shape)
    shape[axis] *= len(parts)
    out = jnp.zeros(shape, parts[0].dtype)
    for shift, part in enumerate(parts):
        out = lax.dynamic_update_slice_in_dim(out, part, (me ^ shift) * step, axis)
    return out


def gather_dp(own, axis=0):
    return place([own] + [lax.ppermute(own, "dp", dp_pairs(s)) for s in range(1, lax.axis_size("dp"))], axis)


def sum_dp(block_for, during=None, alongside=(), gate=None):
    me = lax.axis_index("dp")
    sent = [block_for(me ^ s).astype(BF) for s in range(1, lax.axis_size("dp"))]
    if gate is not None:
        sent = [after(block, gate) for block in sent]
    total = block_for(me)
    aside = None
    if during is not None:
        aside = during(*sent)
        total = after(total, *aside, *alongside)
    for s, block in enumerate(sent, 1):
        total = total + lax.ppermute(block, "dp", dp_pairs(s)).astype(F32)
    return total if during is None else (total, aside)


def after(value, *others):
    return lax.optimization_barrier((value, *others))[0]


def pass_core(x):
    return lax.ppermute(x, "mp", [(j, j ^ 1) for j in range(lax.axis_size("mp"))])


def pass_chip(x, shift):
    return lax.ppermute(x, "mp", [(j, j ^ (2 * shift)) for j in range(lax.axis_size("mp"))])


def pick(x, index):
    return lax.dynamic_index_in_dim(x, index, 0, keepdims=False)


CHIPS = 4


def cross_chips(near):
    if len(near) == 1:
        return [lax.psum_scatter(near[0], "mp", scatter_dimension=0, tiled=True)]
    return [near[0]] + [pass_chip(near[s].astype(BF), s) for s in range(1, len(near))]


def collect(near):
    return sum(part.astype(F32) for part in cross_chips(near))


def core_half(partial, axis):
    core = lax.axis_index("mp") % 2
    away = lax.dynamic_index_in_dim(partial, 1 - core, axis, keepdims=False).astype(BF)
    return lax.dynamic_index_in_dim(partial, core, axis, keepdims=False) + pass_core(away).astype(F32)


def chip_sums(partial):
    if lax.axis_size("mp") != 2 * CHIPS:
        return [partial]
    near = core_half(partial.reshape(CHIPS, 2, -1, partial.shape[1]), 1)
    near = [pick(near, (lax.axis_index("mp") // 2) ^ s) for s in range(CHIPS)]
    return [near[0]] + [part.astype(BF) for part in near[1:]]


def body(
    tokens,
    cotangent,
    domain_ids,
    domain_weight,
    gains,
    gain_mom,
    factor_w,
    factor_mom,
    out_w,
    out_mom,
    gate_up_w,
    gate_up_mom,
    down_w,
    down_mom,
):
    n_dp, n_mp = lax.axis_size("dp"), lax.axis_size("mp")
    me, mz = lax.axis_index("dp"), lax.axis_index("mp")
    rows = tokens.shape[0]
    d_own = factor_w.shape[0]
    hidden_own = gate_up_w.shape[2]
    out_own = d_own // n_mp
    base = me.astype(jnp.int32).reshape(1)
    shifts = range(1, n_dp)

    edge = NQ + 2 * NK

    def q_rows(m):
        return jnp.concatenate([m[edge : edge + WQ], m[:NQ]])

    def kv_rows(m):
        return jnp.concatenate([m[edge + WQ :], m[NQ:edge]])

    factor_own = factor_w.T.astype(BF)
    kv_low = gather_dp(kv_rows(factor_own), 1)
    x_float = tokens.astype(F32)
    first_normed, first_scale = normalize(x_float)
    first_own = (first_normed * gains[0]).astype(BF)
    domain_range = jnp.arange(domain_weight.shape[0], dtype=jnp.int32)
    seq_weight = jnp.sum(jnp.where(domain_ids[0, 0] == domain_range, domain_weight, 0.0))
    d_output = cotangent.astype(F32) * seq_weight
    d_output_all = lax.all_gather(d_output.astype(BF), "mp", axis=0, tiled=True)
    kv_all = gather_dp(dot_nt(first_own, kv_low))
    q_low = gather_dp(q_rows(factor_own), 1)
    q_own = dot_nt(first_own, q_low)
    attended, lse, queries, key_vecs, values = attn_fwd(base, q_own, kv_all)
    out_low = gather_dp(after(out_w.astype(BF), kv_all))
    residual = x_float + dot(attended, out_low)
    second_normed, second_scale = normalize(residual)

    ffn_own = jnp.stack([gate_up_w[0].T, gate_up_w[1].T, down_w])
    ffn_low = gather_dp(after(ffn_own.astype(BF), out_low), 2)
    second_own = (second_normed * gains[1]).astype(BF)
    to_ffn = lambda target: target < FFN
    ffn_slot = jnp.minimum(me, FFN - 1)
    ffn_mom = after(jnp.stack([gate_up_mom[0].T, gate_up_mom[1].T, down_mom]), ffn_low)
    own_mom = [pick(ffn_mom, ffn_slot)]
    for s in shifts:
        own_mom.append(lax.ppermute(pick(ffn_mom, jnp.minimum(me ^ s, FFN - 1)), "dp", dp_pairs(s, to_ffn)))
    second_in = lax.all_gather(second_own, "mp", axis=0, tiled=True)
    d_second, branch, *saved = ffn_tokens(second_in, d_output_all, after(ffn_low, *own_mom[1:]))
    d_second = lax.psum_scatter(d_second, "mp", scatter_dimension=0, tiled=True).astype(F32)
    grads = ffn_grads(saved, second_in, d_output_all, n_dp)
    branch = chip_sums(branch)
    d_second = after(d_second, grads, *branch)
    own_mom = MOMENTUM * place(own_mom, 1)
    matrix = lax.psum_scatter(grads, "dp", scatter_dimension=0, tiled=True)

    d_resid_norm, gain_second = norm_back(d_second, second_normed, second_scale, gains[1])
    d_residual = d_output + d_resid_norm
    d_residual_low = d_residual.astype(BF)
    d_attended = dot_nt(d_residual_low, out_low).astype(BF)

    def backward(pairs, us, *gates):
        return attn_bwd(pairs, after(base, *gates), queries, key_vecs, values, d_attended, lse, q_own, kv_all, us)

    grad_out = dot_tn(attended, d_residual_low)
    if n_mp == 2 * CHIPS:
        grad_out = core_half(grad_out.reshape(n_dp, CHIPS, 2, out_own, D), 2)
    grad_out = grad_out.reshape(n_dp, -1, D)
    last, branch = branch[3:], cross_chips([after(part, d_second) for part in branch[:3]])
    grad_out, (d_q, d_kv) = sum_dp(
        lambda t: pick(grad_out, t), during=functools.partial(backward, (0, HEADS // 2), 26), alongside=branch[1:]
    )
    d_q, d_kv = after((d_q, d_kv), grad_out)
    if n_mp == 2 * CHIPS:
        grad_out = grad_out.reshape(CHIPS, out_own, D)
        near = [pick(grad_out, (mz // 2) ^ s) for s in range(CHIPS)]
        near = near[:1] + [part.astype(BF) for part in near[1:]]
        grad_out = collect(near)
    else:
        grad_out = lax.psum_scatter(grad_out, "mp", scatter_dimension=0, tiled=True)
    out_tile = MOMENTUM * lax.dynamic_slice_in_dim(out_mom, mz * out_own, out_own, 0) + grad_out
    out_rows = place([out_tile] + [lax.ppermute(out_tile, "dp", [(j ^ s, j) for j in range(FFN, n_dp)]) for s in shifts], 0)
    out_rows = after(out_rows, matrix)
    out_rows = jnp.pad(out_rows, ((0, hidden_own - out_rows.shape[0]), (0, 0)))
    matrix = jnp.where(me < FFN, own_mom + matrix.astype(F32), out_rows)
    gram_part = gram_upper(matrix)
    gram = lax.psum(gram_part, "mp")

    d_kv = sum_dp(lambda t: lax.dynamic_slice_in_dim(d_kv, t * rows, rows, 0))
    d_q, d_kv = d_q.astype(BF), d_kv.astype(BF)
    d_first = dot(d_q, q_low) + dot(d_kv, kv_low)
    d_input_norm, gain_first = norm_back(d_first, first_normed, first_scale, gains[0])
    input_grad = d_residual + d_input_norm

    gain_rows = jnp.stack([gain_first, gain_second])
    filler = -(factor_w.shape[1] + 2) % (8 * n_mp)

    d_all = jnp.concatenate([d_q[:, WQ:], d_kv[:, 2 * WK :], d_q[:, :WQ], d_kv[:, : 2 * WK]], axis=1)
    grad_factor = jnp.concatenate([dot_tn(d_all, first_own), jnp.pad(gain_rows, ((0, filler), (0, 0)))])
    height = grad_factor.shape[0] // n_mp
    if n_mp == 2 * CHIPS:
        grad_factor = core_half(grad_factor.reshape(CHIPS, 2, height, D), 1).reshape(CHIPS * height, D)
    grad_factor = sum_dp(lambda t: lax.dynamic_slice_in_dim(grad_factor, t * d_own, d_own, 1))
    dp_summed = grad_factor
    if n_mp == 2 * CHIPS:
        grad_factor = grad_factor.reshape(CHIPS, height, d_own)
        grad_factor = collect([pick(grad_factor, (mz // 2) ^ s) for s in range(CHIPS)])
    else:
        grad_factor = lax.psum_scatter(grad_factor, "mp", scatter_dimension=0, tiled=True)
    factor_piece = jnp.pad(MOMENTUM * factor_mom.T, ((0, filler + 2), (0, 0)))
    factor_piece = lax.dynamic_slice_in_dim(factor_piece, mz * height, height, 0) + grad_factor
    factor_all = lax.all_gather(factor_piece, ("dp", "mp"), axis=0, tiled=True).reshape(n_dp, n_mp * height, d_own)
    factor_tile = pick(factor_all, me)
    gain_grad = factor_tile[factor_w.shape[1] : factor_w.shape[1] + 2]

    def give_back(whole):
        pieces = [lax.dynamic_slice_in_dim(whole, (me ^ s) * d_own, d_own, 1) for s in range(n_dp)]
        came = [lax.ppermute(pieces[s], "dp", dp_pairs(s, lambda t: t ^ s < FFN))[None] for s in shifts]
        return place([pieces[0][None]] + came, 0), pieces[1:], came

    mom_back, _, came = give_back(after(matrix, dp_summed))
    ortho = ns_big(gram, after(matrix, factor_piece, *came))
    ortho = after(ortho, factor_all)
    branch += [pass_chip(after(part, gram), 3) for part in last]
    ortho = after(ortho, *branch[3:])
    block_out = (residual + sum(part.astype(F32) for part in branch)).astype(BF)
    out_ortho = lax.dynamic_slice_in_dim(ortho, me * out_own, out_own, 0)
    for s in shifts:
        piece = lax.dynamic_slice_in_dim(ortho, (me ^ s) * out_own, out_own, 0)
        piece = lax.ppermute(piece, "dp", [(j, j ^ s) for j in range(FFN, n_dp)])
        out_ortho = jnp.where(me ^ s == FFN, piece, out_ortho)
    out_pair = after(jnp.stack([out_tile, out_ortho]), factor_all)
    out_both = lax.all_gather(out_pair, "mp", axis=1, tiled=True)
    new_out_mom = out_both[0]
    new_out_w = out_w - LEARN * 0.2 * math.sqrt(D) * out_both[1]
    ortho_back, sent, _ = give_back(after(ortho, out_ortho))
    factor_ortho = ns_factor(factor_all, after(factor_tile, out_pair, *sent))
    ortho_back = after(ortho_back, factor_ortho)
    turn = lambda stack: jnp.stack([stack[0].T, stack[1].T])
    ffn_rate = LEARN * 0.2 * math.sqrt(max(D, hidden_own * n_mp))
    new_gate_up_mom, new_down_mom = turn(mom_back), mom_back[2]
    new_gate_up_w = gate_up_w - ffn_rate * turn(ortho_back)
    new_down_w = down_w - ffn_rate * ortho_back[2]
    widths = [NQ, NK, NK, WQ, WK, WK]
    factor_rate = jnp.concatenate([jnp.full((w, 1), LEARN * 0.2 * math.sqrt(max(D, w)), F32) for w in widths])
    new_factor_mom = factor_tile[: factor_w.shape[1]].T
    new_factor_w = factor_w - (factor_rate * factor_ortho[: factor_w.shape[1]]).T

    new_gain_mom = MOMENTUM * gain_mom + gain_grad
    new_gains = lax.dynamic_slice_in_dim(gains, me * d_own, d_own, 1) - LEARN_VEC * new_gain_mom
    return (
        block_out,
        input_grad,
        gain_grad,
        new_gains,
        new_gain_mom,
        new_factor_mom,
        new_factor_w,
        new_out_mom,
        new_out_w,
        new_gate_up_mom,
        new_gate_up_w,
        new_down_mom,
        new_down_w,
    )


def solution(mesh):
    token = P(("mp", "dp"), None)
    row = P("dp", None)
    ffn = P(None, "dp", "mp")
    down = P("mp", "dp")
    vec = P(None, "dp")
    return jax.shard_map(
        body,
        mesh=mesh,
        in_specs=(token, token, P("mp", None), P(), P(), vec, row, row, row, row, ffn, ffn, down, down),
        out_specs=(token, token, vec, vec, vec, row, row, row, row, ffn, ffn, down, down),
        check_vma=False,
    )
```

```python
import functools
import math
import jax
import jax.numpy as jnp
from jax import lax
from jax.experimental import pallas as pl
from jax.experimental.pallas import tpu as pltpu
BF=jnp.bfloat16; F32=jnp.float32
HEADS=16; HD=64; RQ=6; RK=2; D=1024
COEF_A=3.4445; COEF_B=-4.775; COEF_C=2.0315
NEG=-1e30
NS_STEPS=5

def split2(x):
    hi=x.astype(BF); return hi,(x-hi.astype(F32)).astype(BF)
def dot(a,b): return jnp.dot(a,b,preferred_element_type=F32)
def dot_nt(a,b): return lax.dot_general(a,b,(((1,),(1,)),((),())),preferred_element_type=F32)
def dot_tn(a,b): return lax.dot_general(a,b,(((0,),(0,)),((),())),preferred_element_type=F32)

def index_map(ref, heads):
    row=lax.broadcasted_iota(jnp.int32,ref.shape,0); col=lax.broadcasted_iota(jnp.int32,ref.shape,1)
    row=jnp.where(row>=heads,row-heads,row)
    ref[...]=row-HEADS*lax.shift_right_logical(col,7)-(lax.bitwise_and(col,127)>=HD).astype(jnp.int32)

def one_hot(ref, pair): return jnp.where(ref[...]==2*pair,1.0,0.0).astype(BF)

def twice(dims,r,scale):
    part=dims[:,r*HD:(r+1)*HD]*scale
    return jnp.concatenate([part,part],axis=1)

WQ,WK=RQ*HD,RK*HD
NQ,NK=RQ*HEADS,RK*HEADS

def attn_setup(base_ref,fq_ref,fk_ref,bias_ref,hq,hk,dq,dk,iq,ik,scaled):
    rows,keys=bias_ref.shape
    r_id=lax.broadcasted_iota(jnp.int32,(rows,keys),0)+base_ref[0]*rows
    c_id=lax.broadcasted_iota(jnp.int32,(rows,keys),1)
    bias_ref[...]=jnp.where(c_id<=r_id,0.0,NEG)
    hq[...]=jnp.concatenate(split2(fq_ref[:,WQ:]),axis=1); hk[...]=jnp.concatenate(split2(fk_ref[:,2*WK:]),axis=1)
    for r in range(RQ): dq[r]=twice(fq_ref,r,1.0/RQ if scaled else 1.0)
    for r in range(2*RK): dk[r]=twice(fk_ref,r,1.0/RK if scaled else 1.0)
    index_map(iq,NQ); index_map(ik,2*NK)

def attn_scratch(rows,keys):
    return [pltpu.VMEM((rows,keys),F32),pltpu.VMEM((rows,2*NQ),BF),pltpu.VMEM((keys,4*NK),BF),pltpu.VMEM((RQ,rows,128),F32),pltpu.VMEM((2*RK,keys,128),F32),
        pltpu.VMEM((2*NQ,RQ*128),jnp.int32),pltpu.VMEM((4*NK,2*RK*128),jnp.int32)]

def lanes(x,r): return x[:,r*128:(r+1)*128]

def attn_fwd_body(base_ref,fq_ref,fk_ref,o_ref,lse_ref,q_ref,k_ref,v_ref,bias_ref,hq,hk,dq,dk,iq,ik):
    attn_setup(base_ref,fq_ref,fk_ref,bias_ref,hq,hk,dq,dk,iq,ik,True)
    lane=lax.broadcasted_iota(jnp.int32,(1,128),1)
    head_id=lax.broadcasted_iota(jnp.int32,(1,HEADS),1)
    lse_ref[...]=jnp.zeros_like(lse_ref)
    def step(pair,_):
        cols=pl.ds(pl.multiple_of(pair*128,128),128)
        wide_q=dot(hq[...],one_hot(iq,pair)); wide_k=dot(hk[...],one_hot(ik,pair))
        q=sum(lanes(wide_q,r)*dq[r] for r in range(RQ)).astype(BF)
        k=sum(lanes(wide_k,r)*dk[r] for r in range(RK)).astype(BF)
        v=sum(lanes(wide_k,r)*dk[r] for r in range(RK,2*RK)).astype(BF)
        q_ref[:,cols]=q; k_ref[:,cols]=k; v_ref[:,cols]=v
        qs=q.astype(F32)*(HD**-0.5)
        out=None
        for half in range(2):
            keep=(lane>=HD) if half else (lane<HD)
            qm=jnp.where(keep,qs,0.0).astype(BF)
            s=dot_nt(qm,k)+bias_ref[...]
            m=jnp.max(s,axis=1,keepdims=True)
            e=jnp.exp(s-m)
            l=jnp.sum(e,axis=1,keepdims=True)
            p=(e*(1.0/l)).astype(BF)
            o=dot(p,v)
            out=jnp.where(keep,o,out) if half else o
            lse_ref[...]=jnp.where(head_id==2*pair+half,m+jnp.log(l),lse_ref[...])
        o_ref[:,cols]=out.astype(BF)
        return 0
    lax.fori_loop(0,HEADS//2,step,0)

VM=pl.BlockSpec(memory_space=pltpu.VMEM)
SM=pl.BlockSpec(memory_space=pltpu.SMEM)
def shape(dims,dtype=F32): return jax.ShapeDtypeStruct(dims,dtype)
def cost(us): return pl.CostEstimate(flops=int(us*1.15e9),transcendentals=0,bytes_accessed=1<<20)
def limit(mib): return pltpu.CompilerParams(vmem_limit_bytes=mib<<20)

def attn_fwd(base,fq,fk,interpret=False):
    rows,keys=fq.shape[0],fk.shape[0]
    return pl.pallas_call(attn_fwd_body,
        out_shape=(shape((rows,D),BF),shape((rows,HEADS)),shape((rows,D),BF),shape((keys,D),BF),shape((keys,D),BF)),
        in_specs=[SM,VM,VM],out_specs=(VM,)*5,scratch_shapes=attn_scratch(rows,keys),
        compiler_params=limit(28),cost_estimate=cost(16),name="attn_fwd",interpret=interpret)(base,fq,fk)

def attn_bwd_body(first,last,base_ref,q_ref,k_ref,v_ref,do_ref,lse_ref,fq_ref,fk_ref,gq_ref,gk_ref,bias_ref,hq,hk,dq,dk,iq,ik,aq,ak,tq,tk):
    attn_setup(base_ref,fq_ref,fk_ref,bias_ref,hq,hk,dq,dk,iq,ik,False)
    for ref in (aq,ak,tq,tk): ref[...]=jnp.zeros_like(ref)
    lane=lax.broadcasted_iota(jnp.int32,(1,128),1)
    head_id=lax.broadcasted_iota(jnp.int32,(1,HEADS),1)
    def back(grads,h,d,index,acc,tot,pair):
        e=one_hot(index,pair)
        wide=dot(h[...],e)
        for r,grad in enumerate(grads): acc[r]+=grad*lanes(wide,r)
        terms=jnp.concatenate([(grad*d[r]).astype(BF) for r,grad in enumerate(grads)],axis=1)
        tot[...]+=dot_nt(terms,e[:tot.shape[1]])
    def step(pair,_):
        cols=pl.ds(pl.multiple_of(pair*128,128),128)
        q=q_ref[:,cols]; k=k_ref[:,cols]; v=v_ref[:,cols]; do=do_ref[:,cols]
        qs=q.astype(F32)*(HD**-0.5); dof=do.astype(F32)
        gq=gk=gv=None
        for half in range(2):
            keep=(lane>=HD) if half else (lane<HD)
            qm=jnp.where(keep,qs,0.0).astype(BF); dom=jnp.where(keep,dof,0.0).astype(BF)
            lse=jnp.sum(jnp.where(head_id==2*pair+half,lse_ref[...],0.0),axis=1,keepdims=True)
            p=jnp.exp(dot_nt(qm,k)+bias_ref[...]-lse)
            dp=dot_nt(dom,v)
            inner=jnp.sum(p*dp,axis=1,keepdims=True)
            ds=(p*(dp-inner)).astype(BF)
            nq=dot(ds,k); nk=dot_tn(ds,qm); nv=dot_tn(p.astype(BF),dom)
            if half==0: gq,gk,gv=nq,nk,nv
            else:
                gq=jnp.where(keep,nq,gq); gk=gk+nk; gv=gv+nv
        gq=gq*(HD**-0.5/RQ); gk=gk*(1.0/RK); gv=gv*(1.0/RK)
        back([gq]*RQ,hq,dq,iq,aq,tq,pair)
        back([gk]*RK+[gv]*RK,hk,dk,ik,ak,tk,pair)
        return 0
    lax.fori_loop(first,last,step,0)
    for acc,tot,ref in ((aq,tq,gq_ref),(ak,tk,gk_ref)):
        count=acc.shape[0]
        for r in range(0,count,2):
            even=acc[r]; odd=acc[r+1]
            ref[:,r*HD:(r+2)*HD]=jnp.concatenate([even[:,:HD]+even[:,HD:],odd[:,:HD]+odd[:,HD:]],axis=1)
        ref[:,count*HD:]=tot[...]

def attn_bwd(pairs,base,q,k,v,do,lse,fq,fk,us,interpret=False):
    rows,keys=q.shape[0],k.shape[0]
    return pl.pallas_call(functools.partial(attn_bwd_body,*pairs),out_shape=(shape(fq.shape),shape(fk.shape)),
        in_specs=[SM]+[VM]*7,out_specs=(VM,)*2,
        scratch_shapes=attn_scratch(rows,keys)+[pltpu.VMEM((RQ,rows,128),F32),pltpu.VMEM((2*RK,keys,128),F32),pltpu.VMEM((rows,NQ),F32),pltpu.VMEM((keys,2*NK),F32)],
        compiler_params=limit(36),cost_estimate=cost(us),name="attn_bwd",interpret=interpret)(base,q,k,v,do,lse,fq,fk)

BK=256
def tri_cols(j): return (j*(j+1)//2)*BK

def store_sym(hi,lo,i,j,val):
    h,l=split2(val)
    hi[i*BK:(i+1)*BK,j*BK:(j+1)*BK]=h; lo[i*BK:(i+1)*BK,j*BK:(j+1)*BK]=l
    if i!=j:
        t=val.T
        h,l=split2(t)
        hi[j*BK:(j+1)*BK,i*BK:(i+1)*BK]=h; lo[j*BK:(j+1)*BK,i*BK:(i+1)*BK]=l

def mul_upper(xh,xl,yh,yl,n,emit):
    for j in reversed(range(n)):
        top=(j+1)*BK; cs=slice(j*BK,(j+1)*BK)
        r=dot(xh[:top,:],yh[:,cs])+dot(xh[:top,:],yl[:,cs])+dot(xl[:top,:],yh[:,cs])
        for i in range(j+1): emit(i,j,r[i*BK:(i+1)*BK])

def ns_body(g_ref,y_ref,o_ref,a_up,ah,al,ph,pw,bh,bl):
    n=o_ref.shape[1]//BK
    eye=(lax.broadcasted_iota(jnp.int32,(BK,BK),0)==lax.broadcasted_iota(jnp.int32,(BK,BK),1)).astype(F32)
    blk=lambda i,j:(slice(i*BK,(i+1)*BK),slice(j*BK,(j+1)*BK))
    trace=None
    for j in range(n):
        off=tri_cols(j)+j*BK
        part=g_ref[:,off:off+BK]*eye
        trace=part if trace is None else trace+part
    trace=jnp.sum(jnp.sum(trace,axis=1,keepdims=True),axis=0,keepdims=True)
    scale=1.0/(jnp.sqrt(trace)+1e-7)
    for j in range(n):
        for i in range(j+1):
            off=tri_cols(j)+i*BK
            val=g_ref[:,off:off+BK]*(scale*scale)
            a_up[blk(i,j)]=val; store_sym(ah,al,i,j,val)
    o_ref[...]=y_ref[...]*scale
    def poly():
        def emit(i,j,c):
            store_sym(ph,pw,i,j,COEF_B*a_up[blk(i,j)]+COEF_C*c)
        mul_upper(ah,al,ah,al,n,emit)
    def apply():
        y=o_ref[...]; yh,yl=split2(y)
        o_ref[...]=COEF_A*y+(dot(yh,ph[...])+dot(yh,pw[...])+dot(yl,ph[...]))
    def step(k,c):
        poly()
        def emit_b(i,j,m):
            val=COEF_A*a_up[blk(i,j)]+m
            a_up[blk(i,j)]=val; store_sym(bh,bl,i,j,val)
        mul_upper(ah,al,ph,pw,n,emit_b)
        apply()
        def emit_a(i,j,m):
            val=COEF_A*a_up[blk(i,j)]+m
            a_up[blk(i,j)]=val; store_sym(ah,al,i,j,val)
        mul_upper(bh,bl,ph,pw,n,emit_a)
        return c
    lax.fori_loop(0,NS_STEPS-1,step,0)
    poly(); apply()

def ns_big(gram,y,interpret=False):
    w,d=y.shape
    vm=pl.BlockSpec(memory_space=pltpu.VMEM)
    return pl.pallas_call(ns_body,out_shape=jax.ShapeDtypeStruct((w,d),F32),
        in_specs=[vm,vm],out_specs=vm,
        scratch_shapes=[pltpu.VMEM((d,d),F32)]+[pltpu.VMEM((d,d),BF)]*6,
        compiler_params=pltpu.CompilerParams(vmem_limit_bytes=40<<20),cost_estimate=cost(71),name="ns_gram",interpret=interpret)(gram,y)

def gram_body(y_ref,g_ref):
    n=y_ref.shape[1]//BK
    yh,yl=split2(y_ref[...])
    for j in range(n):
        top=(j+1)*BK; cs=slice(j*BK,top)
        r=dot_tn(yh[:,:top],yh[:,cs])+dot_tn(yh[:,:top],yl[:,cs])+dot_tn(yl[:,:top],yh[:,cs])
        for i in range(j+1):
            off=tri_cols(j)+i*BK
            g_ref[:,off:off+BK]=r[i*BK:(i+1)*BK]

def gram_upper(y,interpret=False):
    d=y.shape[1]; n=d//BK
    vm=pl.BlockSpec(memory_space=pltpu.VMEM)
    return pl.pallas_call(gram_body,out_shape=jax.ShapeDtypeStruct((BK,n*(n+1)//2*BK),F32),in_specs=[vm],out_specs=vm,
        compiler_params=pltpu.CompilerParams(vmem_limit_bytes=16<<20),cost_estimate=cost(3),name="gram_upper",interpret=interpret)(y)


def mm3(x,y,f=dot):
    xh,xl=split2(x); yh,yl=split2(y)
    return f(xh,yh)+f(xh,yl)+f(xl,yh)

def seg_mask(n,widths):
    def ids(axis):
        pos=lax.broadcasted_iota(jnp.int32,(n,n),axis); out=jnp.zeros_like(pos); edge=0
        for w in widths:
            edge+=w; out=out+(pos>=edge).astype(jnp.int32)
        return out
    return (ids(0)==ids(1)).astype(F32)

GROUPS=((0,(NQ,NK,NK)),(NQ+2*NK,(WQ,)),(NQ+2*NK+WQ,(WK,WK)))

def ns_factor_body(all_ref,own_ref,out_ref):
    out_ref[sum(GROUPS[-1][1])+GROUPS[-1][0]:,:]=jnp.zeros((out_ref.shape[0]-sum(GROUPS[-1][1])-GROUPS[-1][0],out_ref.shape[1]),F32)
    state=[]
    for start,widths in GROUPS:
        n=sum(widths); rs=slice(start,start+n)
        mask=seg_mask(n,widths)
        eye=(lax.broadcasted_iota(jnp.int32,(n,n),0)==lax.broadcasted_iota(jnp.int32,(n,n),1)).astype(F32)
        a=mask*sum(mm3(all_ref[d,rs,:],all_ref[d,rs,:],dot_nt) for d in range(all_ref.shape[0]))
        diag=a*eye
        row=jnp.sum(mask*jnp.sum(diag,axis=1,keepdims=True),axis=0,keepdims=True)
        col=jnp.sum(mask*jnp.sum(diag,axis=0,keepdims=True),axis=1,keepdims=True)
        row=1.0/(jnp.sqrt(row)+1e-7); col=1.0/(jnp.sqrt(col)+1e-7)
        state+=[a*row*col,own_ref[rs,:]*col]
    def step(_,c):
        out=[]
        for a,x in zip(c[::2],c[1::2]):
            p=COEF_B*a+COEF_C*mm3(a,a)
            x=COEF_A*x+mm3(p,x)
            b=COEF_A*a+mm3(a,p)
            out+=[COEF_A*b+mm3(b,p),x]
        return tuple(out)
    state=lax.fori_loop(0,NS_STEPS-1,step,tuple(state))
    for (start,widths),a,x in zip(GROUPS,state[::2],state[1::2]):
        out_ref[start:start+sum(widths),:]=COEF_A*x+mm3(COEF_B*a+COEF_C*mm3(a,a),x)

def ns_factor(tiles,own,interpret=False):
    return pl.pallas_call(ns_factor_body,out_shape=shape(own.shape),in_specs=[VM]*2,out_specs=VM,
        compiler_params=limit(28),cost_estimate=cost(22),name="ns_factor",interpret=interpret)(tiles,own)

def ffn_body(x_ref,g_ref,w_ref,second_ref,branch_ref,hid_ref,dg_ref,du_ref):
    x=x_ref[...]
    gate=dot_nt(x,w_ref[0]); up=dot_nt(x,w_ref[1]); dh=dot_nt(g_ref[...],w_ref[2])
    sig=1.0/(1.0+jnp.exp(-gate))
    act=gate*sig
    hid=(act*up).astype(BF)
    dg=(dh*up*sig*(1.0+gate*(1.0-sig))).astype(BF)
    du=(dh*act).astype(BF)
    hid_ref[...]=hid; dg_ref[...]=dg; du_ref[...]=du
    second_ref[...]=(dot(dg,w_ref[0])+dot(du,w_ref[1])).astype(BF)
    branch_ref[...]=dot(hid,w_ref[2]).astype(BF)

def in_hbm(x): return pltpu.with_memory_space_constraint(x,pltpu.HBM)

def ffn_tokens(x_all,g_all,w,interpret=False):
    tokens=x_all.shape[0]; rows=256; hid=w.shape[1]
    block=pl.BlockSpec((rows,D),lambda i:(i,0)); part=pl.BlockSpec((rows,hid),lambda i:(i,0))
    return pl.pallas_call(ffn_body,out_shape=(pltpu.HBM((tokens,D),BF),)*2+(pltpu.HBM((tokens,hid),BF),)*3,
        grid=(tokens//rows,),in_specs=[block,block,pl.BlockSpec(w.shape,lambda i:(0,0,0),pipeline_mode=pl.Buffered(1))],
        out_specs=(block,block,part,part,part),
        compiler_params=limit(20),cost_estimate=cost(20),name="ffn_tokens",interpret=interpret)(in_hbm(x_all),in_hbm(g_all),w)

def ffn_grads_body(steps,hid_ref,dg_ref,du_ref,x_ref,g_ref,grad_ref,*total):
    width=hid_ref.shape[1]
    for c,(left,right) in enumerate(((dg_ref,x_ref),(du_ref,x_ref),(hid_ref,g_ref))):
        here=slice(c*width,(c+1)*width)
        part=dot_tn(left[...],right[...])
        if steps>1:
            part=jnp.where(pl.program_id(0)==0,part,part+total[0][c])
            total[0][c]=part
        grad_ref[here,:]=part.astype(BF)
    grad_ref[3*width:,:]=jnp.zeros((grad_ref.shape[0]-3*width,D),BF)

def ffn_grads(saved,x_all,g_all,n_dp,interpret=False):
    tokens,hid=saved[0].shape; rows=min(tokens,2048); steps=tokens//rows
    block=pl.BlockSpec((rows,D),lambda i:(i,0)); part=pl.BlockSpec((rows,hid),lambda i:(i,0))
    out=(n_dp*hid,D)
    return pl.pallas_call(functools.partial(ffn_grads_body,steps),out_shape=shape(out,BF),grid=(steps,),
        in_specs=[part]*3+[block]*2,out_specs=pl.BlockSpec(out,lambda i:(0,0)),
        scratch_shapes=[] if steps==1 else [pltpu.VMEM((3,hid,D),F32)],
        compiler_params=limit(40),cost_estimate=cost(10),name="ffn_grads",interpret=interpret)(*saved,x_all,g_all)


EPS = 1e-06
MOMENTUM = 0.5
LEARN = 0.2
LEARN_VEC = 0.002
P = jax.sharding.PartitionSpec
FFN = 3


def normalize(values):
    row_scale = lax.rsqrt(jnp.mean(values * values, axis=-1, keepdims=True) + EPS)
    return values * row_scale, row_scale


def norm_back(grad_in, normed, row_scale, gain):
    scaled = grad_in * gain
    inner_sum = jnp.mean(scaled * normed, axis=-1, keepdims=True)
    return row_scale * (scaled - normed * inner_sum), jnp.sum(grad_in * normed, axis=0)


def dp_pairs(shift, keep=lambda target: True):
    return [(j, j ^ shift) for j in range(lax.axis_size("dp")) if keep(j ^ shift)]


def place(parts, axis, me=None):
    me = lax.axis_index("dp") if me is None else me
    step = parts[0].shape[axis]
    shape = list(parts[0].shape)
    shape[axis] *= len(parts)
    out = jnp.zeros(shape, parts[0].dtype)
    for shift, part in enumerate(parts):
        out = lax.dynamic_update_slice_in_dim(out, part, (me ^ shift) * step, axis)
    return out


def gather_dp(own, axis=0):
    return place([own] + [lax.ppermute(own, "dp", dp_pairs(s)) for s in range(1, lax.axis_size("dp"))], axis)


def sum_dp(block_for, during=None, alongside=(), gate=None):
    me = lax.axis_index("dp")
    sent = [block_for(me ^ s).astype(BF) for s in range(1, lax.axis_size("dp"))]
    if gate is not None:
        sent = [after(block, gate) for block in sent]
    total = block_for(me)
    aside = None
    if during is not None:
        aside = during(*sent)
        total = after(total, *aside, *alongside)
    for s, block in enumerate(sent, 1):
        total = total + lax.ppermute(block, "dp", dp_pairs(s)).astype(F32)
    return total if during is None else (total, aside)


def after(value, *others):
    return lax.optimization_barrier((value, *others))[0]


def pass_core(x):
    return lax.ppermute(x, "mp", [(j, j ^ 1) for j in range(lax.axis_size("mp"))])


def pass_chip(x, shift):
    return lax.ppermute(x, "mp", [(j, j ^ (2 * shift)) for j in range(lax.axis_size("mp"))])


def pick(x, index):
    return lax.dynamic_index_in_dim(x, index, 0, keepdims=False)


CHIPS = 4


def cross_chips(near):
    if len(near) == 1:
        return [lax.psum_scatter(near[0], "mp", scatter_dimension=0, tiled=True)]
    return [near[0]] + [pass_chip(near[s].astype(BF), s) for s in range(1, len(near))]


def collect(near):
    return sum(part.astype(F32) for part in cross_chips(near))


def core_half(partial, axis):
    core = lax.axis_index("mp") % 2
    away = lax.dynamic_index_in_dim(partial, 1 - core, axis, keepdims=False).astype(BF)
    return lax.dynamic_index_in_dim(partial, core, axis, keepdims=False) + pass_core(away).astype(F32)


def chip_sums(partial):
    if lax.axis_size("mp") != 2 * CHIPS:
        return [partial]
    near = core_half(partial.reshape(CHIPS, 2, -1, partial.shape[1]), 1)
    near = [pick(near, (lax.axis_index("mp") // 2) ^ s) for s in range(CHIPS)]
    return [near[0]] + [part.astype(BF) for part in near[1:]]


def body(
    tokens,
    cotangent,
    domain_ids,
    domain_weight,
    gains,
    gain_mom,
    factor_w,
    factor_mom,
    out_w,
    out_mom,
    gate_up_w,
    gate_up_mom,
    down_w,
    down_mom,
):
    n_dp, n_mp = lax.axis_size("dp"), lax.axis_size("mp")
    me, mz = lax.axis_index("dp"), lax.axis_index("mp")
    rows = tokens.shape[0]
    d_own = factor_w.shape[0]
    hidden_own = gate_up_w.shape[2]
    out_own = d_own // n_mp
    base = me.astype(jnp.int32).reshape(1)
    shifts = range(1, n_dp)

    edge = NQ + 2 * NK

    def q_rows(m):
        return jnp.concatenate([m[edge : edge + WQ], m[:NQ]])

    def kv_rows(m):
        return jnp.concatenate([m[edge + WQ :], m[NQ:edge]])

    factor_own = factor_w.T.astype(BF)
    kv_low = gather_dp(kv_rows(factor_own), 1)
    x_float = tokens.astype(F32)
    first_normed, first_scale = normalize(x_float)
    first_own = (first_normed * gains[0]).astype(BF)
    domain_range = jnp.arange(domain_weight.shape[0], dtype=jnp.int32)
    seq_weight = jnp.sum(jnp.where(domain_ids[0, 0] == domain_range, domain_weight, 0.0))
    d_output = cotangent.astype(F32) * seq_weight
    d_output_all = lax.all_gather(d_output.astype(BF), "mp", axis=0, tiled=True)
    kv_all = gather_dp(dot_nt(first_own, kv_low))
    q_low = gather_dp(q_rows(factor_own), 1)
    q_own = dot_nt(first_own, q_low)
    attended, lse, queries, key_vecs, values = attn_fwd(base, q_own, kv_all)
    out_low = gather_dp(after(out_w.astype(BF), kv_all))
    residual = x_float + dot(attended, out_low)
    second_normed, second_scale = normalize(residual)

    ffn_own = jnp.stack([gate_up_w[0].T, gate_up_w[1].T, down_w])
    ffn_low = gather_dp(after(ffn_own.astype(BF), out_low), 2)
    second_own = (second_normed * gains[1]).astype(BF)
    to_ffn = lambda target: target < FFN
    ffn_slot = jnp.minimum(me, FFN - 1)
    ffn_mom = after(jnp.stack([gate_up_mom[0].T, gate_up_mom[1].T, down_mom]), ffn_low)
    own_mom = [pick(ffn_mom, ffn_slot)]
    for s in shifts:
        own_mom.append(lax.ppermute(pick(ffn_mom, jnp.minimum(me ^ s, FFN - 1)), "dp", dp_pairs(s, to_ffn)))
    second_in = lax.all_gather(second_own, "mp", axis=0, tiled=True)
    d_second, branch, *saved = ffn_tokens(second_in, d_output_all, after(ffn_low, *own_mom[1:]))
    d_second = lax.psum_scatter(d_second, "mp", scatter_dimension=0, tiled=True).astype(F32)
    grads = ffn_grads(saved, second_in, d_output_all, n_dp)
    branch = chip_sums(branch)
    d_second = after(d_second, grads, *branch)
    own_mom = MOMENTUM * place(own_mom, 1)
    matrix = lax.psum_scatter(grads, "dp", scatter_dimension=0, tiled=True)

    d_resid_norm, gain_second = norm_back(d_second, second_normed, second_scale, gains[1])
    d_residual = d_output + d_resid_norm
    d_residual_low = d_residual.astype(BF)
    d_attended = dot_nt(d_residual_low, out_low).astype(BF)

    def backward(pairs, us, *gates):
        return attn_bwd(pairs, after(base, *gates), queries, key_vecs, values, d_attended, lse, q_own, kv_all, us)

    grad_out = dot_tn(attended, d_residual_low)
    if n_mp == 2 * CHIPS:
        grad_out = core_half(grad_out.reshape(n_dp, CHIPS, 2, out_own, D), 2)
    grad_out = grad_out.reshape(n_dp, -1, D)
    last, branch = branch[3:], cross_chips([after(part, d_second) for part in branch[:3]])
    grad_out, (d_q, d_kv) = sum_dp(
        lambda t: pick(grad_out, t), during=functools.partial(backward, (0, HEADS // 2), 26), alongside=branch[1:]
    )
    d_q, d_kv = after((d_q, d_kv), grad_out)
    if n_mp == 2 * CHIPS:
        grad_out = grad_out.reshape(CHIPS, out_own, D)
        near = [pick(grad_out, (mz // 2) ^ s) for s in range(CHIPS)]
        near = near[:1] + [part.astype(BF) for part in near[1:]]
        grad_out = collect(near)
    else:
        grad_out = lax.psum_scatter(grad_out, "mp", scatter_dimension=0, tiled=True)
    out_tile = MOMENTUM * lax.dynamic_slice_in_dim(out_mom, mz * out_own, out_own, 0) + grad_out
    out_tile = after(out_tile, matrix)
    out_rows = place([out_tile] + [lax.ppermute(out_tile, "dp", [(j ^ s, j) for j in range(FFN, n_dp)]) for s in shifts], 0)
    out_rows = jnp.pad(out_rows, ((0, hidden_own - out_rows.shape[0]), (0, 0)))
    matrix = jnp.where(me < FFN, own_mom + matrix.astype(F32), out_rows)
    gram_part = gram_upper(matrix)
    gram = lax.psum(gram_part, "mp")

    d_kv = sum_dp(lambda t: lax.dynamic_slice_in_dim(d_kv, t * rows, rows, 0))
    d_q, d_kv = d_q.astype(BF), d_kv.astype(BF)
    d_first = dot(d_q, q_low) + dot(d_kv, kv_low)
    d_input_norm, gain_first = norm_back(d_first, first_normed, first_scale, gains[0])
    input_grad = d_residual + d_input_norm

    gain_rows = jnp.stack([gain_first, gain_second])
    filler = -(factor_w.shape[1] + 2) % (8 * n_mp)

    d_all = jnp.concatenate([d_q[:, WQ:], d_kv[:, 2 * WK :], d_q[:, :WQ], d_kv[:, : 2 * WK]], axis=1)
    grad_factor = jnp.concatenate([dot_tn(d_all, first_own), jnp.pad(gain_rows, ((0, filler), (0, 0)))])
    height = grad_factor.shape[0] // n_mp
    if n_mp == 2 * CHIPS:
        grad_factor = core_half(grad_factor.reshape(CHIPS, 2, height, D), 1).reshape(CHIPS * height, D)
    grad_factor = sum_dp(lambda t: lax.dynamic_slice_in_dim(grad_factor, t * d_own, d_own, 1))
    dp_summed = grad_factor
    if n_mp == 2 * CHIPS:
        grad_factor = grad_factor.reshape(CHIPS, height, d_own)
        grad_factor = collect([pick(grad_factor, (mz // 2) ^ s) for s in range(CHIPS)])
    else:
        grad_factor = lax.psum_scatter(grad_factor, "mp", scatter_dimension=0, tiled=True)
    factor_piece = jnp.pad(MOMENTUM * factor_mom.T, ((0, filler + 2), (0, 0)))
    factor_piece = lax.dynamic_slice_in_dim(factor_piece, mz * height, height, 0) + grad_factor
    factor_all = lax.all_gather(factor_piece, ("dp", "mp"), axis=0, tiled=True).reshape(n_dp, n_mp * height, d_own)
    factor_tile = pick(factor_all, me)
    gain_grad = factor_tile[factor_w.shape[1] : factor_w.shape[1] + 2]

    def give_back(whole):
        pieces = [lax.dynamic_slice_in_dim(whole, (me ^ s) * d_own, d_own, 1) for s in range(n_dp)]
        came = [lax.ppermute(pieces[s], "dp", dp_pairs(s, lambda t: t ^ s < FFN))[None] for s in shifts]
        return place([pieces[0][None]] + came, 0), pieces[1:], came

    mom_back, _, came = give_back(after(matrix, dp_summed))
    ortho = ns_big(gram, after(matrix, factor_piece, *came))
    ortho = after(ortho, factor_all)
    branch += [pass_chip(after(part, gram), 3) for part in last]
    ortho = after(ortho, *branch[3:])
    block_out = (residual + sum(part.astype(F32) for part in branch)).astype(BF)
    out_ortho = lax.dynamic_slice_in_dim(ortho, me * out_own, out_own, 0)
    for s in shifts:
        piece = lax.dynamic_slice_in_dim(ortho, (me ^ s) * out_own, out_own, 0)
        piece = lax.ppermute(piece, "dp", [(j, j ^ s) for j in range(FFN, n_dp)])
        out_ortho = jnp.where(me ^ s == FFN, piece, out_ortho)
    out_pair = after(jnp.stack([out_tile, out_ortho]), factor_all)
    out_both = lax.all_gather(out_pair, "mp", axis=1, tiled=True)
    new_out_mom = out_both[0]
    new_out_w = out_w - LEARN * 0.2 * math.sqrt(D) * out_both[1]
    ortho_back, sent, _ = give_back(after(ortho, out_ortho))
    factor_ortho = ns_factor(factor_all, after(factor_tile, out_pair, *sent))
    ortho_back = after(ortho_back, factor_ortho)
    turn = lambda stack: jnp.stack([stack[0].T, stack[1].T])
    ffn_rate = LEARN * 0.2 * math.sqrt(max(D, hidden_own * n_mp))
    new_gate_up_mom, new_down_mom = turn(mom_back), mom_back[2]
    new_gate_up_w = gate_up_w - ffn_rate * turn(ortho_back)
    new_down_w = down_w - ffn_rate * ortho_back[2]
    widths = [NQ, NK, NK, WQ, WK, WK]
    factor_rate = jnp.concatenate([jnp.full((w, 1), LEARN * 0.2 * math.sqrt(max(D, w)), F32) for w in widths])
    new_factor_mom = factor_tile[: factor_w.shape[1]].T
    new_factor_w = factor_w - (factor_rate * factor_ortho[: factor_w.shape[1]]).T

    new_gain_mom = MOMENTUM * gain_mom + gain_grad
    new_gains = lax.dynamic_slice_in_dim(gains, me * d_own, d_own, 1) - LEARN_VEC * new_gain_mom
    return (
        block_out,
        input_grad,
        gain_grad,
        new_gains,
        new_gain_mom,
        new_factor_mom,
        new_factor_w,
        new_out_mom,
        new_out_w,
        new_gate_up_mom,
        new_gate_up_w,
        new_down_mom,
        new_down_w,
    )


def solution(mesh):
    token = P(("mp", "dp"), None)
    row = P("dp", None)
    ffn = P(None, "dp", "mp")
    down = P("mp", "dp")
    vec = P(None, "dp")
    return jax.shard_map(
        body,
        mesh=mesh,
        in_specs=(token, token, P("mp", None), P(), P(), vec, row, row, row, row, ffn, ffn, down, down),
        out_specs=(token, token, vec, vec, vec, row, row, row, row, ffn, ffn, down, down),
        check_vma=False,
    )
```

```python
import functools
import math
import jax
import jax.numpy as jnp
from jax import lax
from jax.experimental import pallas as pl
from jax.experimental.pallas import tpu as pltpu
BF=jnp.bfloat16; F32=jnp.float32
HEADS=16; HD=64; RQ=6; RK=2; D=1024
COEF_A=3.4445; COEF_B=-4.775; COEF_C=2.0315
NEG=-1e30
NS_STEPS=5

def split2(x):
    hi=x.astype(BF); return hi,(x-hi.astype(F32)).astype(BF)
def dot(a,b): return jnp.dot(a,b,preferred_element_type=F32)
def dot_nt(a,b): return lax.dot_general(a,b,(((1,),(1,)),((),())),preferred_element_type=F32)
def dot_tn(a,b): return lax.dot_general(a,b,(((0,),(0,)),((),())),preferred_element_type=F32)

def index_map(ref, heads):
    row=lax.broadcasted_iota(jnp.int32,ref.shape,0); col=lax.broadcasted_iota(jnp.int32,ref.shape,1)
    row=jnp.where(row>=heads,row-heads,row)
    ref[...]=row-HEADS*lax.shift_right_logical(col,7)-(lax.bitwise_and(col,127)>=HD).astype(jnp.int32)

def one_hot(ref, pair): return jnp.where(ref[...]==2*pair,1.0,0.0).astype(BF)

def twice(dims,r,scale):
    part=dims[:,r*HD:(r+1)*HD]*scale
    return jnp.concatenate([part,part],axis=1)

WQ,WK=RQ*HD,RK*HD
NQ,NK=RQ*HEADS,RK*HEADS

def attn_setup(base_ref,fq_ref,fk_ref,bias_ref,hq,hk,dq,dk,iq,ik,scaled):
    rows,keys=bias_ref.shape
    r_id=lax.broadcasted_iota(jnp.int32,(rows,keys),0)+base_ref[0]*rows
    c_id=lax.broadcasted_iota(jnp.int32,(rows,keys),1)
    bias_ref[...]=jnp.where(c_id<=r_id,0.0,NEG)
    hq[...]=jnp.concatenate(split2(fq_ref[:,WQ:]),axis=1); hk[...]=jnp.concatenate(split2(fk_ref[:,2*WK:]),axis=1)
    for r in range(RQ): dq[r]=twice(fq_ref,r,1.0/RQ if scaled else 1.0)
    for r in range(2*RK): dk[r]=twice(fk_ref,r,1.0/RK if scaled else 1.0)
    index_map(iq,NQ); index_map(ik,2*NK)

def attn_scratch(rows,keys):
    return [pltpu.VMEM((rows,keys),F32),pltpu.VMEM((rows,2*NQ),BF),pltpu.VMEM((keys,4*NK),BF),pltpu.VMEM((RQ,rows,128),F32),pltpu.VMEM((2*RK,keys,128),F32),
        pltpu.VMEM((2*NQ,RQ*128),jnp.int32),pltpu.VMEM((4*NK,2*RK*128),jnp.int32)]

def lanes(x,r): return x[:,r*128:(r+1)*128]

def attn_fwd_body(base_ref,fq_ref,fk_ref,o_ref,lse_ref,q_ref,k_ref,v_ref,bias_ref,hq,hk,dq,dk,iq,ik):
    attn_setup(base_ref,fq_ref,fk_ref,bias_ref,hq,hk,dq,dk,iq,ik,True)
    lane=lax.broadcasted_iota(jnp.int32,(1,128),1)
    head_id=lax.broadcasted_iota(jnp.int32,(1,HEADS),1)
    lse_ref[...]=jnp.zeros_like(lse_ref)
    def step(pair,_):
        cols=pl.ds(pl.multiple_of(pair*128,128),128)
        wide_q=dot(hq[...],one_hot(iq,pair)); wide_k=dot(hk[...],one_hot(ik,pair))
        q=sum(lanes(wide_q,r)*dq[r] for r in range(RQ)).astype(BF)
        k=sum(lanes(wide_k,r)*dk[r] for r in range(RK)).astype(BF)
        v=sum(lanes(wide_k,r)*dk[r] for r in range(RK,2*RK)).astype(BF)
        q_ref[:,cols]=q; k_ref[:,cols]=k; v_ref[:,cols]=v
        qs=q.astype(F32)*(HD**-0.5)
        out=None
        for half in range(2):
            keep=(lane>=HD) if half else (lane<HD)
            qm=jnp.where(keep,qs,0.0).astype(BF)
            s=dot_nt(qm,k)+bias_ref[...]
            m=jnp.max(s,axis=1,keepdims=True)
            e=jnp.exp(s-m)
            l=jnp.sum(e,axis=1,keepdims=True)
            p=(e*(1.0/l)).astype(BF)
            o=dot(p,v)
            out=jnp.where(keep,o,out) if half else o
            lse_ref[...]=jnp.where(head_id==2*pair+half,m+jnp.log(l),lse_ref[...])
        o_ref[:,cols]=out.astype(BF)
        return 0
    lax.fori_loop(0,HEADS//2,step,0)

VM=pl.BlockSpec(memory_space=pltpu.VMEM)
SM=pl.BlockSpec(memory_space=pltpu.SMEM)
def shape(dims,dtype=F32): return jax.ShapeDtypeStruct(dims,dtype)
def cost(us): return pl.CostEstimate(flops=int(us*1.15e9),transcendentals=0,bytes_accessed=1<<20)
def limit(mib): return pltpu.CompilerParams(vmem_limit_bytes=mib<<20)

def attn_fwd(base,fq,fk,interpret=False):
    rows,keys=fq.shape[0],fk.shape[0]
    return pl.pallas_call(attn_fwd_body,
        out_shape=(shape((rows,D),BF),shape((rows,HEADS)),shape((rows,D),BF),shape((keys,D),BF),shape((keys,D),BF)),
        in_specs=[SM,VM,VM],out_specs=(VM,)*5,scratch_shapes=attn_scratch(rows,keys),
        compiler_params=limit(28),cost_estimate=cost(16),name="attn_fwd",interpret=interpret)(base,fq,fk)

def attn_bwd_body(first,last,base_ref,q_ref,k_ref,v_ref,do_ref,lse_ref,fq_ref,fk_ref,gq_ref,gk_ref,bias_ref,hq,hk,dq,dk,iq,ik,aq,ak,tq,tk):
    attn_setup(base_ref,fq_ref,fk_ref,bias_ref,hq,hk,dq,dk,iq,ik,False)
    for ref in (aq,ak,tq,tk): ref[...]=jnp.zeros_like(ref)
    lane=lax.broadcasted_iota(jnp.int32,(1,128),1)
    head_id=lax.broadcasted_iota(jnp.int32,(1,HEADS),1)
    def back(grads,h,d,index,acc,tot,pair):
        e=one_hot(index,pair)
        wide=dot(h[...],e)
        for r,grad in enumerate(grads): acc[r]+=grad*lanes(wide,r)
        terms=jnp.concatenate([(grad*d[r]).astype(BF) for r,grad in enumerate(grads)],axis=1)
        tot[...]+=dot_nt(terms,e[:tot.shape[1]])
    def step(pair,_):
        cols=pl.ds(pl.multiple_of(pair*128,128),128)
        q=q_ref[:,cols]; k=k_ref[:,cols]; v=v_ref[:,cols]; do=do_ref[:,cols]
        qs=q.astype(F32)*(HD**-0.5); dof=do.astype(F32)
        gq=gk=gv=None
        for half in range(2):
            keep=(lane>=HD) if half else (lane<HD)
            qm=jnp.where(keep,qs,0.0).astype(BF); dom=jnp.where(keep,dof,0.0).astype(BF)
            lse=jnp.sum(jnp.where(head_id==2*pair+half,lse_ref[...],0.0),axis=1,keepdims=True)
            p=jnp.exp(dot_nt(qm,k)+bias_ref[...]-lse)
            dp=dot_nt(dom,v)
            inner=jnp.sum(p*dp,axis=1,keepdims=True)
            ds=(p*(dp-inner)).astype(BF)
            nq=dot(ds,k); nk=dot_tn(ds,qm); nv=dot_tn(p.astype(BF),dom)
            if half==0: gq,gk,gv=nq,nk,nv
            else:
                gq=jnp.where(keep,nq,gq); gk=gk+nk; gv=gv+nv
        gq=gq*(HD**-0.5/RQ); gk=gk*(1.0/RK); gv=gv*(1.0/RK)
        back([gq]*RQ,hq,dq,iq,aq,tq,pair)
        back([gk]*RK+[gv]*RK,hk,dk,ik,ak,tk,pair)
        return 0
    lax.fori_loop(first,last,step,0)
    for acc,tot,ref in ((aq,tq,gq_ref),(ak,tk,gk_ref)):
        count=acc.shape[0]
        for r in range(0,count,2):
            even=acc[r]; odd=acc[r+1]
            ref[:,r*HD:(r+2)*HD]=jnp.concatenate([even[:,:HD]+even[:,HD:],odd[:,:HD]+odd[:,HD:]],axis=1)
        ref[:,count*HD:]=tot[...]

def attn_bwd(pairs,base,q,k,v,do,lse,fq,fk,us,interpret=False):
    rows,keys=q.shape[0],k.shape[0]
    return pl.pallas_call(functools.partial(attn_bwd_body,*pairs),out_shape=(shape(fq.shape),shape(fk.shape)),
        in_specs=[SM]+[VM]*7,out_specs=(VM,)*2,
        scratch_shapes=attn_scratch(rows,keys)+[pltpu.VMEM((RQ,rows,128),F32),pltpu.VMEM((2*RK,keys,128),F32),pltpu.VMEM((rows,NQ),F32),pltpu.VMEM((keys,2*NK),F32)],
        compiler_params=limit(36),cost_estimate=cost(us),name="attn_bwd",interpret=interpret)(base,q,k,v,do,lse,fq,fk)

BK=256
def tri_cols(j): return (j*(j+1)//2)*BK

def store_sym(hi,lo,i,j,val):
    h,l=split2(val)
    hi[i*BK:(i+1)*BK,j*BK:(j+1)*BK]=h; lo[i*BK:(i+1)*BK,j*BK:(j+1)*BK]=l
    if i!=j:
        t=val.T
        h,l=split2(t)
        hi[j*BK:(j+1)*BK,i*BK:(i+1)*BK]=h; lo[j*BK:(j+1)*BK,i*BK:(i+1)*BK]=l

def mul_upper(xh,xl,yh,yl,n,emit):
    for j in reversed(range(n)):
        top=(j+1)*BK; cs=slice(j*BK,(j+1)*BK)
        r=dot(xh[:top,:],yh[:,cs])+dot(xh[:top,:],yl[:,cs])+dot(xl[:top,:],yh[:,cs])
        for i in range(j+1): emit(i,j,r[i*BK:(i+1)*BK])

def ns_body(g_ref,y_ref,o_ref,a_up,ah,al,ph,pw,bh,bl):
    n=o_ref.shape[1]//BK
    eye=(lax.broadcasted_iota(jnp.int32,(BK,BK),0)==lax.broadcasted_iota(jnp.int32,(BK,BK),1)).astype(F32)
    blk=lambda i,j:(slice(i*BK,(i+1)*BK),slice(j*BK,(j+1)*BK))
    trace=None
    for j in range(n):
        off=tri_cols(j)+j*BK
        part=g_ref[:,off:off+BK]*eye
        trace=part if trace is None else trace+part
    trace=jnp.sum(jnp.sum(trace,axis=1,keepdims=True),axis=0,keepdims=True)
    scale=1.0/(jnp.sqrt(trace)+1e-7)
    for j in range(n):
        for i in range(j+1):
            off=tri_cols(j)+i*BK
            val=g_ref[:,off:off+BK]*(scale*scale)
            a_up[blk(i,j)]=val; store_sym(ah,al,i,j,val)
    o_ref[...]=y_ref[...]*scale
    def poly():
        def emit(i,j,c):
            store_sym(ph,pw,i,j,COEF_B*a_up[blk(i,j)]+COEF_C*c)
        mul_upper(ah,al,ah,al,n,emit)
    def apply():
        y=o_ref[...]; yh,yl=split2(y)
        o_ref[...]=COEF_A*y+(dot(yh,ph[...])+dot(yh,pw[...])+dot(yl,ph[...]))
    def step(k,c):
        poly()
        def emit_b(i,j,m):
            val=COEF_A*a_up[blk(i,j)]+m
            a_up[blk(i,j)]=val; store_sym(bh,bl,i,j,val)
        mul_upper(ah,al,ph,pw,n,emit_b)
        apply()
        def emit_a(i,j,m):
            val=COEF_A*a_up[blk(i,j)]+m
            a_up[blk(i,j)]=val; store_sym(ah,al,i,j,val)
        mul_upper(bh,bl,ph,pw,n,emit_a)
        return c
    lax.fori_loop(0,NS_STEPS-1,step,0)
    poly(); apply()

def ns_big(gram,y,interpret=False):
    w,d=y.shape
    vm=pl.BlockSpec(memory_space=pltpu.VMEM)
    return pl.pallas_call(ns_body,out_shape=jax.ShapeDtypeStruct((w,d),F32),
        in_specs=[vm,vm],out_specs=vm,
        scratch_shapes=[pltpu.VMEM((d,d),F32)]+[pltpu.VMEM((d,d),BF)]*6,
        compiler_params=pltpu.CompilerParams(vmem_limit_bytes=40<<20),cost_estimate=cost(71),name="ns_gram",interpret=interpret)(gram,y)

def gram_body(y_ref,g_ref):
    n=y_ref.shape[1]//BK
    yh,yl=split2(y_ref[...])
    for j in range(n):
        top=(j+1)*BK; cs=slice(j*BK,top)
        r=dot_tn(yh[:,:top],yh[:,cs])+dot_tn(yh[:,:top],yl[:,cs])+dot_tn(yl[:,:top],yh[:,cs])
        for i in range(j+1):
            off=tri_cols(j)+i*BK
            g_ref[:,off:off+BK]=r[i*BK:(i+1)*BK]

def gram_upper(y,interpret=False):
    d=y.shape[1]; n=d//BK
    vm=pl.BlockSpec(memory_space=pltpu.VMEM)
    return pl.pallas_call(gram_body,out_shape=jax.ShapeDtypeStruct((BK,n*(n+1)//2*BK),F32),in_specs=[vm],out_specs=vm,
        compiler_params=pltpu.CompilerParams(vmem_limit_bytes=16<<20),cost_estimate=cost(3),name="gram_upper",interpret=interpret)(y)


def mm3(x,y,f=dot):
    xh,xl=split2(x); yh,yl=split2(y)
    return f(xh,yh)+f(xh,yl)+f(xl,yh)

def seg_mask(n,widths):
    def ids(axis):
        pos=lax.broadcasted_iota(jnp.int32,(n,n),axis); out=jnp.zeros_like(pos); edge=0
        for w in widths:
            edge+=w; out=out+(pos>=edge).astype(jnp.int32)
        return out
    return (ids(0)==ids(1)).astype(F32)

GROUPS=((0,(NQ,NK,NK)),(NQ+2*NK,(WQ,)),(NQ+2*NK+WQ,(WK,WK)))

def ns_factor_body(all_ref,own_ref,out_ref):
    out_ref[sum(GROUPS[-1][1])+GROUPS[-1][0]:,:]=jnp.zeros((out_ref.shape[0]-sum(GROUPS[-1][1])-GROUPS[-1][0],out_ref.shape[1]),F32)
    state=[]
    for start,widths in GROUPS:
        n=sum(widths); rs=slice(start,start+n)
        mask=seg_mask(n,widths)
        eye=(lax.broadcasted_iota(jnp.int32,(n,n),0)==lax.broadcasted_iota(jnp.int32,(n,n),1)).astype(F32)
        a=mask*sum(mm3(all_ref[d,rs,:],all_ref[d,rs,:],dot_nt) for d in range(all_ref.shape[0]))
        diag=a*eye
        row=jnp.sum(mask*jnp.sum(diag,axis=1,keepdims=True),axis=0,keepdims=True)
        col=jnp.sum(mask*jnp.sum(diag,axis=0,keepdims=True),axis=1,keepdims=True)
        row=1.0/(jnp.sqrt(row)+1e-7); col=1.0/(jnp.sqrt(col)+1e-7)
        state+=[a*row*col,own_ref[rs,:]*col]
    def step(_,c):
        out=[]
        for a,x in zip(c[::2],c[1::2]):
            p=COEF_B*a+COEF_C*mm3(a,a)
            x=COEF_A*x+mm3(p,x)
            b=COEF_A*a+mm3(a,p)
            out+=[COEF_A*b+mm3(b,p),x]
        return tuple(out)
    state=lax.fori_loop(0,NS_STEPS-1,step,tuple(state))
    for (start,widths),a,x in zip(GROUPS,state[::2],state[1::2]):
        out_ref[start:start+sum(widths),:]=COEF_A*x+mm3(COEF_B*a+COEF_C*mm3(a,a),x)

def ns_factor(tiles,own,interpret=False):
    return pl.pallas_call(ns_factor_body,out_shape=shape(own.shape),in_specs=[VM]*2,out_specs=VM,
        compiler_params=limit(28),cost_estimate=cost(22),name="ns_factor",interpret=interpret)(tiles,own)

def ffn_body(x_ref,g_ref,w_ref,second_ref,branch_ref,hid_ref,dg_ref,du_ref):
    x=x_ref[...]
    gate=dot_nt(x,w_ref[0]); up=dot_nt(x,w_ref[1]); dh=dot_nt(g_ref[...],w_ref[2])
    sig=1.0/(1.0+jnp.exp(-gate))
    act=gate*sig
    hid=(act*up).astype(BF)
    dg=(dh*up*sig*(1.0+gate*(1.0-sig))).astype(BF)
    du=(dh*act).astype(BF)
    hid_ref[...]=hid; dg_ref[...]=dg; du_ref[...]=du
    second_ref[...]=(dot(dg,w_ref[0])+dot(du,w_ref[1])).astype(BF)
    branch_ref[...]=dot(hid,w_ref[2]).astype(BF)

def in_hbm(x): return pltpu.with_memory_space_constraint(x,pltpu.HBM)

def ffn_tokens(x_all,g_all,w,interpret=False):
    tokens=x_all.shape[0]; rows=256; hid=w.shape[1]
    block=pl.BlockSpec((rows,D),lambda i:(i,0)); part=pl.BlockSpec((rows,hid),lambda i:(i,0))
    return pl.pallas_call(ffn_body,out_shape=(pltpu.HBM((tokens,D),BF),)*2+(pltpu.HBM((tokens,hid),BF),)*3,
        grid=(tokens//rows,),in_specs=[block,block,pl.BlockSpec(w.shape,lambda i:(0,0,0),pipeline_mode=pl.Buffered(1))],
        out_specs=(block,block,part,part,part),
        compiler_params=limit(20),cost_estimate=cost(20),name="ffn_tokens",interpret=interpret)(in_hbm(x_all),in_hbm(g_all),w)

def ffn_grads_body(steps,hid_ref,dg_ref,du_ref,x_ref,g_ref,grad_ref,*total):
    width=hid_ref.shape[1]
    for c,(left,right) in enumerate(((dg_ref,x_ref),(du_ref,x_ref),(hid_ref,g_ref))):
        here=slice(c*width,(c+1)*width)
        part=dot_tn(left[...],right[...])
        if steps>1:
            part=jnp.where(pl.program_id(0)==0,part,part+total[0][c])
            total[0][c]=part
        grad_ref[here,:]=part.astype(BF)
    grad_ref[3*width:,:]=jnp.zeros((grad_ref.shape[0]-3*width,D),BF)

def ffn_grads(saved,x_all,g_all,n_dp,interpret=False):
    tokens,hid=saved[0].shape; rows=min(tokens,2048); steps=tokens//rows
    block=pl.BlockSpec((rows,D),lambda i:(i,0)); part=pl.BlockSpec((rows,hid),lambda i:(i,0))
    out=(n_dp*hid,D)
    return pl.pallas_call(functools.partial(ffn_grads_body,steps),out_shape=shape(out,BF),grid=(steps,),
        in_specs=[part]*3+[block]*2,out_specs=pl.BlockSpec(out,lambda i:(0,0)),
        scratch_shapes=[] if steps==1 else [pltpu.VMEM((3,hid,D),F32)],
        compiler_params=limit(40),cost_estimate=cost(10),name="ffn_grads",interpret=interpret)(*saved,x_all,g_all)


EPS = 1e-06
MOMENTUM = 0.5
LEARN = 0.2
LEARN_VEC = 0.002
P = jax.sharding.PartitionSpec
FFN = 3


def normalize(values):
    row_scale = lax.rsqrt(jnp.mean(values * values, axis=-1, keepdims=True) + EPS)
    return values * row_scale, row_scale


def norm_back(grad_in, normed, row_scale, gain):
    scaled = grad_in * gain
    inner_sum = jnp.mean(scaled * normed, axis=-1, keepdims=True)
    return row_scale * (scaled - normed * inner_sum), jnp.sum(grad_in * normed, axis=0)


def dp_pairs(shift, keep=lambda target: True):
    return [(j, j ^ shift) for j in range(lax.axis_size("dp")) if keep(j ^ shift)]


def place(parts, axis, me=None):
    me = lax.axis_index("dp") if me is None else me
    step = parts[0].shape[axis]
    shape = list(parts[0].shape)
    shape[axis] *= len(parts)
    out = jnp.zeros(shape, parts[0].dtype)
    for shift, part in enumerate(parts):
        out = lax.dynamic_update_slice_in_dim(out, part, (me ^ shift) * step, axis)
    return out


def gather_dp(own, axis=0):
    return place([own] + [lax.ppermute(own, "dp", dp_pairs(s)) for s in range(1, lax.axis_size("dp"))], axis)


def sum_dp(block_for, during=None, alongside=(), gate=None):
    me = lax.axis_index("dp")
    sent = [block_for(me ^ s).astype(BF) for s in range(1, lax.axis_size("dp"))]
    if gate is not None:
        sent = [after(block, gate) for block in sent]
    total = block_for(me)
    aside = None
    if during is not None:
        aside = during(*sent)
        total = after(total, *aside, *alongside)
    for s, block in enumerate(sent, 1):
        total = total + lax.ppermute(block, "dp", dp_pairs(s)).astype(F32)
    return total if during is None else (total, aside)


def after(value, *others):
    return lax.optimization_barrier((value, *others))[0]


def pass_core(x):
    return lax.ppermute(x, "mp", [(j, j ^ 1) for j in range(lax.axis_size("mp"))])


def pass_chip(x, shift):
    return lax.ppermute(x, "mp", [(j, j ^ (2 * shift)) for j in range(lax.axis_size("mp"))])


def pick(x, index):
    return lax.dynamic_index_in_dim(x, index, 0, keepdims=False)


CHIPS = 4


def cross_chips(near):
    if len(near) == 1:
        return [lax.psum_scatter(near[0], "mp", scatter_dimension=0, tiled=True)]
    return [near[0]] + [pass_chip(near[s].astype(BF), s) for s in range(1, len(near))]


def collect(near):
    return sum(part.astype(F32) for part in cross_chips(near))


def core_half(partial, axis):
    core = lax.axis_index("mp") % 2
    away = lax.dynamic_index_in_dim(partial, 1 - core, axis, keepdims=False).astype(BF)
    return lax.dynamic_index_in_dim(partial, core, axis, keepdims=False) + pass_core(away).astype(F32)


def chip_sums(partial):
    if lax.axis_size("mp") != 2 * CHIPS:
        return [partial]
    near = core_half(partial.reshape(CHIPS, 2, -1, partial.shape[1]), 1)
    near = [pick(near, (lax.axis_index("mp") // 2) ^ s) for s in range(CHIPS)]
    return [near[0]] + [part.astype(BF) for part in near[1:]]


def body(
    tokens,
    cotangent,
    domain_ids,
    domain_weight,
    gains,
    gain_mom,
    factor_w,
    factor_mom,
    out_w,
    out_mom,
    gate_up_w,
    gate_up_mom,
    down_w,
    down_mom,
):
    n_dp, n_mp = lax.axis_size("dp"), lax.axis_size("mp")
    me, mz = lax.axis_index("dp"), lax.axis_index("mp")
    rows = tokens.shape[0]
    d_own = factor_w.shape[0]
    hidden_own = gate_up_w.shape[2]
    out_own = d_own // n_mp
    base = me.astype(jnp.int32).reshape(1)
    shifts = range(1, n_dp)

    edge = NQ + 2 * NK

    def q_rows(m):
        return jnp.concatenate([m[edge : edge + WQ], m[:NQ]])

    def kv_rows(m):
        return jnp.concatenate([m[edge + WQ :], m[NQ:edge]])

    factor_own = factor_w.T.astype(BF)
    kv_low = gather_dp(kv_rows(factor_own), 1)
    x_float = tokens.astype(F32)
    first_normed, first_scale = normalize(x_float)
    first_own = (first_normed * gains[0]).astype(BF)
    domain_range = jnp.arange(domain_weight.shape[0], dtype=jnp.int32)
    seq_weight = jnp.sum(jnp.where(domain_ids[0, 0] == domain_range, domain_weight, 0.0))
    d_output = cotangent.astype(F32) * seq_weight
    d_output_all = lax.all_gather(d_output.astype(BF), "mp", axis=0, tiled=True)
    kv_all = gather_dp(dot_nt(first_own, kv_low))
    q_low = gather_dp(q_rows(factor_own), 1)
    q_own = dot_nt(first_own, q_low)
    attended, lse, queries, key_vecs, values = attn_fwd(base, q_own, kv_all)
    out_low = gather_dp(after(out_w.astype(BF), kv_all))
    residual = x_float + dot(attended, out_low)
    second_normed, second_scale = normalize(residual)

    ffn_own = jnp.stack([gate_up_w[0].T, gate_up_w[1].T, down_w])
    ffn_low = gather_dp(after(ffn_own.astype(BF), out_low), 2)
    second_own = (second_normed * gains[1]).astype(BF)
    to_ffn = lambda target: target < FFN
    ffn_slot = jnp.minimum(me, FFN - 1)
    ffn_mom = after(jnp.stack([gate_up_mom[0].T, gate_up_mom[1].T, down_mom]), ffn_low)
    own_mom = [pick(ffn_mom, ffn_slot)]
    for s in shifts:
        own_mom.append(lax.ppermute(pick(ffn_mom, jnp.minimum(me ^ s, FFN - 1)), "dp", dp_pairs(s, to_ffn)))
    second_in = lax.all_gather(second_own, "mp", axis=0, tiled=True)
    d_second, branch, *saved = ffn_tokens(second_in, d_output_all, after(ffn_low, *own_mom[1:]))
    d_second = lax.psum_scatter(d_second, "mp", scatter_dimension=0, tiled=True).astype(F32)
    grads = ffn_grads(saved, second_in, d_output_all, n_dp)
    branch = chip_sums(branch)
    d_second = after(d_second, grads, *branch)
    own_mom = MOMENTUM * place(own_mom, 1)
    matrix = lax.psum_scatter(grads, "dp", scatter_dimension=0, tiled=True)

    d_resid_norm, gain_second = norm_back(d_second, second_normed, second_scale, gains[1])
    d_residual = d_output + d_resid_norm
    d_residual_low = d_residual.astype(BF)
    d_attended = dot_nt(d_residual_low, out_low).astype(BF)

    def backward(pairs, us, *gates):
        return attn_bwd(pairs, after(base, *gates), queries, key_vecs, values, d_attended, lse, q_own, kv_all, us)

    grad_out = dot_tn(attended, d_residual_low)
    if n_mp == 2 * CHIPS:
        grad_out = core_half(grad_out.reshape(n_dp, CHIPS, 2, out_own, D), 2)
    grad_out = grad_out.reshape(n_dp, -1, D)
    last, branch = branch[3:], cross_chips([after(part, d_second) for part in branch[:3]])
    grad_out, (d_q, d_kv) = sum_dp(
        lambda t: pick(grad_out, t), during=functools.partial(backward, (0, HEADS // 2), 26), alongside=branch[1:]
    )
    d_q, d_kv = after((d_q, d_kv), grad_out)
    if n_mp == 2 * CHIPS:
        grad_out = grad_out.reshape(CHIPS, out_own, D)
        near = [pick(grad_out, (mz // 2) ^ s) for s in range(CHIPS)]
        near = near[:1] + [part.astype(BF) for part in near[1:]]
        grad_out = collect(near)
    else:
        grad_out = lax.psum_scatter(grad_out, "mp", scatter_dimension=0, tiled=True)
    out_tile = MOMENTUM * lax.dynamic_slice_in_dim(out_mom, mz * out_own, out_own, 0) + grad_out
    out_tile = after(out_tile, matrix)
    out_rows = place([out_tile] + [lax.ppermute(out_tile, "dp", [(j ^ s, j) for j in range(FFN, n_dp)]) for s in shifts], 0)
    out_rows = jnp.pad(out_rows, ((0, hidden_own - out_rows.shape[0]), (0, 0)))
    matrix = jnp.where(me < FFN, own_mom + matrix.astype(F32), out_rows)
    gram_part = gram_upper(matrix)
    gram = lax.psum(gram_part, "mp")

    d_kv = sum_dp(lambda t: lax.dynamic_slice_in_dim(d_kv, t * rows, rows, 0))
    d_q, d_kv = d_q.astype(BF), d_kv.astype(BF)
    d_first = dot(d_q, q_low) + dot(d_kv, kv_low)
    d_input_norm, gain_first = norm_back(d_first, first_normed, first_scale, gains[0])
    input_grad = d_residual + d_input_norm

    gain_rows = jnp.stack([gain_first, gain_second])
    filler = -(factor_w.shape[1] + 2) % (8 * n_mp)

    d_all = jnp.concatenate([d_q[:, WQ:], d_kv[:, 2 * WK :], d_q[:, :WQ], d_kv[:, : 2 * WK]], axis=1)
    grad_factor = jnp.concatenate([dot_tn(d_all, first_own), jnp.pad(gain_rows, ((0, filler), (0, 0)))])
    height = grad_factor.shape[0] // n_mp
    if n_mp == 2 * CHIPS:
        grad_factor = core_half(grad_factor.reshape(CHIPS, 2, height, D), 1).reshape(CHIPS * height, D)
    grad_factor = sum_dp(lambda t: lax.dynamic_slice_in_dim(grad_factor, t * d_own, d_own, 1))
    dp_summed = grad_factor
    if n_mp == 2 * CHIPS:
        grad_factor = grad_factor.reshape(CHIPS, height, d_own)
        grad_factor = collect([pick(grad_factor, (mz // 2) ^ s) for s in range(CHIPS)])
    else:
        grad_factor = lax.psum_scatter(grad_factor, "mp", scatter_dimension=0, tiled=True)
    factor_piece = jnp.pad(MOMENTUM * factor_mom.T, ((0, filler + 2), (0, 0)))
    factor_piece = lax.dynamic_slice_in_dim(factor_piece, mz * height, height, 0) + grad_factor
    factor_all = lax.all_gather(factor_piece, ("dp", "mp"), axis=0, tiled=True).reshape(n_dp, n_mp * height, d_own)
    factor_tile = pick(factor_all, me)

    def give_back(whole):
        pieces = [lax.dynamic_slice_in_dim(whole, (me ^ s) * d_own, d_own, 1) for s in range(n_dp)]
        came = [lax.ppermute(pieces[s], "dp", dp_pairs(s, lambda t: t ^ s < FFN))[None] for s in shifts]
        return place([pieces[0][None]] + came, 0), pieces[1:], came

    mom_back, _, came = give_back(after(matrix, dp_summed))
    ortho = ns_big(gram, after(matrix, factor_piece, *came))
    ortho = after(ortho, factor_all)
    branch += [pass_chip(after(part, gram), 3) for part in last]
    ortho = after(ortho, *branch[3:])
    out_ortho = lax.dynamic_slice_in_dim(ortho, me * out_own, out_own, 0)
    for s in shifts:
        piece = lax.dynamic_slice_in_dim(ortho, (me ^ s) * out_own, out_own, 0)
        piece = lax.ppermute(piece, "dp", [(j, j ^ s) for j in range(FFN, n_dp)])
        out_ortho = jnp.where(me ^ s == FFN, piece, out_ortho)
    out_pair = after(jnp.stack([out_tile, out_ortho]), factor_all)
    branch = [after(part, out_pair) for part in branch]
    block_out = (residual + sum(part.astype(F32) for part in branch)).astype(BF)
    factor_tile = after(factor_tile, out_pair)
    gain_grad = factor_tile[factor_w.shape[1] : factor_w.shape[1] + 2]
    out_both = lax.all_gather(out_pair, "mp", axis=1, tiled=True)
    new_out_mom = out_both[0]
    new_out_w = out_w - LEARN * 0.2 * math.sqrt(D) * out_both[1]
    ortho_back, sent, _ = give_back(after(ortho, out_ortho))
    factor_ortho = ns_factor(factor_all, after(factor_tile, out_pair, *sent))
    ortho_back = after(ortho_back, factor_ortho)
    turn = lambda stack: jnp.stack([stack[0].T, stack[1].T])
    ffn_rate = LEARN * 0.2 * math.sqrt(max(D, hidden_own * n_mp))
    new_gate_up_mom, new_down_mom = turn(mom_back), mom_back[2]
    new_gate_up_w = gate_up_w - ffn_rate * turn(ortho_back)
    new_down_w = down_w - ffn_rate * ortho_back[2]
    widths = [NQ, NK, NK, WQ, WK, WK]
    factor_rate = jnp.concatenate([jnp.full((w, 1), LEARN * 0.2 * math.sqrt(max(D, w)), F32) for w in widths])
    new_factor_mom = factor_tile[: factor_w.shape[1]].T
    new_factor_w = factor_w - (factor_rate * factor_ortho[: factor_w.shape[1]]).T

    new_gain_mom = MOMENTUM * gain_mom + gain_grad
    new_gains = lax.dynamic_slice_in_dim(gains, me * d_own, d_own, 1) - LEARN_VEC * new_gain_mom
    return (
        block_out,
        input_grad,
        gain_grad,
        new_gains,
        new_gain_mom,
        new_factor_mom,
        new_factor_w,
        new_out_mom,
        new_out_w,
        new_gate_up_mom,
        new_gate_up_w,
        new_down_mom,
        new_down_w,
    )


def solution(mesh):
    token = P(("mp", "dp"), None)
    row = P("dp", None)
    ffn = P(None, "dp", "mp")
    down = P("mp", "dp")
    vec = P(None, "dp")
    return jax.shard_map(
        body,
        mesh=mesh,
        in_specs=(token, token, P("mp", None), P(), P(), vec, row, row, row, row, ffn, ffn, down, down),
        out_specs=(token, token, vec, vec, vec, row, row, row, row, ffn, ffn, down, down),
        check_vma=False,
    )
```
